32 devices in a mesh: wide: 8 (over y, x, core), samp: 4 (over z).
Axes of the slice: x: 2, y: 2, z: 4, core: 2. Of those that a mesh axis runs over, the one named last changes fastest.
Arguments:
- features: bfloat16 [4, 32, 96, 128], P('samp', 'wide'), may hold values from -6 to 6
- labels: int32 [4, 32, 96], P('samp', 'wide'), may hold values from 0 to 8
- conv_weight: bfloat16 [3, 3, 128, 128], replicated, may hold values from -0.1875 to 0.1875
- down_weight: bfloat16 [512, 1024], replicated, may hold values from -0.25 to 0.25
- expand_weight: bfloat16 [3, 3, 1024, 2048], P(None, None, None, 'wide'), may hold values from -0.0625 to 0.0625
- reduce_weight: bfloat16 [3, 3, 2048, 1024], P(None, None, 'wide'), may hold values from -0.046875 to 0.046875
- up_weight: bfloat16 [1024, 512], replicated, may hold values from -0.1875 to 0.1875
- class_weight: bfloat16 [128, 9], replicated, may hold values from -3 to 3
Outputs:
- conv_grad: float32 [3, 3, 128, 128], replicated
- down_grad: float32 [512, 1024], replicated
- expand_grad: float32 [3, 3, 1024, 2048], P(None, None, 'samp', 'wide')
- reduce_grad: float32 [3, 3, 2048, 1024], P(None, None, 'wide', 'samp')
- up_grad: float32 [1024, 512], replicated
- class_grad: float32 [128, 9], replicated
The draws below stay inside these ranges and needn't reach their ends.
All inputs are finite; a program needn't handle non-finite values.
Results may differ from the reference program's by a relative error of at most 0.012.
Values may be sent and summed in bfloat16 or wider, within the bound.
No kernel may reach another device: no remote copies, remote signals or barrier semaphores. Data moves between devices by JAX's collectives and lax.ppermute only.
A program may use at most 192 MiB of HBM per device.

```python
import math
import jax
import jax.numpy as jnp
from jax import lax

C1 = 128
CB = 1024
CF = 2048
NCLS = 9
COLS = 96
H = 32
SAMPLES = 4
PIXELS = 12288


def place_ends(drawn, own_key, smallest, largest):
    longest = drawn.shape.index(max(drawn.shape))
    spots = []
    for shift in (0, 1):
        where = [jax.random.randint(jax.random.fold_in(own_key, axis), (), 0, length) for axis, length in enumerate(drawn.shape)]
        where[longest] = (where[longest] + shift) % drawn.shape[longest]
        spots.append(tuple(where))
    return drawn.at[spots[0]].set(smallest).at[spots[1]].set(largest)


def shard_levels(rng, extent, cuts, low, largest):
    level = 1.0
    for position, shards_of in cuts:
        draws = jax.random.uniform(jax.random.fold_in(jax.random.fold_in(rng, 6), position), (shards_of,), jnp.float32, low / len(cuts), largest / len(cuts))
        level = level * jnp.repeat(jnp.exp(draws), extent[position] // shards_of).reshape((-1,) + (1,) * (len(extent) - 1 - position))
    return level


def gaussian(key, dims, spread, bound, cuts=(), kind=jnp.bfloat16):
    level = shard_levels(key, dims, cuts, -0.22, 0.18) if cuts else 1.0
    drawn = jax.random.normal(key, dims, jnp.float32) * spread * level
    return jnp.minimum(jnp.maximum(drawn, -bound), bound).astype(kind)


def setup_inputs(seed: int = 0) -> dict:
    streams_of = jax.random.split(jax.random.key(seed), 9)
    return {
        "features": gaussian(streams_of[0], (SAMPLES, H, COLS, C1), 1.0, 6.0, ((0, 4), (1, 8))),
        "labels": place_ends(jax.random.randint(streams_of[1], (SAMPLES, H, COLS), 0, NCLS), jax.random.fold_in(streams_of[1], 1), 0, NCLS - 1).astype(jnp.int32),
        "conv_weight": gaussian(streams_of[2], (3, 3, C1, C1), (9 * C1) ** -0.5, 0.1875),
        "down_weight": gaussian(streams_of[3], (4 * C1, CB), (4 * C1) ** -0.5, 0.25),
        "expand_weight": gaussian(streams_of[4], (3, 3, CB, CF), (9 * CB) ** -0.5, 0.0625, ((3, 8),)),
        "reduce_weight": gaussian(streams_of[5], (3, 3, CF, CB), (9 * CF) ** -0.5, 0.046875, ((2, 8),)),
        "up_weight": gaussian(streams_of[6], (CB, 4 * C1), CB ** -0.5, 0.1875),
        "class_weight": gaussian(streams_of[7], (C1, NCLS), (max(C1 // 32, 1)) ** -0.5, 3.0),
    }


def silu_slope(value):
    logistic = jax.nn.sigmoid(value)
    return logistic * (1.0 + value * (1.0 - logistic))

def pad_both(values):
    return jnp.pad(values, ((1, 1), (1, 1), (0, 0)))

def to_depth(grid):
    height, across, channels = grid.shape
    blocks = grid.reshape(height // 2, 2, across // 2, 2, channels)
    return jnp.transpose(blocks, (0, 2, 1, 3, 4)).reshape(height // 2, across // 2, 4 * channels)

def from_depth(grid):
    height, across, channels = grid.shape
    blocks = grid.reshape(height, across, 2, 2, channels // 4)
    return jnp.transpose(blocks, (0, 2, 1, 3, 4)).reshape(2 * height, 2 * across, channels // 4)

def taps_in(padded, height, across):
    return jnp.concatenate([padded[p:p + height, q:q + across] for p in range(3) for q in range(3)], axis=-1)

def taps_out(values):
    return jnp.concatenate([jnp.pad(values, ((p, 2 - p), (q, 2 - q), (0, 0))) for p in range(3) for q in range(3)], axis=-1)

def conv_padded(padded, weight):
    height = padded.shape[0] - 2
    across = padded.shape[1] - 2
    inward = weight.shape[2]
    outward = weight.shape[3]
    if inward <= outward:
        window = taps_in(padded, height, across).reshape(height * across, 9 * inward)
        result = jnp.dot(window, weight.reshape(9 * inward, outward), preferred_element_type=jnp.float32)
        return result.reshape(height, across, outward)
    flattened = padded.reshape((height + 2) * (across + 2), inward)
    stacked = jnp.transpose(weight, (2, 0, 1, 3)).reshape(inward, 9 * outward)
    spread_out = jnp.dot(flattened, stacked, preferred_element_type=jnp.float32).reshape(height + 2, across + 2, 9, outward)
    summed = spread_out[0:height, 0:across, 0]
    for offset in range(1, 9):
        p = offset // 3
        q = offset % 3
        summed = summed + spread_out[p:p + height, q:q + across, offset]
    return summed

def correlate(padded, values):
    height, across, outward = values.shape
    inward = padded.shape[-1]
    if inward <= outward:
        window = taps_in(padded, height, across).reshape(height * across, 9 * inward)
        result = lax.dot_general(window, values.reshape(height * across, outward), (((0,), (0,)), ((), ())), preferred_element_type=jnp.float32)
        return result.reshape(3, 3, inward, outward)
    shifted = taps_out(values).reshape((height + 2) * (across + 2), 9 * outward)
    result = lax.dot_general(padded.reshape(-1, inward), shifted, (((0,), (0,)), ((), ())), preferred_element_type=jnp.float32)
    return jnp.transpose(result.reshape(inward, 3, 3, outward), (1, 2, 0, 3))

def contract_rows(left, right):
    left_flat = left.reshape(-1, left.shape[-1])
    right_flat = right.reshape(-1, right.shape[-1])
    return lax.dot_general(left_flat, right_flat, (((0,), (0,)), ((), ())), preferred_element_type=jnp.float32)

def flip_kernel(weight):
    return jnp.transpose(weight[::-1, ::-1], (0, 1, 3, 2))

def reference(features, labels, conv_weight, down_weight, expand_weight, reduce_weight, up_weight, class_weight):
    loss_scale = 8.0 / math.sqrt(PIXELS)
    classes = lax.broadcasted_iota(jnp.int32, (1, 1, NCLS), 2)
    back_reduce = flip_kernel(reduce_weight)
    back_expand = flip_kernel(expand_weight)
    conv_grad = jnp.zeros(conv_weight.shape, jnp.float32)
    down_grad = jnp.zeros(down_weight.shape, jnp.float32)
    expand_grad = jnp.zeros(expand_weight.shape, jnp.float32)
    reduce_grad = jnp.zeros(reduce_weight.shape, jnp.float32)
    up_grad = jnp.zeros(up_weight.shape, jnp.float32)
    class_grad = jnp.zeros(class_weight.shape, jnp.float32)
    for sample in range(SAMPLES):
        crop_rows = features[sample]
        label_map = labels[sample]
        padded_in = pad_both(crop_rows)
        hidden_pre = conv_padded(padded_in, conv_weight)
        hidden = jax.nn.silu(hidden_pre).astype(jnp.bfloat16)
        stacked = to_depth(hidden)
        coarse = jnp.dot(stacked, down_weight, preferred_element_type=jnp.float32).astype(jnp.bfloat16)
        coarse_pad = pad_both(coarse)
        expand_pre = conv_padded(coarse_pad, expand_weight)
        expanded = jax.nn.silu(expand_pre).astype(jnp.bfloat16)
        expand_pad = pad_both(expanded)
        bottom = (coarse.astype(jnp.float32) + conv_padded(expand_pad, reduce_weight)).astype(jnp.bfloat16)
        upward = from_depth(jnp.dot(bottom, up_weight, preferred_element_type=jnp.float32))
        joined_pre = upward + hidden.astype(jnp.float32)
        joined = jax.nn.silu(joined_pre).astype(jnp.bfloat16)
        logits = jnp.dot(joined, class_weight, preferred_element_type=jnp.float32)
        exp_logits = jnp.exp(logits)
        probability = exp_logits / lax.optimization_barrier(jnp.sum(exp_logits, axis=-1, keepdims=True))
        onehot = (label_map[:, :, None] == classes).astype(jnp.float32)
        logit_grad = ((probability - onehot) * loss_scale).astype(jnp.bfloat16)
        class_grad = class_grad + contract_rows(joined, logit_grad)
        joined_grad = lax.dot_general(logit_grad, class_weight, (((2,), (1,)), ((), ())), preferred_element_type=jnp.float32)
        upward_grad = (joined_grad * silu_slope(joined_pre)).astype(jnp.bfloat16)
        stacked_grad = to_depth(upward_grad)
        up_grad = up_grad + contract_rows(bottom, stacked_grad)
        bottom_grad = lax.dot_general(stacked_grad, up_weight, (((2,), (1,)), ((), ())), preferred_element_type=jnp.float32).astype(jnp.bfloat16)
        reduce_grad = reduce_grad + correlate(expand_pad, bottom_grad)
        expanded_back = conv_padded(pad_both(bottom_grad), back_reduce)
        expanded_grad = (expanded_back * silu_slope(expand_pre)).astype(jnp.bfloat16)
        expand_grad = expand_grad + correlate(coarse_pad, expanded_grad)
        coarse_back = conv_padded(pad_both(expanded_grad), back_expand)
        coarse_grad = (bottom_grad.astype(jnp.float32) + coarse_back).astype(jnp.bfloat16)
        down_grad = down_grad + contract_rows(stacked, coarse_grad)
        down_back = lax.dot_general(coarse_grad, down_weight, (((2,), (1,)), ((), ())), preferred_element_type=jnp.float32)
        hidden_sum = from_depth(down_back) + upward_grad.astype(jnp.float32)
        hidden_grad = (hidden_sum * silu_slope(hidden_pre)).astype(jnp.bfloat16)
        conv_grad = conv_grad + correlate(padded_in, hidden_grad)
    return (conv_grad, down_grad, expand_grad, reduce_grad, up_grad, class_grad)
```

```python
import math

import jax
import jax.numpy as jnp
from jax import lax
from jax.sharding import PartitionSpec as P


def swap(values, axis, mask):
    count = lax.axis_size(axis)
    return lax.ppermute(values, axis, [(i, i ^ mask) for i in range(count)])


def bit_of(axis, mask):
    return (lax.axis_index(axis) // mask) % 2


def chip_masks():
    count = lax.axis_size("wide")
    masks = []
    mask = 2
    while mask < count:
        masks.append(mask)
        mask *= 2
    return masks


def split_lanes(values, count):
    return jnp.split(values, count, axis=-1)


def join_pair(mine, other, bit, axis):
    low = jnp.where(bit == 0, mine, other)
    high = jnp.where(bit == 0, other, mine)
    return jnp.stack([low, high], axis=axis)


def gather_wide(piece):
    masks = chip_masks()
    count = len(masks)
    rows, lanes = piece.shape
    parts = [
        part.reshape((1,) * count + part.shape) for part in split_lanes(piece, count)
    ]
    for stage in range(count):
        received = [
            swap(part, "wide", masks[(stage + index) % count]) for index, part in enumerate(parts)
        ]
        joined = []
        for index, (part, other) in enumerate(zip(parts, received)):
            place = (stage + index) % count
            axis = count - 1 - place
            bit = bit_of("wide", masks[place])
            low = jnp.where(bit == 0, part, other)
            high = jnp.where(bit == 0, other, part)
            joined.append(jnp.concatenate([low, high], axis=axis))
        parts = joined
    chips = 2**count
    whole = jnp.concatenate(parts, axis=-1).reshape(chips, rows, lanes)
    other = swap(whole, "wide", 1)
    return join_pair(whole, other, bit_of("wide", 1), 1).reshape(2 * chips * rows, lanes)


def scatter_wide(whole):
    masks = chip_masks()
    count = len(masks)
    chips = 2**count
    rows = whole.shape[0] // (2 * chips)
    lanes = whole.shape[1]
    view = whole.reshape(chips, 2, rows, lanes)
    core = bit_of("wide", 1)
    sent = lax.dynamic_index_in_dim(view, 1 - core, 1, keepdims=False).astype(jnp.bfloat16)
    kept = lax.dynamic_index_in_dim(view, core, 1, keepdims=False)
    summed = kept.astype(jnp.float32) + swap(sent, "wide", 1).astype(jnp.float32)
    parts = [
        part.reshape((2,) * count + (rows, lanes // count)) for part in split_lanes(summed, count)
    ]
    for stage in range(count):
        sends = []
        keeps = []
        for index, part in enumerate(parts):
            place = (stage + index) % count
            axis = count - 1 - place
            bit = bit_of("wide", masks[place])
            sends.append(
                swap(
                    lax.dynamic_index_in_dim(part, 1 - bit, axis).astype(jnp.bfloat16),
                    "wide",
                    masks[place],
                )
            )
            keeps.append(lax.dynamic_index_in_dim(part, bit, axis))
        parts = [keep + sent.astype(jnp.float32) for keep, sent in zip(keeps, sends)]
    return jnp.concatenate([part.reshape(rows, lanes // count) for part in parts], axis=-1)


def exchange_samples(pieces_of):
    count = lax.axis_size("samp")
    own = lax.axis_index("samp")
    received = [pieces_of(own)]
    for mask in range(1, count):
        received.append(swap(pieces_of(own ^ mask), "samp", mask))
    return jnp.stack(received)


def sum_samples(values):
    rounded = values.astype(jnp.bfloat16)
    count = lax.axis_size("samp")
    terms = [rounded.astype(jnp.float32)]
    for mask in range(1, count):
        terms.append(swap(rounded, "samp", mask).astype(jnp.float32))
    while len(terms) > 1:
        terms = [terms[i] + terms[i + 1] for i in range(0, len(terms), 2)]
    return terms[0]


def sum_everywhere(packed):
    rows = packed.shape[0]
    unit = 16 * lax.axis_size("wide")
    padded = -(-rows // unit) * unit
    if padded != rows:
        packed = jnp.pad(packed, ((0, padded - rows), (0, 0)))
    own = sum_samples(scatter_wide(packed)).astype(jnp.bfloat16)
    return gather_wide(own)[:rows].astype(jnp.float32)


def fold_rows(values, lanes):
    times = lanes // values.shape[1]
    return jnp.concatenate(jnp.split(values, times, axis=0), axis=1)


def unfold_rows(values, narrow):
    times = values.shape[1] // narrow
    return jnp.concatenate(jnp.split(values, times, axis=1), axis=0)


def silu_slope(value):
    logistic = jax.nn.sigmoid(value)
    return logistic * (1.0 + value * (1.0 - logistic))


def to_depth(grid):
    height, across, channels = grid.shape
    blocks = grid.reshape(height // 2, 2, across // 2, 2, channels)
    return jnp.transpose(blocks, (0, 2, 1, 3, 4)).reshape(height // 2, across // 2, 4 * channels)


def from_depth(grid):
    height, across, channels = grid.shape
    blocks = grid.reshape(height, across, 2, 2, channels // 4)
    return jnp.transpose(blocks, (0, 2, 1, 3, 4)).reshape(2 * height, 2 * across, channels // 4)


def shift_columns(grid, offset):
    across = grid.shape[-2]
    pads = [(0, 0)] * grid.ndim
    if offset > 0:
        pads[-2] = (0, offset)
        return jnp.pad(lax.slice_in_dim(grid, offset, across, axis=-2 % grid.ndim), pads)
    if offset < 0:
        pads[-2] = (-offset, 0)
        return jnp.pad(lax.slice_in_dim(grid, 0, across + offset, axis=-2 % grid.ndim), pads)
    return grid


def shift_rows(grid, offset):
    height = grid.shape[-3]
    pads = [(0, 0)] * grid.ndim
    if offset > 0:
        pads[-3] = (0, offset)
        return jnp.pad(lax.slice_in_dim(grid, offset, height, axis=-3 % grid.ndim), pads)
    if offset < 0:
        pads[-3] = (-offset, 0)
        return jnp.pad(lax.slice_in_dim(grid, 0, height + offset, axis=-3 % grid.ndim), pads)
    return grid


def taps(grid, sign):
    columns = [shift_columns(grid, sign * (q - 1)) for q in range(3)]
    return [shift_rows(columns[q], sign * (p - 1)) for p in range(3) for q in range(3)]


def conv_in(grid, weight, sign, transposed):
    height, across, channels = grid.shape
    window = jnp.concatenate(taps(grid, sign), axis=-1).reshape(height * across, 9 * channels)
    if transposed:
        flat = jnp.transpose(weight, (0, 1, 3, 2)).reshape(9 * channels, weight.shape[2])
    else:
        flat = weight.reshape(9 * channels, weight.shape[3])
    result = jnp.dot(window, flat, preferred_element_type=jnp.float32)
    return result.reshape(height, across, -1)


def correlate_samples(left, right):
    samples, height, across, inward = left.shape
    outward = right.shape[-1]
    flat = left.reshape(samples * height * across, inward)
    shifted = jnp.concatenate(taps(right, -1), axis=-1).reshape(-1, 9 * outward)
    result = lax.dot_general(
        flat, shifted, (((0,), (0,)), ((), ())), preferred_element_type=jnp.float32
    )
    return jnp.transpose(result.reshape(inward, 3, 3, outward), (1, 2, 0, 3))


def contract_rows(left, right):
    left_flat = left.reshape(-1, left.shape[-1])
    right_flat = right.reshape(-1, right.shape[-1])
    return lax.dot_general(
        left_flat, right_flat, (((0,), (0,)), ((), ())), preferred_element_type=jnp.float32
    )


def project(values, weight, dim):
    return lax.dot_general(
        values, weight, (((values.ndim - 1,), (dim,)), ((), ())), preferred_element_type=jnp.float32
    )


def slices_of_samples(whole):
    count = lax.axis_size("samp")
    positions, lanes = whole.shape
    narrow = lanes // count
    core = bit_of("wide", 1)
    half = positions // 2
    mine = lax.dynamic_slice_in_dim(whole, core * half, half, axis=0)

    def piece(target):
        return lax.dynamic_slice_in_dim(mine, target * narrow, narrow, axis=1)

    gathered = exchange_samples(piece)
    other = swap(gathered, "wide", 1)
    return join_pair(gathered, other, core, 1).reshape(count, positions, narrow)


def local(
    features,
    labels,
    conv_weight,
    down_weight,
    expand_weight,
    reduce_weight,
    up_weight,
    class_weight,
):
    crop_rows = features[0]
    label_map = labels[0]
    height, across, channels = crop_rows.shape
    wide = lax.axis_size("wide")
    pixel_count = wide * lax.axis_size("samp") * height * across
    loss_scale = 8.0 / math.sqrt(pixel_count)
    classes = lax.broadcasted_iota(jnp.int32, (1, 1, class_weight.shape[1]), 2)

    forward = [(i, i + 1) for i in range(wide - 1)]
    backward = [(target, source) for source, target in forward]
    above = lax.ppermute(crop_rows[-1:], "wide", forward)
    below = lax.ppermute(crop_rows[:1], "wide", backward)
    near_rows = jnp.concatenate([above, crop_rows, below], axis=0)
    columns = [shift_columns(near_rows, q - 1) for q in range(3)]
    window = jnp.concatenate(
        [columns[q][p : p + height] for p in range(3) for q in range(3)], axis=-1
    ).reshape(height * across, 9 * channels)
    hidden_pre = jnp.dot(
        window, conv_weight.reshape(9 * channels, -1), preferred_element_type=jnp.float32
    ).reshape(height, across, -1)
    hidden = jax.nn.silu(hidden_pre).astype(jnp.bfloat16)
    stacked = to_depth(hidden)
    low_rows, low_across, _ = stacked.shape
    coarse = project(stacked, down_weight, 0).astype(jnp.bfloat16)
    base = coarse.shape[-1]
    coarse_all = gather_wide(coarse.reshape(low_rows * low_across, base))
    grid = (wide * low_rows, low_across)

    expand_pre = conv_in(coarse_all.reshape(*grid, base), expand_weight, 1, False)
    expanded = jax.nn.silu(expand_pre).astype(jnp.bfloat16)
    inner = expanded.shape[-1]
    partial = conv_in(expanded, reduce_weight, 1, False).astype(jnp.bfloat16)
    coarse_slices = slices_of_samples(coarse_all)
    expanded_samples = exchange_samples(lambda target: expanded)
    summed = scatter_wide(partial.reshape(-1, base)).reshape(low_rows, low_across, base)
    bottom = (coarse.astype(jnp.float32) + summed).astype(jnp.bfloat16)
    upward = from_depth(project(bottom, up_weight, 0))
    joined_pre = upward + hidden.astype(jnp.float32)
    joined = jax.nn.silu(joined_pre).astype(jnp.bfloat16)
    logits = jnp.dot(joined, class_weight, preferred_element_type=jnp.float32)
    exp_logits = jnp.exp(logits)
    probability = exp_logits / jnp.sum(exp_logits, axis=-1, keepdims=True)
    onehot = (label_map[:, :, None] == classes).astype(jnp.float32)
    logit_grad = ((probability - onehot) * loss_scale).astype(jnp.bfloat16)
    class_grad = contract_rows(joined, logit_grad)
    joined_grad = project(logit_grad, class_weight, 1)
    upward_grad = (joined_grad * silu_slope(joined_pre)).astype(jnp.bfloat16)
    stacked_grad = to_depth(upward_grad)
    up_grad = contract_rows(bottom, stacked_grad)
    bottom_grad = project(stacked_grad, up_weight, 1).astype(jnp.bfloat16)
    bottom_all = gather_wide(bottom_grad.reshape(low_rows * low_across, base))

    expanded_back = conv_in(bottom_all.reshape(*grid, base), reduce_weight, -1, True)
    expanded_grad = (expanded_back * silu_slope(expand_pre)).astype(jnp.bfloat16)
    back_partial = conv_in(expanded_grad, expand_weight, -1, True).astype(jnp.bfloat16)
    bottom_slices = slices_of_samples(bottom_all)
    grad_samples = exchange_samples(lambda target: expanded_grad)
    back_sum = scatter_wide(back_partial.reshape(-1, base)).reshape(low_rows, low_across, base)
    coarse_grad = (bottom_grad.astype(jnp.float32) + back_sum).astype(jnp.bfloat16)
    down_grad = contract_rows(stacked, coarse_grad)
    down_back = project(coarse_grad, down_weight, 1)
    hidden_sum = from_depth(down_back) + upward_grad.astype(jnp.float32)
    hidden_grad = (hidden_sum * silu_slope(hidden_pre)).astype(jnp.bfloat16)
    conv_grad = contract_rows(window, hidden_grad)

    samples = lax.axis_size("samp")
    narrow = base // samples
    reduce_grad = correlate_samples(
        expanded_samples.reshape(samples, *grid, inner),
        bottom_slices.reshape(samples, *grid, narrow),
    )
    expand_grad = correlate_samples(
        coarse_slices.reshape(samples, *grid, narrow),
        grad_samples.reshape(samples, *grid, inner),
    )

    lanes = base
    class_lanes = 128
    class_pad = jnp.pad(class_grad, ((0, 0), (0, class_lanes - class_grad.shape[1])))
    up_pack = fold_rows(up_grad, lanes)
    up_sum = sum_everywhere(up_pack)
    folded = [
        fold_rows(down_grad, lanes),
        fold_rows(conv_grad, lanes),
        fold_rows(class_pad, lanes),
    ]
    sizes = [item.shape[0] for item in folded]
    total = sum_everywhere(jnp.concatenate(folded, axis=0))
    down_total = unfold_rows(total[: sizes[0]], down_grad.shape[1])
    conv_total = unfold_rows(total[sizes[0] : sizes[0] + sizes[1]], conv_grad.shape[1])
    class_total = unfold_rows(total[sizes[0] + sizes[1] :], class_lanes)
    return (
        conv_total.reshape(conv_weight.shape),
        down_total,
        expand_grad,
        reduce_grad,
        unfold_rows(up_sum, up_grad.shape[1]),
        class_total[:, : class_grad.shape[1]],
    )


def solution(mesh):
    return jax.shard_map(
        local,
        mesh=mesh,
        in_specs=(
            P("samp", "wide", None, None),
            P("samp", "wide", None),
            P(),
            P(),
            P(None, None, None, "wide"),
            P(None, None, "wide", None),
            P(),
            P(),
        ),
        out_specs=(
            P(),
            P(),
            P(None, None, "samp", "wide"),
            P(None, None, "wide", "samp"),
            P(),
            P(),
        ),
        check_vma=False,
    )
```

```python
import functools
import math

import jax
import jax.numpy as jnp
from jax import lax
from jax.experimental import pallas as pl
from jax.experimental.pallas import tpu as pltpu
from jax.sharding import PartitionSpec as P


def swap(values, axis, mask):
    count = lax.axis_size(axis)
    return lax.ppermute(values, axis, [(i, i ^ mask) for i in range(count)])


def bit_of(axis, mask):
    return (lax.axis_index(axis) // mask) % 2


def chip_masks():
    count = lax.axis_size("wide")
    masks = []
    mask = 2
    while mask < count:
        masks.append(mask)
        mask *= 2
    return masks


def split_lanes(values, count):
    return jnp.split(values, count, axis=-1)


def join_pair(mine, other, bit, axis):
    low = jnp.where(bit == 0, mine, other)
    high = jnp.where(bit == 0, other, mine)
    return jnp.stack([low, high], axis=axis)


def gather_chips(piece):
    masks = chip_masks()
    count = len(masks)
    rows, lanes = piece.shape
    parts = [
        part.reshape((1,) * count + part.shape) for part in split_lanes(piece, count)
    ]
    for stage in range(count):
        received = [
            swap(part, "wide", masks[(stage + index) % count])
            for index, part in enumerate(parts)
        ]
        joined = []
        for index, (part, other) in enumerate(zip(parts, received)):
            place = (stage + index) % count
            axis = count - 1 - place
            bit = bit_of("wide", masks[place])
            low = jnp.where(bit == 0, part, other)
            high = jnp.where(bit == 0, other, part)
            joined.append(jnp.concatenate([low, high], axis=axis))
        parts = joined
    chips = 2**count
    return jnp.concatenate(parts, axis=-1).reshape(chips * rows, lanes)


def join_cores(mine, other, rows):
    chips = mine.shape[0] // rows
    lanes = mine.shape[1]
    pair = join_pair(
        mine.reshape(chips, rows, lanes), other.reshape(chips, rows, lanes), bit_of("wide", 1), 1
    )
    return pair.reshape(2 * chips * rows, lanes)


def part_cores(whole, rows):
    lanes = whole.shape[1]
    view = whole.reshape(-1, 2, rows, lanes)
    core = bit_of("wide", 1)
    own = lax.dynamic_index_in_dim(view, core, 1, keepdims=False)
    partner = lax.dynamic_index_in_dim(view, 1 - core, 1, keepdims=False)
    return jnp.stack([own, partner]).reshape(2, -1, lanes)


def scatter_cores(parted):
    sent = parted[1].astype(jnp.bfloat16)
    return parted[0].astype(jnp.float32) + swap(sent, "wide", 1).astype(jnp.float32)


def scatter_chips(summed):
    masks = chip_masks()
    count = len(masks)
    chips = 2**count
    rows = summed.shape[0] // chips
    lanes = summed.shape[1]
    parts = [
        part.reshape((2,) * count + (rows, lanes // count)) for part in split_lanes(summed, count)
    ]
    for stage in range(count):
        sends = []
        keeps = []
        for index, part in enumerate(parts):
            place = (stage + index) % count
            axis = count - 1 - place
            bit = bit_of("wide", masks[place])
            sends.append(
                swap(
                    lax.dynamic_index_in_dim(part, 1 - bit, axis).astype(jnp.bfloat16),
                    "wide",
                    masks[place],
                )
            )
            keeps.append(lax.dynamic_index_in_dim(part, bit, axis))
        parts = [keep + sent.astype(jnp.float32) for keep, sent in zip(keeps, sends)]
    return jnp.concatenate([part.reshape(rows, lanes // count) for part in parts], axis=-1)


def exchange_samples(piece_of):
    count = lax.axis_size("samp")
    own = lax.axis_index("samp")
    received = [piece_of(own)]
    for mask in range(1, count):
        received.append(swap(piece_of(own ^ mask), "samp", mask))
    return received


def add_pairs(terms):
    while len(terms) > 1:
        terms = [terms[i] + terms[i + 1] for i in range(0, len(terms), 2)]
    return terms[0]


def sum_samples(values):
    count = lax.axis_size("samp")
    own = lax.axis_index("samp")
    _, lanes = values.shape
    narrow = lanes // count
    rounded = values.astype(jnp.bfloat16)

    def block(target):
        return lax.dynamic_slice_in_dim(rounded, target * narrow, narrow, axis=1)

    terms = [item.astype(jnp.float32) for item in exchange_samples(block)]
    total = add_pairs(terms).astype(jnp.bfloat16)
    gathered = exchange_samples(lambda target: total)
    result = []
    for place in range(count):
        chosen = gathered[0]
        for mask in range(1, count):
            chosen = jnp.where(own ^ mask == place, gathered[mask], chosen)
        result.append(chosen)
    return jnp.concatenate(result, axis=1)


def silu_slope(value):
    logistic = jax.nn.sigmoid(value)
    return logistic * (1.0 + value * (1.0 - logistic))


def to_depth(grid):
    height, across, channels = grid.shape
    blocks = grid.reshape(height // 2, 2, across // 2, 2, channels)
    return jnp.transpose(blocks, (0, 2, 1, 3, 4)).reshape(height // 2, across // 2, 4 * channels)


def from_depth(grid):
    height, across, channels = grid.shape
    blocks = grid.reshape(height, across, 2, 2, channels // 4)
    return jnp.transpose(blocks, (0, 2, 1, 3, 4)).reshape(2 * height, 2 * across, channels // 4)


def shift_columns(grid, offset):
    across = grid.shape[-2]
    pads = [(0, 0)] * grid.ndim
    if offset > 0:
        pads[-2] = (0, offset)
        return jnp.pad(lax.slice_in_dim(grid, offset, across, axis=-2 % grid.ndim), pads)
    if offset < 0:
        pads[-2] = (-offset, 0)
        return jnp.pad(lax.slice_in_dim(grid, 0, across + offset, axis=-2 % grid.ndim), pads)
    return grid


def shift_rows(grid, offset):
    height = grid.shape[-3]
    pads = [(0, 0)] * grid.ndim
    if offset > 0:
        pads[-3] = (0, offset)
        return jnp.pad(lax.slice_in_dim(grid, offset, height, axis=-3 % grid.ndim), pads)
    if offset < 0:
        pads[-3] = (-offset, 0)
        return jnp.pad(lax.slice_in_dim(grid, 0, height + offset, axis=-3 % grid.ndim), pads)
    return grid


def taps(grid, sign):
    columns = [shift_columns(grid, sign * (q - 1)) for q in range(3)]
    return [shift_rows(columns[q], sign * (p - 1)) for p in range(3) for q in range(3)]


def conv_in(grid, weight, sign, transposed):
    height, across, channels = grid.shape
    window = jnp.concatenate(taps(grid, sign), axis=-1).reshape(height * across, 9 * channels)
    if transposed:
        flat = jnp.transpose(weight, (0, 1, 3, 2)).reshape(9 * channels, weight.shape[2])
    else:
        flat = weight.reshape(9 * channels, weight.shape[3])
    result = jnp.dot(window, flat, preferred_element_type=jnp.float32)
    return result.reshape(height, across, -1)


def correlate_samples(left, right):
    samples, height, across, inward = left.shape
    outward = right.shape[-1]
    flat = left.reshape(samples * height * across, inward)
    shifted = jnp.concatenate(taps(right, -1), axis=-1).reshape(-1, 9 * outward)
    result = lax.dot_general(
        flat, shifted, (((0,), (0,)), ((), ())), preferred_element_type=jnp.float32
    )
    return jnp.transpose(result.reshape(inward, 3, 3, outward), (1, 2, 0, 3))


def project(values, weight, dim):
    return lax.dot_general(
        values, weight, (((values.ndim - 1,), (dim,)), ((), ())), preferred_element_type=jnp.float32
    )


def column_mask(shape, column):
    return lax.broadcasted_iota(jnp.int32, shape, 1) == column


def from_left(values, across):
    view = values.reshape(-1, across, values.shape[-1])
    moved = pltpu.roll(view, 1, 1)
    return jnp.where(column_mask(view.shape, 0), 0.0, moved).reshape(values.shape)


def from_right(values, across):
    view = values.reshape(-1, across, values.shape[-1])
    moved = pltpu.roll(view, across - 1, 1)
    return jnp.where(column_mask(view.shape, across - 1), 0.0, moved).reshape(values.shape)


def place_blocks(core, mine_ref, other_ref, padded, rows, across):
    blocks = mine_ref.shape[0] // rows
    for block in range(blocks):
        span = pl.ds(block * rows, rows)
        here = pl.multiple_of(across + (2 * block + core) * rows, 16)
        there = pl.multiple_of(across + (2 * block + 1 - core) * rows, 16)
        padded[pl.ds(here, rows), :] = mine_ref[span, :]
        padded[pl.ds(there, rows), :] = other_ref[span, :]


def clear_edges(padded, across):
    total = padded.shape[0]
    blank = jnp.zeros((across, padded.shape[1]), padded.dtype)
    padded[0:across, :] = blank
    padded[total - across : total, :] = blank


def weight_copies(expand_hbm, reduce_hbm, expand_buf, reduce_buf, sems):
    inner = expand_hbm.shape[-1]
    expand_copies = []
    for p in range(3):
        for q in range(3):
            expand_copies.append(
                pltpu.make_async_copy(
                    expand_hbm.at[p, q],
                    expand_buf.at[p, :, pl.ds(q * inner, inner)],
                    sems.at[3 * p + q],
                )
            )
    reduce_copies = []
    for p in range(3):
        for q in range(3):
            reduce_copies.append(
                pltpu.make_async_copy(
                    reduce_hbm.at[p, q],
                    reduce_buf.at[p, pl.ds(q * inner, inner), :],
                    sems.at[9 + 3 * p + q],
                )
            )
    return expand_copies, reduce_copies


def store_blocks(core, source, own_ref, sent_ref, lane_slice, rows):
    blocks = source.shape[0] // (2 * rows)

    def store(first_ref, second_ref):
        for block in range(blocks):
            for half, target in enumerate((first_ref, second_ref)):
                start = (2 * block + half) * rows
                target[pl.ds(block * rows, rows), lane_slice] = source[start : start + rows, :]

    @pl.when(core == 0)
    def _():
        store(own_ref, sent_ref)

    @pl.when(core != 0)
    def _():
        store(sent_ref, own_ref)


def forward_kernel(
    core_ref, mine_ref, other_ref, expand_hbm, reduce_hbm,
    pre_ref, exp_ref, own_ref, sent_ref,
    padded, shifted, expand_buf, reduce_buf, sems, *, rows, across,
):
    core = core_ref[0]
    expand_copies, reduce_copies = weight_copies(
        expand_hbm, reduce_hbm, expand_buf, reduce_buf, sems
    )
    for copy in expand_copies + reduce_copies:
        copy.start()
    clear_edges(padded, across)
    clear_edges(shifted, across)
    place_blocks(core, mine_ref, other_ref, padded, rows, across)
    inner = expand_hbm.shape[-1]
    positions = pre_ref.shape[0]
    total = None
    for p in range(3):
        for q in range(3):
            expand_copies[3 * p + q].wait()
        term = jnp.dot(
            padded[p * across : p * across + positions, :],
            expand_buf[p],
            preferred_element_type=jnp.float32,
        )
        total = term if total is None else total + term
    pre = (
        total[:, inner : 2 * inner]
        + from_left(total[:, 0:inner], across)
        + from_right(total[:, 2 * inner : 3 * inner], across)
    )
    pre_ref[...] = pre
    expanded = (pre * jax.nn.sigmoid(pre)).astype(jnp.bfloat16)
    exp_ref[...] = expanded
    wide = expanded.astype(jnp.float32)
    shifted[across : across + positions, 0:inner] = from_left(wide, across).astype(jnp.bfloat16)
    shifted[across : across + positions, inner : 2 * inner] = expanded
    shifted[across : across + positions, 2 * inner : 3 * inner] = from_right(wide, across).astype(
        jnp.bfloat16
    )
    for copy in reduce_copies:
        copy.wait()
    base = own_ref.shape[-1]
    chunk = min(256, base)
    for lane in range(0, base, chunk):
        lane_slice = pl.ds(lane, chunk)
        out = None
        for p in range(3):
            term = jnp.dot(
                shifted[p * across : p * across + positions, :],
                reduce_buf[p, :, lane_slice],
                preferred_element_type=jnp.float32,
            )
            out = term if out is None else out + term
        store_blocks(core, out.astype(jnp.bfloat16), own_ref, sent_ref, lane_slice, rows)


def transposed_dot(left, right):
    return lax.dot_general(
        left, right, (((1,), (1,)), ((), ())), preferred_element_type=jnp.float32
    )


def backward_kernel(
    core_ref, mine_ref, other_ref, expand_hbm, reduce_hbm, pre_ref,
    grad_ref, own_ref, sent_ref,
    padded, shifted, expand_buf, reduce_buf, sems, *, rows, across,
):
    core = core_ref[0]
    expand_copies, reduce_copies = weight_copies(
        expand_hbm, reduce_hbm, expand_buf, reduce_buf, sems
    )
    for copy in reduce_copies + expand_copies:
        copy.start()
    clear_edges(padded, across)
    clear_edges(shifted, across)
    place_blocks(core, mine_ref, other_ref, padded, rows, across)
    inner = expand_hbm.shape[-1]
    positions = pre_ref.shape[0]
    total = None
    for p in range(3):
        for q in range(3):
            reduce_copies[3 * p + q].wait()
        start = (2 - p) * across
        term = transposed_dot(padded[start : start + positions, :], reduce_buf[p])
        total = term if total is None else total + term
    back = (
        total[:, inner : 2 * inner]
        + from_right(total[:, 0:inner], across)
        + from_left(total[:, 2 * inner : 3 * inner], across)
    )
    pre = pre_ref[...]
    logistic = jax.nn.sigmoid(pre)
    slope = logistic * (1.0 + pre * (1.0 - logistic))
    grad = (back * slope).astype(jnp.bfloat16)
    grad_ref[...] = grad
    wide = grad.astype(jnp.float32)
    shifted[across : across + positions, 0:inner] = from_right(wide, across).astype(jnp.bfloat16)
    shifted[across : across + positions, inner : 2 * inner] = grad
    shifted[across : across + positions, 2 * inner : 3 * inner] = from_left(wide, across).astype(
        jnp.bfloat16
    )
    for copy in expand_copies:
        copy.wait()
    base = own_ref.shape[-1]
    chunk = min(256, base)
    for lane in range(0, base, chunk):
        lane_slice = pl.ds(lane, chunk)
        out = None
        for p in range(3):
            start = (2 - p) * across
            term = transposed_dot(
                shifted[start : start + positions, :], expand_buf[p, lane_slice, :]
            )
            out = term if out is None else out + term
        store_blocks(core, out.astype(jnp.bfloat16), own_ref, sent_ref, lane_slice, rows)


def bottleneck_call(kernel, core, mine, other, expand_weight, reduce_weight, pre, rows, across):
    positions = 2 * mine.shape[0]
    base = mine.shape[1]
    inner = expand_weight.shape[-1]
    vmem = pl.BlockSpec(memory_space=pltpu.VMEM)
    smem = pl.BlockSpec(memory_space=pltpu.SMEM)
    hbm = pl.BlockSpec(memory_space=pl.ANY)
    inner_bf16 = jax.ShapeDtypeStruct((positions, inner), jnp.bfloat16)
    inner_f32 = jax.ShapeDtypeStruct((positions, inner), jnp.float32)
    part = jax.ShapeDtypeStruct((positions // 2, base), jnp.bfloat16)
    operands = [core, mine, other, expand_weight, reduce_weight]
    specs = [smem, vmem, vmem, hbm, hbm]
    if pre is None:
        outs = (inner_f32, inner_bf16, part, part)
    else:
        outs = (inner_bf16, part, part)
        operands.append(pre)
        specs.append(vmem)
    return pl.pallas_call(
        functools.partial(kernel, rows=rows, across=across),
        out_shape=outs,
        in_specs=specs,
        out_specs=tuple(vmem for _ in outs),
        scratch_shapes=[
            pltpu.VMEM((positions + 2 * across, base), jnp.bfloat16),
            pltpu.VMEM((positions + 2 * across, 3 * inner), jnp.bfloat16),
            pltpu.VMEM((3, base, 3 * inner), jnp.bfloat16),
            pltpu.VMEM((3, 3 * inner, base), jnp.bfloat16),
            pltpu.SemaphoreType.DMA((18,)),
        ],
    )(*operands)


def correlate_kernel(core_ref, *refs, count, rows, across, split_left):
    whole = refs[:count]
    mine = refs[count : 2 * count]
    other = refs[2 * count]
    out_ref = refs[2 * count + 1]
    joined, shifted = refs[2 * count + 2 :]
    core = core_ref[0]
    outward = shifted.shape[-1] // 3
    positions = whole[0].shape[0]
    clear_edges(shifted, across)
    for sample in range(count):
        place_blocks(core, mine[sample], other.at[sample], joined, rows, across)
        split = joined[across : across + positions, :]
        if split_left:
            left, right = split, whole[sample][...]
        else:
            left, right = whole[sample][...], split
        turned = jnp.transpose(left, (1, 0))
        wide = right.astype(jnp.float32)
        shifted[across : across + positions, 0:outward] = from_right(wide, across).astype(
            jnp.bfloat16
        )
        shifted[across : across + positions, outward : 2 * outward] = right
        shifted[across : across + positions, 2 * outward : 3 * outward] = from_left(
            wide, across
        ).astype(jnp.bfloat16)
        for p in range(3):
            start = (2 - p) * across
            term = jnp.dot(
                turned, shifted[start : start + positions, :], preferred_element_type=jnp.float32
            )
            for q in range(3):
                piece = term[:, q * outward : (q + 1) * outward]
                if sample == 0:
                    out_ref[p, q] = piece
                else:
                    out_ref[p, q] += piece


def correlate_call(core, whole, mine, other, split_left, rows, across):
    count = len(whole)
    positions, full_lanes = whole[0].shape
    split_lanes_ = mine[0].shape[1]
    inward, outward = (split_lanes_, full_lanes) if split_left else (full_lanes, split_lanes_)
    vmem = pl.BlockSpec(memory_space=pltpu.VMEM)
    smem = pl.BlockSpec(memory_space=pltpu.SMEM)
    return pl.pallas_call(
        functools.partial(
            correlate_kernel, count=count, rows=rows, across=across, split_left=split_left
        ),
        out_shape=jax.ShapeDtypeStruct((3, 3, inward, outward), jnp.float32),
        in_specs=[smem] + [vmem] * (2 * count + 1),
        out_specs=vmem,
        scratch_shapes=[
            pltpu.VMEM((positions + 2 * across, split_lanes_), jnp.bfloat16),
            pltpu.VMEM((positions + 2 * across, 3 * outward), jnp.bfloat16),
        ],
        name="correlate_kernel",
    )(core, *whole, *mine, other)


def turned_dot(left, right):
    return lax.dot_general(
        left, right, (((0,), (0,)), ((), ())), preferred_element_type=jnp.float32
    )


def fold_ends(shapes, lanes):
    ends = []
    for rows, narrow in shapes:
        ends.append(rows * narrow // lanes + (ends[-1] if ends else 0))
    return ends


def pack_kernel(
    core_ref, stacked_ref, coarse_grad_ref, bottom_ref, stacked_grad_ref,
    window_ref, hidden_grad_ref, joined_ref, logit_grad_ref,
    own_ref, sent_ref, pack_ref, *, rows,
):
    lanes = pack_ref.shape[1]
    base = 0
    for left, right in (
        (stacked_ref, coarse_grad_ref),
        (bottom_ref, stacked_grad_ref),
        (window_ref, hidden_grad_ref),
        (joined_ref, logit_grad_ref),
    ):
        value = turned_dot(left[...], right[...]).astype(jnp.bfloat16)
        times = lanes // value.shape[1]
        part = value.shape[0] // times
        for index in range(times):
            pack_ref[base : base + part, index * value.shape[1] : (index + 1) * value.shape[1]] = (
                value[index * part : (index + 1) * part, :]
            )
        base += part
    if base < pack_ref.shape[0]:
        pack_ref[base:, :] = jnp.zeros((pack_ref.shape[0] - base, lanes), pack_ref.dtype)
    store_blocks(core_ref[0], pack_ref, own_ref, sent_ref, pl.ds(0, lanes), rows)


def pack_call(core, operands, shapes, lanes, wide):
    unit = 16 * wide
    filled = fold_ends(shapes, lanes)[-1]
    padded = -(-filled // unit) * unit
    vmem = pl.BlockSpec(memory_space=pltpu.VMEM)
    half = jax.ShapeDtypeStruct((padded // 2, lanes), jnp.bfloat16)
    return pl.pallas_call(
        functools.partial(pack_kernel, rows=padded // wide),
        out_shape=(half, half),
        in_specs=[pl.BlockSpec(memory_space=pltpu.SMEM)] + [vmem] * len(operands),
        out_specs=(vmem, vmem),
        scratch_shapes=[pltpu.VMEM((padded, lanes), jnp.bfloat16)],
        name="pack_kernel",
    )(core, *operands)


def unpack_kernel(core_ref, mine_ref, other_ref, *refs, rows, narrows):
    out_refs, pack_ref = refs[:-1], refs[-1]
    core = core_ref[0]
    lanes = pack_ref.shape[1]
    for block in range(mine_ref.shape[0] // rows):
        span = pl.ds(block * rows, rows)
        here = pl.multiple_of((2 * block + core) * rows, 16)
        there = pl.multiple_of((2 * block + 1 - core) * rows, 16)
        pack_ref[pl.ds(here, rows), :] = mine_ref[span, :]
        pack_ref[pl.ds(there, rows), :] = other_ref[span, :]
    base = 0
    for out_ref, narrow in zip(out_refs, narrows):
        times = lanes // narrow
        part = out_ref.shape[0] // times
        for index in range(times):
            piece = pack_ref[base : base + part, index * narrow : (index + 1) * narrow]
            out_ref[index * part : (index + 1) * part, :] = piece.astype(jnp.float32)[
                :, : out_ref.shape[1]
            ]
        base += part


def unpack_call(core, mine, other, out_shapes, narrows, rows):
    vmem = pl.BlockSpec(memory_space=pltpu.VMEM)
    return pl.pallas_call(
        functools.partial(unpack_kernel, rows=rows, narrows=narrows),
        out_shape=tuple(jax.ShapeDtypeStruct(shape, jnp.float32) for shape in out_shapes),
        in_specs=[pl.BlockSpec(memory_space=pltpu.SMEM), vmem, vmem],
        out_specs=tuple(vmem for _ in out_shapes),
        scratch_shapes=[pltpu.VMEM((2 * mine.shape[0], mine.shape[1]), jnp.bfloat16)],
        name="unpack_kernel",
    )(core, mine, other)


def lane_slices(mine):
    narrow = mine.shape[1] // lax.axis_size("samp")
    return exchange_samples(
        lambda target: lax.dynamic_slice_in_dim(mine, target * narrow, narrow, axis=1)
    )


def step(
    features,
    labels,
    conv_weight,
    down_weight,
    expand_weight,
    reduce_weight,
    up_weight,
    class_weight,
):
    crop_rows = features[0]
    label_map = labels[0]
    height, across, channels = crop_rows.shape
    wide = lax.axis_size("wide")
    pixel_count = wide * lax.axis_size("samp") * height * across
    loss_scale = 8.0 / math.sqrt(pixel_count)
    classes = lax.broadcasted_iota(jnp.int32, (1, 1, class_weight.shape[1]), 2)

    forward = [(i, i + 1) for i in range(wide - 1)]
    backward = [(target, source) for source, target in forward]
    above = lax.ppermute(crop_rows[-1:], "wide", forward)
    below = lax.ppermute(crop_rows[:1], "wide", backward)
    near_rows = jnp.concatenate([above, crop_rows, below], axis=0)
    columns = [shift_columns(near_rows, q - 1) for q in range(3)]
    window = jnp.concatenate(
        [columns[q][p : p + height] for p in range(3) for q in range(3)], axis=-1
    ).reshape(height * across, 9 * channels)
    hidden_pre = jnp.dot(
        window, conv_weight.reshape(9 * channels, -1), preferred_element_type=jnp.float32
    ).reshape(height, across, -1)
    hidden = jax.nn.silu(hidden_pre).astype(jnp.bfloat16)
    stacked = to_depth(hidden)
    low_rows, low_across, _ = stacked.shape
    coarse = project(stacked, down_weight, 0).astype(jnp.bfloat16)
    base = coarse.shape[-1]
    block_rows = low_rows * low_across
    core = bit_of("wide", 1).astype(jnp.int32).reshape(1)
    inner = expand_weight.shape[-1]
    samples = lax.axis_size("samp")
    narrow = base // samples
    grid = (wide * low_rows, low_across)
    own_kernels = inner % 128 == 0 and narrow % 128 == 0 and block_rows % 16 == 0
    coarse_mine = gather_chips(coarse.reshape(block_rows, base))
    coarse_other = swap(coarse_mine, "wide", 1)
    if own_kernels:
        expand_pre, expanded, *partial = bottleneck_call(
            forward_kernel, core, coarse_mine, coarse_other, expand_weight, reduce_weight,
            None, block_rows, low_across,
        )
    else:
        coarse_all = join_cores(coarse_mine, coarse_other, block_rows)
        expand_grid = conv_in(coarse_all.reshape(*grid, base), expand_weight, 1, False)
        expanded_grid = jax.nn.silu(expand_grid).astype(jnp.bfloat16)
        partial = part_cores(
            conv_in(expanded_grid, reduce_weight, 1, False).astype(jnp.bfloat16).reshape(-1, base),
            block_rows,
        )
        expand_pre = expand_grid.reshape(-1, inner)
        expanded = expanded_grid.reshape(-1, inner)
    coarse_slices = lane_slices(coarse_mine)
    coarse_slices_other = swap(jnp.stack(coarse_slices), "wide", 1)
    expanded_samples = exchange_samples(lambda target: expanded)
    summed = scatter_chips(scatter_cores(partial)).reshape(low_rows, low_across, base)
    bottom = (coarse.astype(jnp.float32) + summed).astype(jnp.bfloat16)
    upward = from_depth(project(bottom, up_weight, 0))
    joined_pre = upward + hidden.astype(jnp.float32)
    joined = jax.nn.silu(joined_pre).astype(jnp.bfloat16)
    logits = jnp.dot(joined, class_weight, preferred_element_type=jnp.float32)
    exp_logits = jnp.exp(logits)
    probability = exp_logits / jnp.sum(exp_logits, axis=-1, keepdims=True)
    onehot = (label_map[:, :, None] == classes).astype(jnp.float32)
    logit_grad = ((probability - onehot) * loss_scale).astype(jnp.bfloat16)
    joined_grad = project(logit_grad, class_weight, 1)
    upward_grad = (joined_grad * silu_slope(joined_pre)).astype(jnp.bfloat16)
    stacked_grad = to_depth(upward_grad)
    bottom_grad = project(stacked_grad, up_weight, 1).astype(jnp.bfloat16)
    bottom_mine = gather_chips(bottom_grad.reshape(block_rows, base))
    bottom_other = swap(bottom_mine, "wide", 1)
    if own_kernels:
        expanded_grad, *back_partial = bottleneck_call(
            backward_kernel, core, bottom_mine, bottom_other, expand_weight, reduce_weight,
            expand_pre, block_rows, low_across,
        )
    else:
        bottom_all = join_cores(bottom_mine, bottom_other, block_rows)
        expanded_back = conv_in(bottom_all.reshape(*grid, base), reduce_weight, -1, True)
        grad_grid = (expanded_back * silu_slope(expand_grid)).astype(jnp.bfloat16)
        back_partial = part_cores(
            conv_in(grad_grid, expand_weight, -1, True).astype(jnp.bfloat16).reshape(-1, base),
            block_rows,
        )
        expanded_grad = grad_grid.reshape(-1, inner)
    bottom_slices = lane_slices(bottom_mine)
    bottom_slices_other = swap(jnp.stack(bottom_slices), "wide", 1)
    grad_samples = exchange_samples(lambda target: expanded_grad)
    back_sum = scatter_chips(scatter_cores(back_partial)).reshape(low_rows, low_across, base)
    coarse_grad = (bottom_grad.astype(jnp.float32) + back_sum).astype(jnp.bfloat16)
    down_back = project(coarse_grad, down_weight, 1)
    hidden_sum = from_depth(down_back) + upward_grad.astype(jnp.float32)
    hidden_grad = (hidden_sum * silu_slope(hidden_pre)).astype(jnp.bfloat16)

    lanes = base
    class_lanes = 128
    class_count = class_weight.shape[1]
    logit_pad = jnp.pad(
        logit_grad.reshape(-1, class_count), ((0, 0), (0, class_lanes - class_count))
    )
    flat_window = window.reshape(height * across, -1)
    operands = (
        stacked.reshape(block_rows, -1),
        coarse_grad.reshape(block_rows, -1),
        bottom.reshape(block_rows, -1),
        stacked_grad.reshape(block_rows, -1),
        flat_window,
        hidden_grad.reshape(height * across, -1),
        joined.reshape(height * across, -1),
        logit_pad,
    )
    shapes = tuple(
        (left.shape[1], right.shape[1]) for left, right in zip(operands[::2], operands[1::2])
    )
    packed = pack_call(core, operands, shapes, lanes, wide)
    started = scatter_cores(packed)

    if own_kernels:
        late_core = lax.optimization_barrier((core, started))[0]
        reduce_grad = correlate_call(
            late_core, expanded_samples, bottom_slices, bottom_slices_other, False,
            block_rows, low_across,
        )
        expand_grad = correlate_call(
            late_core, grad_samples, coarse_slices, coarse_slices_other, True,
            block_rows, low_across,
        )
    else:

        def join_samples(mine, other):
            joined = [join_cores(mine[i], other[i], block_rows) for i in range(samples)]
            return jnp.stack(joined).reshape(samples, *grid, narrow)

        reduce_grad = correlate_samples(
            jnp.stack(expanded_samples).reshape(samples, *grid, inner),
            join_samples(bottom_slices, bottom_slices_other),
        )
        expand_grad = correlate_samples(
            join_samples(coarse_slices, coarse_slices_other),
            jnp.stack(grad_samples).reshape(samples, *grid, inner),
        )

    scattered = scatter_chips(started)
    own_total = sum_samples(scattered)
    total_mine = gather_chips(own_total)
    total_other = swap(total_mine, "wide", 1)
    out_shapes = shapes[:3] + ((shapes[3][0], class_count),)
    down_total, up_total, conv_total, class_total = unpack_call(
        core, total_mine, total_other, out_shapes, tuple(shape[1] for shape in shapes),
        own_total.shape[0],
    )
    return (
        conv_total.reshape(conv_weight.shape),
        down_total,
        expand_grad,
        reduce_grad,
        up_total,
        class_total,
    )


def solution(mesh):
    return jax.shard_map(
        step,
        mesh=mesh,
        in_specs=(
            P("samp", "wide", None, None),
            P("samp", "wide", None),
            P(),
            P(),
            P(None, None, None, "wide"),
            P(None, None, "wide", None),
            P(),
            P(),
        ),
        out_specs=(
            P(),
            P(),
            P(None, None, "samp", "wide"),
            P(None, None, "wide", "samp"),
            P(),
            P(),
        ),
        check_vma=False,
    )
```

```python
import functools
import math

import jax
import jax.numpy as jnp
from jax import lax
from jax.experimental import pallas as pl
from jax.experimental.pallas import tpu as pltpu
from jax.sharding import PartitionSpec as P


def swap(values, axis, mask):
    count = lax.axis_size(axis)
    return lax.ppermute(values, axis, [(i, i ^ mask) for i in range(count)])


def chip_count():
    return lax.axis_size("wide") // 2


def gather_chips(piece):
    return [piece] + [swap(piece, "wide", 2 * r) for r in range(1, chip_count())]


def swap_cores(pieces):
    return [swap(piece, "wide", 1) for piece in pieces]


def scatter_chips(own, sent):
    chips = len(own)
    order = list(range(1, chips)) + [0]
    partner = {r: swap(sent[r], "wide", 1) for r in order}
    sends = [add_all(own[r], [partner[r]]).astype(jnp.bfloat16) for r in range(1, chips)]
    return [own[0], partner[0]] + send_chips(sends)


def send_chips(sends):
    return [swap(piece, "wide", 2 * (r + 1)) for r, piece in enumerate(sends)]


def send_samples(sends):
    return [swap(piece, "samp", mask + 1) for mask, piece in enumerate(sends)]


def lane_block(values, target, count):
    narrow = values.shape[-1] // count
    return lax.dynamic_slice_in_dim(values, target * narrow, narrow, axis=values.ndim - 1)


def add_all(first, rest):
    total = first.astype(jnp.float32)
    for item in rest:
        total = total + item.astype(jnp.float32)
    return total


def silu_slope(value):
    logistic = jax.nn.sigmoid(value)
    return logistic * (1.0 + value * (1.0 - logistic))


def column_mask(shape, column):
    return lax.broadcasted_iota(jnp.int32, shape, 1) == column


def from_left(values, across):
    view = values.reshape(-1, across, values.shape[-1])
    moved = pltpu.roll(view, 1, 1)
    return jnp.where(column_mask(view.shape, 0), 0.0, moved).reshape(values.shape)


def from_right(values, across):
    view = values.reshape(-1, across, values.shape[-1])
    moved = pltpu.roll(view, across - 1, 1)
    return jnp.where(column_mask(view.shape, across - 1), 0.0, moved).reshape(values.shape)


def block_start(place_ref, relative, half, rows, offset=0):
    chip = place_ref[1] ^ relative
    core = place_ref[0] ^ half
    return pl.multiple_of(offset + (2 * chip + core) * rows, 16)


def clear_edges(padded, across):
    total = padded.shape[0]
    blank = jnp.zeros((across, padded.shape[1]), padded.dtype)
    padded[0:across, :] = blank
    padded[total - across : total, :] = blank


def weight_copies(expand_hbm, reduce_hbm, expand_buf, reduce_buf, sems):
    inner = expand_hbm.shape[-1]
    base = expand_hbm.shape[-2]
    expand_copies = []
    reduce_copies = []
    for p in range(3):
        for q in range(3):
            expand_copies.append(
                pltpu.make_async_copy(
                    expand_hbm.at[p, q],
                    expand_buf.at[pl.ds(p * base, base), pl.ds(q * inner, inner)],
                    sems.at[3 * p + q],
                )
            )
            reduce_copies.append(
                pltpu.make_async_copy(
                    reduce_hbm.at[p, q],
                    reduce_buf.at[pl.ds((3 * p + q) * inner, inner), :],
                    sems.at[9 + 3 * p + q],
                )
            )
    return expand_copies, reduce_copies


def wait_all(copies):
    for copy in copies:
        copy.wait()


def plain_dot(left, right):
    return jnp.dot(left, right, preferred_element_type=jnp.float32)


def transposed_dot(left, right):
    return lax.dot_general(
        left, right, (((1,), (1,)), ((), ())), preferred_element_type=jnp.float32
    )


def gather_blocks(shifted, place_ref, half, offset, rows, blocks):
    return jnp.concatenate(
        [
            shifted[pl.ds(block_start(place_ref, block, half, rows, offset), rows), :]
            for block in range(blocks)
        ],
        axis=0,
    )


def store_rows(value, targets):
    rows = targets[0].shape[0]
    for index, target in enumerate(targets):
        target[...] = value[index * rows : (index + 1) * rows, :]


def forward_kernel(place_ref, *refs, blocks, rows, across):
    pieces = refs[: 2 * blocks]
    expand_hbm, reduce_hbm, pre_ref, exp_ref = refs[2 * blocks : 2 * blocks + 4]
    own_refs = refs[2 * blocks + 4 : 3 * blocks + 4]
    sent_refs = refs[3 * blocks + 4 : 4 * blocks + 4]
    padded, shifted, expand_buf, reduce_buf, sems = refs[4 * blocks + 4 :]
    expand_copies, reduce_copies = weight_copies(
        expand_hbm, reduce_hbm, expand_buf, reduce_buf, sems
    )
    for copy in expand_copies + reduce_copies:
        copy.start()
    clear_edges(padded, across)
    clear_edges(shifted, across)
    for index, piece in enumerate(pieces):
        start = block_start(place_ref, index % blocks, index // blocks, rows, across)
        padded[pl.ds(start, rows), :] = piece[...]
    inner = expand_hbm.shape[-1]
    base = expand_hbm.shape[-2]
    positions = pre_ref.shape[0]
    total = None
    for p in range(3):
        wait_all(expand_copies[3 * p : 3 * p + 3])
        term = plain_dot(
            padded[p * across : p * across + positions, :],
            expand_buf[p * base : (p + 1) * base, :],
        )
        total = term if total is None else total + term
    pre = (
        total[:, inner : 2 * inner]
        + from_left(total[:, 0:inner], across)
        + from_right(total[:, 2 * inner : 3 * inner], across)
    )
    pre_ref[...] = pre
    expanded = (pre * jax.nn.sigmoid(pre)).astype(jnp.bfloat16)
    exp_ref[...] = expanded
    wide = expanded.astype(jnp.float32)
    inside = pl.ds(across, positions)
    shifted[inside, 0:inner] = from_left(wide, across).astype(jnp.bfloat16)
    shifted[inside, inner : 2 * inner] = expanded
    shifted[inside, 2 * inner : 3 * inner] = from_right(wide, across).astype(jnp.bfloat16)
    wait_all(reduce_copies)
    for half, targets in ((1, sent_refs), (0, own_refs)):
        left = jnp.concatenate(
            [
                gather_blocks(shifted, place_ref, half, p * across, rows, blocks)
                for p in range(3)
            ],
            axis=1,
        )
        store_rows(plain_dot(left, reduce_buf[...]).astype(jnp.bfloat16), targets)


def backward_kernel(place_ref, *refs, blocks, rows, across):
    pieces = refs[: 2 * blocks]
    expand_hbm, reduce_hbm, pre_ref, grad_ref = refs[2 * blocks : 2 * blocks + 4]
    own_refs = refs[2 * blocks + 4 : 3 * blocks + 4]
    sent_refs = refs[3 * blocks + 4 : 4 * blocks + 4]
    padded, shifted, expand_buf, reduce_buf, sems = refs[4 * blocks + 4 :]
    expand_copies, reduce_copies = weight_copies(
        expand_hbm, reduce_hbm, expand_buf, reduce_buf, sems
    )
    for copy in reduce_copies + expand_copies:
        copy.start()
    clear_edges(padded, across)
    clear_edges(shifted, across)
    for index, piece in enumerate(pieces):
        start = block_start(place_ref, index % blocks, index // blocks, rows, across)
        padded[pl.ds(start, rows), :] = piece[...]
    inner = expand_hbm.shape[-1]
    base = expand_hbm.shape[-2]
    positions = pre_ref.shape[0]
    total = None
    for p in range(3):
        wait_all(reduce_copies[3 * p : 3 * p + 3])
        start = (2 - p) * across
        term = transposed_dot(
            padded[start : start + positions, :],
            reduce_buf[3 * p * inner : 3 * (p + 1) * inner, :],
        )
        total = term if total is None else total + term
    back = (
        total[:, inner : 2 * inner]
        + from_right(total[:, 0:inner], across)
        + from_left(total[:, 2 * inner : 3 * inner], across)
    )
    pre = pre_ref[...]
    grad = (back * silu_slope(pre)).astype(jnp.bfloat16)
    grad_ref[...] = grad
    wide = grad.astype(jnp.float32)
    inside = pl.ds(across, positions)
    shifted[inside, 0:inner] = from_right(wide, across).astype(jnp.bfloat16)
    shifted[inside, inner : 2 * inner] = grad
    shifted[inside, 2 * inner : 3 * inner] = from_left(wide, across).astype(jnp.bfloat16)
    wait_all(expand_copies)
    for half, targets in ((1, sent_refs), (0, own_refs)):
        out = None
        for p in range(3):
            left = gather_blocks(shifted, place_ref, half, (2 - p) * across, rows, blocks)
            term = transposed_dot(left, expand_buf[p * base : (p + 1) * base, :])
            out = term if out is None else out + term
        store_rows(out.astype(jnp.bfloat16), targets)


BOTTLENECK_MIB = 12
CORRELATE_MIB = 8
SMALL_MIB = 6

VMEM_SPEC = pl.BlockSpec(memory_space=pltpu.VMEM)
SMEM_SPEC = pl.BlockSpec(memory_space=pltpu.SMEM)
HBM_SPEC = pl.BlockSpec(memory_space=pltpu.HBM)


def granted(operands, outs, scratch, temporaries):
    total = sum(math.prod(item.shape) * item.dtype.itemsize for item in (*operands, *outs))
    total += sum(math.prod(shape) * jnp.dtype(dtype).itemsize for shape, dtype in scratch)
    limit = min(int(total * 1.1) + (temporaries << 20), 60 << 20)
    return pltpu.CompilerParams(vmem_limit_bytes=limit)


def bottleneck_call(kernel, place, pieces, expand_weight, reduce_weight, pre, across):
    rows, base = pieces[0].shape
    positions = len(pieces) * rows
    inner = expand_weight.shape[-1]
    inner_bf16 = jax.ShapeDtypeStruct((positions, inner), jnp.bfloat16)
    inner_f32 = jax.ShapeDtypeStruct((positions, inner), jnp.float32)
    parts = (jax.ShapeDtypeStruct((rows, base), jnp.bfloat16),) * len(pieces)
    operands = [place, *pieces, expand_weight, reduce_weight]
    specs = [SMEM_SPEC] + [VMEM_SPEC] * len(pieces) + [HBM_SPEC] * 2
    if pre is None:
        outs = (inner_f32, inner_bf16) + parts
    else:
        outs = (inner_bf16,) + parts
        operands.append(pre)
        specs.append(VMEM_SPEC)
    return pl.pallas_call(
        functools.partial(kernel, blocks=len(pieces) // 2, rows=rows, across=across),
        out_shape=outs,
        in_specs=specs,
        out_specs=tuple(VMEM_SPEC for _ in outs),
        scratch_shapes=[
            pltpu.VMEM((positions + 2 * across, base), jnp.bfloat16),
            pltpu.VMEM((positions + 2 * across, 3 * inner), jnp.bfloat16),
            pltpu.VMEM((3 * base, 3 * inner), jnp.bfloat16),
            pltpu.VMEM((9 * inner, base), jnp.bfloat16),
            pltpu.SemaphoreType.DMA((18,)),
        ],
        compiler_params=granted(
            (*pieces, expand_weight, reduce_weight), outs,
            (
                ((positions + 2 * across, base), jnp.bfloat16),
                ((positions + 2 * across, 3 * inner), jnp.bfloat16),
            ),
            BOTTLENECK_MIB,
        ),
    )(*operands)


def correlate_kernel(place_ref, *refs, count, blocks, across, first_slice, split_left):
    whole = refs[:count]
    own = refs[count : count + 2 * blocks]
    others = refs[count + 2 * blocks : count + 4 * blocks]
    out_ref, joined, shifted = refs[count + 4 * blocks :]
    rows = own[0].shape[0]
    outward = shifted.shape[-1] // 3
    narrow = joined.shape[-1]
    positions = whole[0].shape[0]
    clear_edges(shifted, across)
    inside = pl.ds(across, positions)
    lane = pl.multiple_of(place_ref[2] * narrow, 128)
    for sample in range(count):
        for index in range(2 * blocks):
            start = block_start(place_ref, index % blocks, index // blocks, rows)
            if sample == 0:
                piece = own[index][:, pl.ds(lane, narrow)]
            else:
                first = (first_slice + sample - 1) * rows
                piece = others[index][first : first + rows, :]
            joined[pl.ds(start, rows), :] = piece
        if split_left:
            left, right = joined[...], whole[sample][...]
        else:
            left, right = whole[sample][...], joined[...]
        turned = jnp.transpose(left, (1, 0))
        wide = right.astype(jnp.float32)
        shifted[inside, 0:outward] = from_right(wide, across).astype(jnp.bfloat16)
        shifted[inside, outward : 2 * outward] = right
        shifted[inside, 2 * outward : 3 * outward] = from_left(wide, across).astype(jnp.bfloat16)
        for p in range(3):
            start = (2 - p) * across
            term = plain_dot(turned, shifted[start : start + positions, :])
            for q in range(3):
                piece = term[:, q * outward : (q + 1) * outward]
                if sample == 0:
                    out_ref[p, q] = piece
                else:
                    out_ref[p, q] += piece


def correlate_call(place, whole, own, others, first_slice, split_left, across):
    count = len(whole)
    positions, full_lanes = whole[0].shape
    part_lanes = others[0].shape[1]
    inward, outward = (part_lanes, full_lanes) if split_left else (full_lanes, part_lanes)
    out = jax.ShapeDtypeStruct((3, 3, inward, outward), jnp.float32)
    scratch = (
        ((positions, part_lanes), jnp.bfloat16),
        ((positions + 2 * across, 3 * outward), jnp.bfloat16),
    )
    return pl.pallas_call(
        functools.partial(
            correlate_kernel, count=count, blocks=len(own) // 2, across=across,
            first_slice=first_slice, split_left=split_left,
        ),
        out_shape=out,
        in_specs=[SMEM_SPEC] + [VMEM_SPEC] * (count + len(own) + len(others)),
        out_specs=VMEM_SPEC,
        scratch_shapes=[pltpu.VMEM(*item) for item in scratch],
        compiler_params=granted((*whole, *own, *others), (out,), scratch, CORRELATE_MIB),
        name="correlate_kernel",
    )(place, *whole, *own, *others)


def fetch(source, target, sem):
    copy = pltpu.make_async_copy(source, target, sem)
    copy.start()
    return copy


def store_lane_blocks(place_ref, source, targets):
    narrow = targets[0].shape[1]
    for index, target in enumerate(targets):
        lane = pl.multiple_of((place_ref[2] ^ (index + 1)) * narrow, 128)
        target[...] = source[:, pl.ds(lane, narrow)]


def front_kernel(place_ref, crop_ref, above_ref, below_ref, conv_hbm, down_hbm, *refs, across):
    columns_ref, pre_ref, stacked_ref, coarse_ref = refs[:4]
    slice_refs = refs[4:-5]
    near_ref, grid_ref, conv_buf, down_buf, sems = refs[-5:]
    conv_copy = fetch(conv_hbm, conv_buf, sems.at[0])
    down_copy = fetch(down_hbm, down_buf, sems.at[1])
    positions = crop_ref.shape[0]
    channels = crop_ref.shape[1]
    near_ref[0:across, :] = above_ref[...]
    near_ref[across : across + positions, :] = crop_ref[...]
    near_ref[across + positions :, :] = below_ref[...]
    wide = near_ref[...].astype(jnp.float32)
    columns_ref[:, 0:channels] = from_left(wide, across).astype(jnp.bfloat16)
    columns_ref[:, channels : 2 * channels] = near_ref[...]
    columns_ref[:, 2 * channels :] = from_right(wide, across).astype(jnp.bfloat16)
    left = jnp.concatenate(
        [columns_ref[p * across : p * across + positions, :] for p in range(3)], axis=1
    )
    conv_copy.wait()
    grid_ref[...] = plain_dot(left, conv_buf[...])
    out = grid_ref.shape[1]
    half = across // 2
    for i in range(positions // (2 * across)):
        for a in range(2):
            for b in range(2):
                lane = (2 * a + b) * out
                pre_ref[i * half : (i + 1) * half, lane : lane + out] = grid_ref[
                    pl.ds((2 * i + a) * across + b, half, stride=2), :
                ]
    pre = pre_ref[...]
    stacked = (pre * jax.nn.sigmoid(pre)).astype(jnp.bfloat16)
    stacked_ref[...] = stacked
    down_copy.wait()
    coarse_ref[...] = plain_dot(stacked, down_buf[...]).astype(jnp.bfloat16)
    store_lane_blocks(place_ref, coarse_ref, slice_refs)


def front_call(place, crop, above, below, conv_flat, down_weight, across, samples):
    positions, channels = crop.shape
    out = conv_flat.shape[1]
    low = positions // 4
    base = down_weight.shape[1]
    outs = (
        jax.ShapeDtypeStruct((positions + 2 * across, 3 * channels), jnp.bfloat16),
        jax.ShapeDtypeStruct((low, 4 * out), jnp.float32),
        jax.ShapeDtypeStruct((low, 4 * out), jnp.bfloat16),
        jax.ShapeDtypeStruct((low, base), jnp.bfloat16),
    )
    outs += (jax.ShapeDtypeStruct((low, base // samples), jnp.bfloat16),) * (samples - 1)
    scratch = (
        ((positions + 2 * across, channels), jnp.bfloat16),
        ((positions, out), jnp.float32),
        (conv_flat.shape, jnp.bfloat16),
        (down_weight.shape, jnp.bfloat16),
    )
    return pl.pallas_call(
        functools.partial(front_kernel, across=across),
        out_shape=outs,
        in_specs=[SMEM_SPEC] + [VMEM_SPEC] * 3 + [HBM_SPEC] * 2,
        out_specs=(VMEM_SPEC,) * len(outs),
        scratch_shapes=[pltpu.VMEM(*item) for item in scratch] + [pltpu.SemaphoreType.DMA((2,))],
        compiler_params=granted((crop, above, below), outs, scratch, SMALL_MIB),
        name="front_kernel",
    )(place, crop, above, below, conv_flat, down_weight)


def middle_kernel(place_ref, *refs, count, loss_scale, class_count):
    first_ref, terms = refs[0], refs[1:count]
    coarse_ref, stacked_ref, label_ref, class_turned_ref, up_hbm = refs[count : count + 5]
    bottom_ref, joined_ref, logit_grad_ref, stacked_grad_ref, bottom_grad_ref = refs[
        count + 5 : count + 10
    ]
    slice_refs = refs[count + 10 : -3]
    class_ref, up_ref, sems = refs[-3:]
    up_copy = fetch(up_hbm, up_ref, sems.at[0])
    lanes, channels = class_ref.shape
    class_ref[...] = jnp.zeros(class_ref.shape, class_ref.dtype)
    class_ref[0:class_count, :] = class_turned_ref[...]
    height, across = label_ref.shape[1:]
    half = across // 2
    label_rows = label_ref[0].astype(jnp.float32).astype(jnp.bfloat16)
    row = lax.broadcasted_iota(jnp.int32, (half, across), 0)
    pixel = lax.broadcasted_iota(jnp.int32, (half, across), 1)
    label_columns = [
        transposed_dot((pixel == 2 * row + b).astype(jnp.float32).astype(jnp.bfloat16), label_rows)
        for b in range(2)
    ]
    total = coarse_ref[...].astype(jnp.float32) + add_all(
        first_ref[...], [term[...] for term in terms]
    )
    bottom = total.astype(jnp.bfloat16)
    bottom_ref[...] = bottom
    up_copy.wait()
    joined_pre = plain_dot(bottom, up_ref[...]) + stacked_ref[...].astype(jnp.float32)
    joined_ref[...] = (joined_pre * jax.nn.sigmoid(joined_pre)).astype(jnp.bfloat16)
    slope = silu_slope(joined_pre)
    column = lax.broadcasted_iota(jnp.int32, (joined_pre.shape[0], lanes), 1)
    column_value = column.astype(jnp.float32)
    for a in range(2):
        for b in range(2):
            block = 2 * a + b
            span = slice(block * channels, (block + 1) * channels)
            label = jnp.concatenate(
                [label_columns[b][:, 2 * i + a : 2 * i + a + 1] for i in range(height // 2)],
                axis=0,
            )
            logits = transposed_dot(joined_ref[:, span], class_ref[...])
            powers = jnp.where(column < class_count, jnp.exp(logits), 0.0)
            probability = powers / jnp.sum(powers, axis=-1, keepdims=True)
            onehot = (column_value == label).astype(jnp.float32)
            logit_grad = ((probability - onehot) * loss_scale).astype(jnp.bfloat16)
            logit_grad_ref[:, block * lanes : (block + 1) * lanes] = logit_grad
            joined_grad = plain_dot(logit_grad, class_ref[...])
            stacked_grad_ref[:, span] = (joined_grad * slope[:, span]).astype(jnp.bfloat16)
    bottom_grad_ref[...] = transposed_dot(stacked_grad_ref[...], up_ref[...]).astype(jnp.bfloat16)
    store_lane_blocks(place_ref, bottom_grad_ref, slice_refs)


def middle_call(
    place, first, terms, coarse, stacked, labels, class_turned, up_weight, loss_scale, class_lanes,
    samples,
):
    rows, base = coarse.shape
    wide = stacked.shape[1]
    channels = class_turned.shape[1]
    shapes = (base, wide, wide // channels * class_lanes, wide, base)
    shapes += (base // samples,) * (samples - 1)
    outs = tuple(jax.ShapeDtypeStruct((rows, lanes), jnp.bfloat16) for lanes in shapes)
    operands = (first, *terms, coarse, stacked, labels, class_turned)
    scratch = (((class_lanes, channels), jnp.bfloat16), (up_weight.shape, jnp.bfloat16))
    return pl.pallas_call(
        functools.partial(
            middle_kernel, count=1 + len(terms), loss_scale=loss_scale,
            class_count=class_turned.shape[0],
        ),
        out_shape=outs,
        in_specs=[SMEM_SPEC] + [VMEM_SPEC] * len(operands) + [HBM_SPEC],
        out_specs=(VMEM_SPEC,) * len(outs),
        scratch_shapes=[pltpu.VMEM(*item) for item in scratch] + [pltpu.SemaphoreType.DMA((1,))],
        compiler_params=granted(operands, outs, scratch, SMALL_MIB),
        name="middle_kernel",
    )(place, *operands, up_weight)


def sum_kernel(place_ref, *refs, count, slices):
    first_ref, terms = refs[0], refs[1:count]
    slice_refs = refs[count : count + slices]
    own_ref = refs[count + slices]
    send_refs = refs[count + slices + 1 : -2]
    stack_ref, total_ref = refs[-2:]
    total_ref[...] = add_all(first_ref[...], [term[...] for term in terms]).astype(jnp.bfloat16)
    narrow = own_ref.shape[1]
    own_ref[...] = total_ref[:, pl.ds(pl.multiple_of(place_ref[2] * narrow, 128), narrow)]
    store_lane_blocks(place_ref, total_ref, send_refs)
    for index, source in enumerate(slice_refs):
        rows = source.shape[0]
        stack_ref[index * rows : (index + 1) * rows, :] = source[...]


def sum_call(place, first, terms, slices, samples):
    rows, lanes = first.shape
    block = jax.ShapeDtypeStruct((rows, lanes // samples), jnp.bfloat16)
    stack = jax.ShapeDtypeStruct((len(slices) * slices[0].shape[0], slices[0].shape[1]), jnp.bfloat16)
    outs = (block,) * samples + (stack,)
    operands = (first, *terms, *slices)
    scratch = ((first.shape, jnp.bfloat16),)
    return pl.pallas_call(
        functools.partial(sum_kernel, count=1 + len(terms), slices=len(slices)),
        out_shape=outs,
        in_specs=[SMEM_SPEC] + [VMEM_SPEC] * len(operands),
        out_specs=(VMEM_SPEC,) * len(outs),
        scratch_shapes=[pltpu.VMEM(*item) for item in scratch],
        compiler_params=granted(operands, outs, scratch, SMALL_MIB),
        name="sum_kernel",
    )(place, *operands)


def turned_dot(left, right):
    return lax.dot_general(
        left, right, (((0,), (0,)), ((), ())), preferred_element_type=jnp.float32
    )


def pack_kernel(place_ref, *refs, count, blocks, rows, across):
    first_ref, terms = refs[0], refs[1:count]
    (
        bottom_grad_ref, stacked_ref, stacked_grad_ref, pre_ref, bottom_ref,
        columns_ref, joined_ref, logit_grad_ref, down_hbm,
    ) = refs[count : count + 9]
    targets = refs[count + 9 : -4]
    pack_ref, grid_ref, down_ref, sems = refs[-4:]
    down_copy = fetch(down_hbm, down_ref, sems.at[0])
    lanes = pack_ref.shape[1]
    total = bottom_grad_ref[...].astype(jnp.float32) + add_all(
        first_ref[...], [term[...] for term in terms]
    )
    coarse_grad = total.astype(jnp.bfloat16)
    down_copy.wait()
    hidden_sum = transposed_dot(coarse_grad, down_ref[...]) + stacked_grad_ref[...].astype(
        jnp.float32
    )
    hidden_grad = (hidden_sum * silu_slope(pre_ref[...])).astype(jnp.bfloat16).astype(jnp.float32)
    positions, channels = grid_ref.shape
    half = across // 2
    for i in range(positions // (2 * across)):
        for a in range(2):
            for b in range(2):
                lane = (2 * a + b) * channels
                grid_ref[pl.ds((2 * i + a) * across + b, half, stride=2), :] = hidden_grad[
                    i * half : (i + 1) * half, lane : lane + channels
                ]
    grid = grid_ref[...].astype(jnp.bfloat16)

    def store(value, base):
        rounded = value.astype(jnp.bfloat16)
        times = lanes // value.shape[1]
        part = value.shape[0] // times
        for index in range(times):
            pack_ref[base : base + part, index * value.shape[1] : (index + 1) * value.shape[1]] = (
                rounded[index * part : (index + 1) * part, :]
            )
        return base + part

    base = store(turned_dot(stacked_ref[...], coarse_grad), 0)
    base = store(turned_dot(bottom_ref[...], stacked_grad_ref[...]), base)
    conv_grad = jnp.concatenate(
        [
            turned_dot(columns_ref[p * across : p * across + positions, :], grid)
            for p in range(3)
        ],
        axis=0,
    )
    base = store(conv_grad, base)
    class_grad = None
    class_lanes = logit_grad_ref.shape[1] // (joined_ref.shape[1] // channels)
    for block in range(joined_ref.shape[1] // channels):
        term = turned_dot(
            logit_grad_ref[:, block * class_lanes : (block + 1) * class_lanes],
            joined_ref[:, block * channels : (block + 1) * channels],
        )
        class_grad = term if class_grad is None else class_grad + term
    base = store(class_grad, base)
    if base < pack_ref.shape[0]:
        pack_ref[base:, :] = jnp.zeros((pack_ref.shape[0] - base, lanes), pack_ref.dtype)
    for index, target in enumerate(targets):
        start = block_start(place_ref, index % blocks, index // blocks, rows)
        target[...] = pack_ref[pl.ds(start, rows), :]


def pack_call(place, first, terms, operands, filled, blocks, across):
    lanes = first.shape[1]
    channels = operands[5].shape[1] // 3
    positions = 4 * first.shape[0]
    unit = 32 * blocks
    padded = -(-filled // unit) * unit
    block = jax.ShapeDtypeStruct((padded // (2 * blocks), lanes), jnp.bfloat16)
    return pl.pallas_call(
        functools.partial(
            pack_kernel, count=1 + len(terms), blocks=blocks, rows=padded // (2 * blocks),
            across=across,
        ),
        out_shape=(block,) * (2 * blocks),
        in_specs=[SMEM_SPEC] + [VMEM_SPEC] * (len(terms) + len(operands)) + [HBM_SPEC],
        out_specs=(VMEM_SPEC,) * (2 * blocks),
        scratch_shapes=[
            pltpu.VMEM((padded, lanes), jnp.bfloat16),
            pltpu.VMEM((positions, channels), jnp.float32),
            pltpu.VMEM(operands[-1].shape, jnp.bfloat16),
            pltpu.SemaphoreType.DMA((1,)),
        ],
        compiler_params=granted(
            (first, *terms, *operands), (block,) * (2 * blocks),
            (((padded, lanes), jnp.bfloat16), ((positions, channels), jnp.float32)),
            CORRELATE_MIB,
        ),
        name="pack_kernel",
    )(place, first, *terms, *operands)


def unpack_kernel(place_ref, *refs, blocks, count, shapes):
    pieces = refs[: 2 * blocks]
    out_refs, pack_ref = refs[2 * blocks : -1], refs[-1]
    lanes = pack_ref.shape[1]
    rows = pieces[0].shape[0]
    narrow = lanes // count
    for index, piece in enumerate(pieces):
        start = block_start(place_ref, index % blocks, index // blocks, rows)
        for mask in range(count):
            lane = pl.multiple_of((place_ref[2] ^ mask) * narrow, 128)
            pack_ref[pl.ds(start, rows), pl.ds(lane, narrow)] = piece[
                :, mask * narrow : (mask + 1) * narrow
            ]
    base = 0
    for out_ref, (height, width) in zip(out_refs, shapes):
        times = lanes // width
        part = height // times
        for index in range(times):
            value = pack_ref[base : base + part, index * width : (index + 1) * width]
            kept = min(part, out_ref.shape[0] - index * part)
            if kept > 0:
                out_ref[index * part : index * part + kept, :] = value.astype(jnp.float32)[:kept, :]
        base += part


def unpack_call(place, pieces, count, out_shapes, shapes):
    rows, lanes = pieces[0].shape
    outs = tuple(jax.ShapeDtypeStruct(shape, jnp.float32) for shape in out_shapes)
    scratch = ((rows * len(pieces), lanes), jnp.bfloat16)
    return pl.pallas_call(
        functools.partial(
            unpack_kernel, blocks=len(pieces) // 2, count=count, shapes=shapes
        ),
        out_shape=outs,
        in_specs=[SMEM_SPEC] + [VMEM_SPEC] * len(pieces),
        out_specs=(VMEM_SPEC,) * len(out_shapes),
        scratch_shapes=[pltpu.VMEM(*scratch)],
        compiler_params=granted(pieces, outs, (scratch,), SMALL_MIB),
        name="unpack_kernel",
    )(place, *pieces)


def shift_columns(grid, offset):
    across = grid.shape[-2]
    pads = [(0, 0)] * grid.ndim
    if offset > 0:
        pads[-2] = (0, offset)
        return jnp.pad(lax.slice_in_dim(grid, offset, across, axis=-2 % grid.ndim), pads)
    if offset < 0:
        pads[-2] = (-offset, 0)
        return jnp.pad(lax.slice_in_dim(grid, 0, across + offset, axis=-2 % grid.ndim), pads)
    return grid


def shift_rows(grid, offset):
    height = grid.shape[-3]
    pads = [(0, 0)] * grid.ndim
    if offset > 0:
        pads[-3] = (0, offset)
        return jnp.pad(lax.slice_in_dim(grid, offset, height, axis=-3 % grid.ndim), pads)
    if offset < 0:
        pads[-3] = (-offset, 0)
        return jnp.pad(lax.slice_in_dim(grid, 0, height + offset, axis=-3 % grid.ndim), pads)
    return grid


def taps(grid, sign):
    columns = [shift_columns(grid, sign * (q - 1)) for q in range(3)]
    return [shift_rows(columns[q], sign * (p - 1)) for p in range(3) for q in range(3)]


def conv_in(grid, weight, sign, transposed):
    height, across, channels = grid.shape
    window = jnp.concatenate(taps(grid, sign), axis=-1).reshape(height * across, 9 * channels)
    if transposed:
        flat = jnp.transpose(weight, (0, 1, 3, 2)).reshape(9 * channels, weight.shape[2])
    else:
        flat = weight.reshape(9 * channels, weight.shape[3])
    result = jnp.dot(window, flat, preferred_element_type=jnp.float32)
    return result.reshape(height, across, -1)


def correlate_samples(left, right):
    samples, height, across, inward = left.shape
    outward = right.shape[-1]
    flat = left.reshape(samples * height * across, inward)
    shifted = jnp.concatenate(taps(right, -1), axis=-1).reshape(-1, 9 * outward)
    result = lax.dot_general(
        flat, shifted, (((0,), (0,)), ((), ())), preferred_element_type=jnp.float32
    )
    return jnp.transpose(result.reshape(inward, 3, 3, outward), (1, 2, 0, 3))


def join_blocks(mine, other):
    wide = lax.axis_size("wide")
    own = lax.axis_index("wide")
    stacked = jnp.stack([mine, other], axis=1).reshape((wide,) + mine.shape[1:])
    return stacked[jnp.arange(wide) ^ own].reshape(-1, mine.shape[-1])


def part_blocks(whole):
    wide = lax.axis_size("wide")
    own = lax.axis_index("wide")
    blocks = whole.reshape(wide, -1, whole.shape[-1])[jnp.arange(wide) ^ own]
    halves = blocks.reshape(wide // 2, 2, -1, whole.shape[-1])
    return [halves[r, half] for half in range(2) for r in range(wide // 2)]


def step(
    features,
    labels,
    conv_weight,
    down_weight,
    expand_weight,
    reduce_weight,
    up_weight,
    class_weight,
):
    crop_rows = features[0]
    height, across, channels = crop_rows.shape
    wide = lax.axis_size("wide")
    samples = lax.axis_size("samp")
    chips = chip_count()
    pixel_count = wide * samples * height * across
    loss_scale = 8.0 / math.sqrt(pixel_count)
    own = lax.axis_index("wide")
    place = jnp.stack([own % 2, own // 2, lax.axis_index("samp")]).astype(jnp.int32)
    base = down_weight.shape[1]
    inner = expand_weight.shape[-1]
    narrow = base // samples
    low_rows, low_across = height // 2, across // 2
    block_rows = low_rows * low_across
    grid = (wide * low_rows, low_across)
    class_count = class_weight.shape[1]
    class_lanes = 128
    own_kernels = inner % 128 == 0 and narrow % 128 == 0

    forward = [(i, i + 1) for i in range(wide - 1)]
    backward = [(target, source) for source, target in forward]
    above = lax.ppermute(crop_rows[height - 1], "wide", forward)
    below = lax.ppermute(crop_rows[0], "wide", backward)
    columns, hidden_pre, stacked, coarse, *coarse_sends = front_call(
        place, crop_rows.reshape(height * across, channels), above, below,
        conv_weight.reshape(9 * channels, -1), down_weight, across, samples,
    )
    coarse_mine = gather_chips(coarse)
    coarse_other = swap_cores(coarse_mine)
    if own_kernels:
        expand_pre, expanded, *partial = bottleneck_call(
            forward_kernel, place, coarse_mine + coarse_other, expand_weight, reduce_weight,
            None, low_across,
        )
    else:
        coarse_all = join_blocks(jnp.stack(coarse_mine), jnp.stack(coarse_other))
        expand_grid = conv_in(coarse_all.reshape(*grid, base), expand_weight, 1, False)
        expanded_grid = jax.nn.silu(expand_grid).astype(jnp.bfloat16)
        partial = conv_in(expanded_grid, reduce_weight, 1, False).astype(jnp.bfloat16)
        partial = part_blocks(partial.reshape(-1, base))
        expanded = expanded_grid.reshape(-1, inner)
    coarse_slices = send_samples(coarse_sends)
    expanded_samples = [expanded] + send_samples([expanded] * (samples - 1))
    first, *terms = scatter_chips(partial[:chips], partial[chips:])
    bottom, joined, logit_grad, stacked_grad, bottom_grad, *bottom_sends = middle_call(
        place, first, terms, coarse, stacked, labels, class_weight.T, up_weight, loss_scale,
        class_lanes, samples,
    )
    bottom_mine = gather_chips(bottom_grad)
    bottom_other = swap_cores(bottom_mine)
    if own_kernels:
        expanded_grad, *back = bottleneck_call(
            backward_kernel, place, bottom_mine + bottom_other, expand_weight, reduce_weight,
            expand_pre, low_across,
        )
    else:
        bottom_all = join_blocks(jnp.stack(bottom_mine), jnp.stack(bottom_other))
        expanded_back = conv_in(bottom_all.reshape(*grid, base), reduce_weight, -1, True)
        grad_grid = (expanded_back * silu_slope(expand_grid)).astype(jnp.bfloat16)
        back = conv_in(grad_grid, expand_weight, -1, True).astype(jnp.bfloat16)
        back = part_blocks(back.reshape(-1, base))
        expanded_grad = grad_grid.reshape(-1, inner)
    bottom_slices = send_samples(bottom_sends)
    grad_samples = [expanded_grad] + send_samples([expanded_grad] * (samples - 1))
    first, *terms = scatter_chips(back[:chips], back[chips:])

    conv_out = conv_weight.shape[-1]
    shapes = (
        (down_weight.shape[0], base),
        (base, up_weight.shape[1]),
        (9 * channels, conv_out),
        (class_lanes, conv_out),
    )
    filled = sum(rows * lanes for rows, lanes in shapes) // base
    packed = pack_call(
        place, first, terms,
        (
            bottom_grad, stacked, stacked_grad, hidden_pre, bottom,
            columns, joined, logit_grad, down_weight,
        ),
        filled, chips, across,
    )
    first, *terms = scatter_chips(packed[:chips], packed[chips:])
    own_part, *part_sends, slices = sum_call(
        place, first, terms, coarse_slices + bottom_slices, samples
    )
    parts = send_samples(part_sends)
    slices_mine = gather_chips(slices)
    slices_other = swap_cores(slices_mine)
    total = add_all(own_part, parts).astype(jnp.bfloat16)
    own_total = jnp.concatenate(
        [total] + send_samples([total] * (samples - 1)), axis=1
    )
    total_mine = gather_chips(own_total)
    total_other = swap_cores(total_mine)
    out_shapes = shapes[:3] + ((class_count, conv_out),)
    down_total, up_total, conv_total, class_total = unpack_call(
        place, total_mine + total_other, samples, out_shapes, shapes,
    )

    if own_kernels:
        reduce_grad = correlate_call(
            place, expanded_samples, bottom_mine + bottom_other, slices_mine + slices_other,
            samples - 1, False, low_across,
        )
        expand_grad = correlate_call(
            place, grad_samples, coarse_mine + coarse_other, slices_mine + slices_other,
            0, True, low_across,
        )
    else:

        def join_samples(mine, other, first_slice):
            sample = lax.axis_index("samp")
            mine_all = jnp.stack(mine)
            other_all = jnp.stack(other)
            joined_ = [
                join_blocks(lane_block(mine_all, sample, samples), lane_block(other_all, sample, samples))
            ]
            for i in range(samples - 1):
                span = slice((first_slice + i) * block_rows, (first_slice + i + 1) * block_rows)
                joined_.append(
                    join_blocks(
                        jnp.stack([item[span] for item in slices_mine]),
                        jnp.stack([item[span] for item in slices_other]),
                    )
                )
            return jnp.stack(joined_).reshape(samples, *grid, narrow)

        reduce_grad = correlate_samples(
            jnp.stack(expanded_samples).reshape(samples, *grid, inner),
            join_samples(bottom_mine, bottom_other, samples - 1),
        )
        expand_grad = correlate_samples(
            join_samples(coarse_mine, coarse_other, 0),
            jnp.stack(grad_samples).reshape(samples, *grid, inner),
        )
    return (
        conv_total.reshape(conv_weight.shape),
        down_total,
        expand_grad,
        reduce_grad,
        up_total,
        class_total.T,
    )


def solution(mesh):
    return jax.shard_map(
        step,
        mesh=mesh,
        in_specs=(
            P("samp", "wide", None, None),
            P("samp", "wide", None),
            P(),
            P(),
            P(None, None, None, "wide"),
            P(None, None, "wide", None),
            P(),
            P(),
        ),
        out_specs=(
            P(),
            P(),
            P(None, None, "samp", "wide"),
            P(None, None, "wide", "samp"),
            P(),
            P(),
        ),
        check_vma=False,
    )
```

```python
import functools
import math

import jax
import jax.numpy as jnp
from jax import lax
from jax.experimental import pallas as pl
from jax.experimental.pallas import tpu as pltpu
from jax.sharding import PartitionSpec as P


def swap(values, axis, mask):
    count = lax.axis_size(axis)
    return lax.ppermute(values, axis, [(i, i ^ mask) for i in range(count)])


def chip_count():
    return lax.axis_size("wide") // 2


def gather_chips(piece):
    return [piece] + [swap(piece, "wide", 2 * r) for r in range(1, chip_count())]


def swap_cores(pieces):
    return [swap(piece, "wide", 1) for piece in pieces]


def scatter_chips(own, sent):
    chips = len(own)
    order = list(range(1, chips)) + [0]
    partner = {r: swap(sent[r], "wide", 1) for r in order}
    sends = [add_all(own[r], [partner[r]]).astype(jnp.bfloat16) for r in range(1, chips)]
    return [own[0], partner[0]] + send_chips(sends)


def send_chips(sends):
    return [swap(piece, "wide", 2 * (r + 1)) for r, piece in enumerate(sends)]


def send_samples(sends):
    return [swap(piece, "samp", mask + 1) for mask, piece in enumerate(sends)]


def lane_block(values, target, count):
    narrow = values.shape[-1] // count
    return lax.dynamic_slice_in_dim(values, target * narrow, narrow, axis=values.ndim - 1)


def in_hbm(values):
    return pltpu.with_memory_space_constraint(values, pltpu.HBM)


def add_all(first, rest):
    total = first.astype(jnp.float32)
    for item in rest:
        total = total + item.astype(jnp.float32)
    return total


def silu_slope(value):
    logistic = jax.nn.sigmoid(value)
    return logistic * (1.0 + value * (1.0 - logistic))


def column_mask(shape, column):
    return lax.broadcasted_iota(jnp.int32, shape, 1) == column


def from_left(values, across):
    view = values.reshape(-1, across, values.shape[-1])
    moved = pltpu.roll(view, 1, 1)
    return jnp.where(column_mask(view.shape, 0), 0.0, moved).reshape(values.shape)


def from_right(values, across):
    view = values.reshape(-1, across, values.shape[-1])
    moved = pltpu.roll(view, across - 1, 1)
    return jnp.where(column_mask(view.shape, across - 1), 0.0, moved).reshape(values.shape)


def block_start(place_ref, relative, half, rows, offset=0):
    chip = place_ref[1] ^ relative
    core = place_ref[0] ^ half
    return pl.multiple_of(offset + (2 * chip + core) * rows, 16)


def clear_edges(padded, across):
    total = padded.shape[0]
    blank = jnp.zeros((across, padded.shape[1]), padded.dtype)
    padded[0:across, :] = blank
    padded[total - across : total, :] = blank


def weight_copies(expand_hbm, reduce_hbm, expand_buf, reduce_buf, sems):
    inner = expand_hbm.shape[-1]
    base = expand_hbm.shape[-2]
    expand_copies = []
    reduce_copies = []
    for p in range(3):
        for q in range(3):
            expand_copies.append(
                pltpu.make_async_copy(
                    expand_hbm.at[p, q],
                    expand_buf.at[pl.ds(p * base, base), pl.ds(q * inner, inner)],
                    sems.at[3 * p + q],
                )
            )
            reduce_copies.append(
                pltpu.make_async_copy(
                    reduce_hbm.at[p, q],
                    reduce_buf.at[pl.ds((3 * p + q) * inner, inner), :],
                    sems.at[9 + 3 * p + q],
                )
            )
    return expand_copies, reduce_copies


def wait_all(copies):
    for copy in copies:
        copy.wait()


def plain_dot(left, right):
    return jnp.dot(left, right, preferred_element_type=jnp.float32)


def transposed_dot(left, right):
    return lax.dot_general(
        left, right, (((1,), (1,)), ((), ())), preferred_element_type=jnp.float32
    )


def gather_blocks(shifted, place_ref, half, offset, rows, blocks):
    return jnp.concatenate(
        [
            shifted[pl.ds(block_start(place_ref, block, half, rows, offset), rows), :]
            for block in range(blocks)
        ],
        axis=0,
    )


def fetch(source, target, sem):
    copy = pltpu.make_async_copy(source, target, sem)
    copy.start()
    return copy


def place_pieces(place_ref, pieces, target, blocks):
    rows = pieces[0].shape[0]
    for index, piece in enumerate(pieces):
        start = block_start(place_ref, index % blocks, index // blocks, rows)
        target[pl.ds(start, rows), :] = piece[...]


def store_own_lanes(place_ref, source, rows, target):
    narrow = target.shape[1]
    target[...] = source[rows, pl.ds(pl.multiple_of(place_ref[2] * narrow, 128), narrow)]


def store_rows(value, targets):
    rows = targets[0].shape[0]
    for index, target in enumerate(targets):
        target[...] = value[index * rows : (index + 1) * rows, :]


def forward_kernel(place_ref, *refs, blocks, rows, across):
    pieces = refs[: 2 * blocks]
    outer_hbm, expand_hbm, reduce_hbm, slice_ref, pre_ref, exp_ref = refs[
        2 * blocks : 2 * blocks + 6
    ]
    own_refs = refs[2 * blocks + 6 : 3 * blocks + 6]
    sent_refs = refs[3 * blocks + 6 : 4 * blocks + 6]
    gathered, outer_buf, padded, shifted, expand_buf, reduce_buf, sems = refs[4 * blocks + 6 :]
    outer_copy = fetch(outer_hbm, outer_buf, sems.at[18])
    expand_copies, reduce_copies = weight_copies(
        expand_hbm, reduce_hbm, expand_buf, reduce_buf, sems
    )
    for copy in expand_copies:
        copy.start()
    clear_edges(padded, across)
    clear_edges(shifted, across)
    inner = expand_hbm.shape[-1]
    base = expand_hbm.shape[-2]
    positions = pre_ref.shape[0]
    inside = pl.ds(across, positions)
    place_pieces(place_ref, pieces, gathered, blocks)
    outer_copy.wait()
    wait_all(expand_copies[:3])
    for copy in reduce_copies:
        copy.start()
    padded[inside, :] = plain_dot(gathered[...], outer_buf[...]).astype(jnp.bfloat16)
    store_own_lanes(place_ref, padded, inside, slice_ref)
    total = None
    for p in range(3):
        if p > 0:
            wait_all(expand_copies[3 * p : 3 * p + 3])
        term = plain_dot(
            padded[p * across : p * across + positions, :],
            expand_buf[p * base : (p + 1) * base, :],
        )
        total = term if total is None else total + term
    pre = (
        total[:, inner : 2 * inner]
        + from_left(total[:, 0:inner], across)
        + from_right(total[:, 2 * inner : 3 * inner], across)
    )
    pre_ref[...] = pre
    expanded = (pre * jax.nn.sigmoid(pre)).astype(jnp.bfloat16)
    exp_ref[...] = expanded
    wide = expanded.astype(jnp.float32)
    shifted[inside, 0:inner] = from_left(wide, across).astype(jnp.bfloat16)
    shifted[inside, inner : 2 * inner] = expanded
    shifted[inside, 2 * inner : 3 * inner] = from_right(wide, across).astype(jnp.bfloat16)
    wait_all(reduce_copies)
    for half, targets in ((1, sent_refs), (0, own_refs)):
        left = jnp.concatenate(
            [
                gather_blocks(shifted, place_ref, half, p * across, rows, blocks)
                for p in range(3)
            ],
            axis=1,
        )
        store_rows(plain_dot(left, reduce_buf[...]).astype(jnp.bfloat16), targets)


def backward_kernel(place_ref, *refs, blocks, rows, across):
    pieces = refs[: 2 * blocks]
    outer_hbm, expand_hbm, reduce_hbm, pre_ref, slice_ref, grad_ref = refs[
        2 * blocks : 2 * blocks + 6
    ]
    own_refs = refs[2 * blocks + 6 : 3 * blocks + 6]
    sent_refs = refs[3 * blocks + 6 : 4 * blocks + 6]
    gathered, outer_buf, padded, shifted, expand_buf, reduce_buf, sems = refs[4 * blocks + 6 :]
    outer_copy = fetch(outer_hbm, outer_buf, sems.at[18])
    expand_copies, reduce_copies = weight_copies(
        expand_hbm, reduce_hbm, expand_buf, reduce_buf, sems
    )
    for copy in reduce_copies + expand_copies:
        copy.start()
    clear_edges(padded, across)
    clear_edges(shifted, across)
    inner = expand_hbm.shape[-1]
    base = expand_hbm.shape[-2]
    positions = pre_ref.shape[0]
    inside = pl.ds(across, positions)
    place_pieces(place_ref, pieces, gathered, blocks)
    outer_copy.wait()
    padded[inside, :] = transposed_dot(gathered[...], outer_buf[...]).astype(jnp.bfloat16)
    store_own_lanes(place_ref, padded, inside, slice_ref)
    total = None
    for p in range(3):
        wait_all(reduce_copies[3 * p : 3 * p + 3])
        start = (2 - p) * across
        term = transposed_dot(
            padded[start : start + positions, :],
            reduce_buf[3 * p * inner : 3 * (p + 1) * inner, :],
        )
        total = term if total is None else total + term
    back = (
        total[:, inner : 2 * inner]
        + from_right(total[:, 0:inner], across)
        + from_left(total[:, 2 * inner : 3 * inner], across)
    )
    pre = pre_ref[...]
    grad = (back * silu_slope(pre)).astype(jnp.bfloat16)
    grad_ref[...] = grad
    wide = grad.astype(jnp.float32)
    shifted[inside, 0:inner] = from_right(wide, across).astype(jnp.bfloat16)
    shifted[inside, inner : 2 * inner] = grad
    shifted[inside, 2 * inner : 3 * inner] = from_left(wide, across).astype(jnp.bfloat16)
    wait_all(expand_copies)
    for half, targets in ((1, sent_refs), (0, own_refs)):
        out = None
        for p in range(3):
            left = gather_blocks(shifted, place_ref, half, (2 - p) * across, rows, blocks)
            term = transposed_dot(left, expand_buf[p * base : (p + 1) * base, :])
            out = term if out is None else out + term
        store_rows(out.astype(jnp.bfloat16), targets)


BOTTLENECK_MIB = 12
CORRELATE_MIB = 8
SMALL_MIB = 6

VMEM_SPEC = pl.BlockSpec(memory_space=pltpu.VMEM)
SMEM_SPEC = pl.BlockSpec(memory_space=pltpu.SMEM)
HBM_SPEC = pl.BlockSpec(memory_space=pltpu.HBM)


def granted(operands, outs, scratch, temporaries):
    total = sum(math.prod(item.shape) * item.dtype.itemsize for item in (*operands, *outs))
    total += sum(math.prod(shape) * jnp.dtype(dtype).itemsize for shape, dtype in scratch)
    limit = min(int(total * 1.1) + (temporaries << 20), 60 << 20)
    return pltpu.CompilerParams(vmem_limit_bytes=limit)


def bottleneck_call(
    kernel, place, pieces, outer_weight, expand_weight, reduce_weight, pre, across, samples
):
    rows, outer = pieces[0].shape
    base = expand_weight.shape[-2]
    positions = len(pieces) * rows
    inner = expand_weight.shape[-1]
    inner_bf16 = jax.ShapeDtypeStruct((positions, inner), jnp.bfloat16)
    inner_f32 = jax.ShapeDtypeStruct((positions, inner), jnp.float32)
    parts = (jax.ShapeDtypeStruct((rows, base), jnp.bfloat16),) * len(pieces)
    operands = [place, *pieces, outer_weight, expand_weight, reduce_weight]
    specs = [SMEM_SPEC] + [VMEM_SPEC] * len(pieces) + [HBM_SPEC] * 3
    part = jax.ShapeDtypeStruct((positions, base // samples), jnp.bfloat16)
    if pre is None:
        outs = (part, inner_f32, inner_bf16) + parts
    else:
        outs = (part, inner_bf16) + parts
        operands.append(pre)
        specs.append(VMEM_SPEC)
    return pl.pallas_call(
        functools.partial(kernel, blocks=len(pieces) // 2, rows=rows, across=across),
        out_shape=outs,
        in_specs=specs,
        out_specs=tuple(VMEM_SPEC for _ in outs),
        scratch_shapes=[
            pltpu.VMEM((positions, outer), jnp.bfloat16),
            pltpu.VMEM(outer_weight.shape, jnp.bfloat16),
            pltpu.VMEM((positions + 2 * across, base), jnp.bfloat16),
            pltpu.VMEM((positions + 2 * across, 3 * inner), jnp.bfloat16),
            pltpu.VMEM((3 * base, 3 * inner), jnp.bfloat16),
            pltpu.VMEM((9 * inner, base), jnp.bfloat16),
            pltpu.SemaphoreType.DMA((19,)),
        ],
        compiler_params=granted(
            (*pieces, outer_weight, expand_weight, reduce_weight), outs,
            (
                ((positions, outer), jnp.bfloat16),
                ((positions + 2 * across, base), jnp.bfloat16),
                ((positions + 2 * across, 3 * inner), jnp.bfloat16),
            ),
            BOTTLENECK_MIB,
        ),
    )(*operands)


def correlate_kernel(place_ref, *refs, count, blocks, across, first_slice, split_left):
    whole = refs[:count]
    own = refs[count]
    others = refs[count + 1 : count + 1 + 2 * blocks]
    out_hbm, out_ref, joined, shifted, sems = refs[count + 1 + 2 * blocks :]
    copies = []
    rows = joined.shape[0] // (2 * blocks)
    outward = shifted.shape[-1] // 3
    positions = joined.shape[0]
    clear_edges(shifted, across)
    inside = pl.ds(across, positions)
    for sample in range(count):
        if sample == 0:
            part = own[...]
        else:
            first = (first_slice + sample - 1) * rows
            for index in range(2 * blocks):
                start = block_start(place_ref, index % blocks, index // blocks, rows)
                joined[pl.ds(start, rows), :] = others[index][first : first + rows, :]
            part = joined[...]
        if split_left:
            left, right = part, whole[sample][...]
        else:
            left, right = whole[sample][...], part
        turned = jnp.transpose(left, (1, 0))
        wide = right.astype(jnp.float32)
        shifted[inside, 0:outward] = from_right(wide, across).astype(jnp.bfloat16)
        shifted[inside, outward : 2 * outward] = right
        shifted[inside, 2 * outward : 3 * outward] = from_left(wide, across).astype(jnp.bfloat16)
        for p in range(3):
            start = (2 - p) * across
            term = plain_dot(turned, shifted[start : start + positions, :])
            for q in range(3):
                piece = term[:, q * outward : (q + 1) * outward]
                if sample == 0:
                    out_ref[p, q] = piece
                else:
                    out_ref[p, q] += piece
            if sample == count - 1:
                copies.append(fetch(out_ref.at[p], out_hbm.at[p], sems.at[p]))
    wait_all(copies)


def correlate_call(place, whole, own, others, first_slice, split_left, across):
    count = len(whole)
    positions, full_lanes = whole[0].shape
    part_lanes = own.shape[1]
    inward, outward = (part_lanes, full_lanes) if split_left else (full_lanes, part_lanes)
    out = jax.ShapeDtypeStruct((3, 3, inward, outward), jnp.float32)
    scratch = (
        ((positions, part_lanes), jnp.bfloat16),
        ((positions + 2 * across, 3 * outward), jnp.bfloat16),
    )
    operands = (*whole, own, *others)
    return pl.pallas_call(
        functools.partial(
            correlate_kernel, count=count, blocks=len(others) // 2, across=across,
            first_slice=first_slice, split_left=split_left,
        ),
        out_shape=out,
        in_specs=[SMEM_SPEC] + [VMEM_SPEC] * len(operands),
        out_specs=HBM_SPEC,
        scratch_shapes=[pltpu.VMEM(out.shape, out.dtype)]
        + [pltpu.VMEM(*item) for item in scratch]
        + [pltpu.SemaphoreType.DMA((3,))],
        compiler_params=granted(operands, (out,), scratch, CORRELATE_MIB),
        name="correlate_kernel",
    )(place, *operands)


def store_lane_blocks(place_ref, source, targets):
    narrow = targets[0].shape[1]
    for index, target in enumerate(targets):
        lane = pl.multiple_of((place_ref[2] ^ (index + 1)) * narrow, 128)
        target[...] = source[:, pl.ds(lane, narrow)]


def front_kernel(place_ref, crop_ref, above_ref, below_ref, conv_hbm, down_hbm, *refs, across):
    columns_ref, pre_ref, stacked_ref, coarse_ref = refs[:4]
    slice_refs = refs[4:-5]
    near_ref, grid_ref, conv_buf, down_buf, sems = refs[-5:]
    conv_copy = fetch(conv_hbm, conv_buf, sems.at[0])
    down_copy = fetch(down_hbm, down_buf, sems.at[1])
    positions = crop_ref.shape[0]
    channels = crop_ref.shape[1]
    near_ref[0:across, :] = above_ref[...]
    near_ref[across : across + positions, :] = crop_ref[...]
    near_ref[across + positions :, :] = below_ref[...]
    wide = near_ref[...].astype(jnp.float32)
    columns_ref[:, 0:channels] = from_left(wide, across).astype(jnp.bfloat16)
    columns_ref[:, channels : 2 * channels] = near_ref[...]
    columns_ref[:, 2 * channels :] = from_right(wide, across).astype(jnp.bfloat16)
    left = jnp.concatenate(
        [columns_ref[p * across : p * across + positions, :] for p in range(3)], axis=1
    )
    conv_copy.wait()
    grid_ref[...] = plain_dot(left, conv_buf[...])
    out = grid_ref.shape[1]
    half = across // 2
    for i in range(positions // (2 * across)):
        for a in range(2):
            for b in range(2):
                lane = (2 * a + b) * out
                pre_ref[i * half : (i + 1) * half, lane : lane + out] = grid_ref[
                    pl.ds((2 * i + a) * across + b, half, stride=2), :
                ]
    pre = pre_ref[...]
    stacked = (pre * jax.nn.sigmoid(pre)).astype(jnp.bfloat16)
    stacked_ref[...] = stacked
    down_copy.wait()
    coarse_ref[...] = plain_dot(stacked, down_buf[...]).astype(jnp.bfloat16)
    store_lane_blocks(place_ref, coarse_ref, slice_refs)


def front_call(place, crop, above, below, conv_flat, down_weight, across, samples):
    positions, channels = crop.shape
    out = conv_flat.shape[1]
    low = positions // 4
    base = down_weight.shape[1]
    outs = (
        jax.ShapeDtypeStruct((positions + 2 * across, 3 * channels), jnp.bfloat16),
        jax.ShapeDtypeStruct((low, 4 * out), jnp.float32),
        jax.ShapeDtypeStruct((low, 4 * out), jnp.bfloat16),
        jax.ShapeDtypeStruct((low, base), jnp.bfloat16),
    )
    outs += (jax.ShapeDtypeStruct((low, base // samples), jnp.bfloat16),) * (samples - 1)
    scratch = (
        ((positions + 2 * across, channels), jnp.bfloat16),
        ((positions, out), jnp.float32),
        (conv_flat.shape, jnp.bfloat16),
        (down_weight.shape, jnp.bfloat16),
    )
    return pl.pallas_call(
        functools.partial(front_kernel, across=across),
        out_shape=outs,
        in_specs=[SMEM_SPEC] + [VMEM_SPEC] * 3 + [HBM_SPEC] * 2,
        out_specs=(VMEM_SPEC,) * len(outs),
        scratch_shapes=[pltpu.VMEM(*item) for item in scratch] + [pltpu.SemaphoreType.DMA((2,))],
        compiler_params=granted((crop, above, below), outs, scratch, SMALL_MIB),
        name="front_kernel",
    )(place, crop, above, below, conv_flat, down_weight)


def middle_kernel(place_ref, *refs, count, loss_scale, class_count):
    first_ref, terms = refs[0], refs[1:count]
    coarse_ref, stacked_ref, label_ref, class_turned_ref, up_hbm = refs[count : count + 5]
    bottom_ref, joined_ref, logit_grad_ref, stacked_grad_ref, bottom_grad_ref = refs[
        count + 5 : count + 10
    ]
    slice_refs = refs[count + 10 : -3]
    class_ref, up_ref, sems = refs[-3:]
    up_copy = fetch(up_hbm, up_ref, sems.at[0])
    lanes, channels = class_ref.shape
    class_ref[...] = jnp.zeros(class_ref.shape, class_ref.dtype)
    class_ref[0:class_count, :] = class_turned_ref[...]
    height, across = label_ref.shape[1:]
    half = across // 2
    label_rows = label_ref[0].astype(jnp.float32).astype(jnp.bfloat16)
    row = lax.broadcasted_iota(jnp.int32, (half, across), 0)
    pixel = lax.broadcasted_iota(jnp.int32, (half, across), 1)
    label_columns = [
        transposed_dot((pixel == 2 * row + b).astype(jnp.float32).astype(jnp.bfloat16), label_rows)
        for b in range(2)
    ]
    total = coarse_ref[...].astype(jnp.float32) + add_all(
        first_ref[...], [term[...] for term in terms]
    )
    bottom = total.astype(jnp.bfloat16)
    bottom_ref[...] = bottom
    up_copy.wait()
    joined_pre = plain_dot(bottom, up_ref[...]) + stacked_ref[...].astype(jnp.float32)
    joined_ref[...] = (joined_pre * jax.nn.sigmoid(joined_pre)).astype(jnp.bfloat16)
    slope = silu_slope(joined_pre)
    column = lax.broadcasted_iota(jnp.int32, (joined_pre.shape[0], lanes), 1)
    column_value = column.astype(jnp.float32)
    for a in range(2):
        for b in range(2):
            block = 2 * a + b
            span = slice(block * channels, (block + 1) * channels)
            label = jnp.concatenate(
                [label_columns[b][:, 2 * i + a : 2 * i + a + 1] for i in range(height // 2)],
                axis=0,
            )
            logits = transposed_dot(joined_ref[:, span], class_ref[...])
            powers = jnp.where(column < class_count, jnp.exp(logits), 0.0)
            probability = powers / jnp.sum(powers, axis=-1, keepdims=True)
            onehot = (column_value == label).astype(jnp.float32)
            logit_grad = ((probability - onehot) * loss_scale).astype(jnp.bfloat16)
            logit_grad_ref[:, block * lanes : (block + 1) * lanes] = logit_grad
            joined_grad = plain_dot(logit_grad, class_ref[...])
            stacked_grad_ref[:, span] = (joined_grad * slope[:, span]).astype(jnp.bfloat16)
    bottom_grad_ref[...] = transposed_dot(stacked_grad_ref[...], up_ref[...]).astype(jnp.bfloat16)
    store_lane_blocks(place_ref, bottom_grad_ref, slice_refs)


def middle_call(
    place, first, terms, coarse, stacked, labels, class_turned, up_weight, loss_scale, class_lanes,
    samples,
):
    rows, base = coarse.shape
    wide = stacked.shape[1]
    channels = class_turned.shape[1]
    shapes = (base, wide, wide // channels * class_lanes, wide, base)
    shapes += (base // samples,) * (samples - 1)
    outs = tuple(jax.ShapeDtypeStruct((rows, lanes), jnp.bfloat16) for lanes in shapes)
    operands = (first, *terms, coarse, stacked, labels, class_turned)
    scratch = (((class_lanes, channels), jnp.bfloat16), (up_weight.shape, jnp.bfloat16))
    return pl.pallas_call(
        functools.partial(
            middle_kernel, count=1 + len(terms), loss_scale=loss_scale,
            class_count=class_turned.shape[0],
        ),
        out_shape=outs,
        in_specs=[SMEM_SPEC] + [VMEM_SPEC] * len(operands) + [HBM_SPEC],
        out_specs=(VMEM_SPEC,) * len(outs),
        scratch_shapes=[pltpu.VMEM(*item) for item in scratch] + [pltpu.SemaphoreType.DMA((1,))],
        compiler_params=granted(operands, outs, scratch, SMALL_MIB),
        name="middle_kernel",
    )(place, *operands, up_weight)


def sum_kernel(place_ref, *refs, count, slices):
    first_ref, terms = refs[0], refs[1:count]
    slice_refs = refs[count : count + slices]
    own_ref = refs[count + slices]
    send_refs = refs[count + slices + 1 : -2]
    stack_ref, total_ref = refs[-2:]
    total_ref[...] = add_all(first_ref[...], [term[...] for term in terms]).astype(jnp.bfloat16)
    narrow = own_ref.shape[1]
    own_ref[...] = total_ref[:, pl.ds(pl.multiple_of(place_ref[2] * narrow, 128), narrow)]
    store_lane_blocks(place_ref, total_ref, send_refs)
    for index, source in enumerate(slice_refs):
        rows = source.shape[0]
        stack_ref[index * rows : (index + 1) * rows, :] = source[...]


def sum_call(place, first, terms, slices, samples):
    rows, lanes = first.shape
    block = jax.ShapeDtypeStruct((rows, lanes // samples), jnp.bfloat16)
    stack = jax.ShapeDtypeStruct((len(slices) * slices[0].shape[0], slices[0].shape[1]), jnp.bfloat16)
    outs = (block,) * samples + (stack,)
    operands = (first, *terms, *slices)
    scratch = ((first.shape, jnp.bfloat16),)
    return pl.pallas_call(
        functools.partial(sum_kernel, count=1 + len(terms), slices=len(slices)),
        out_shape=outs,
        in_specs=[SMEM_SPEC] + [VMEM_SPEC] * len(operands),
        out_specs=(VMEM_SPEC,) * len(outs),
        scratch_shapes=[pltpu.VMEM(*item) for item in scratch],
        compiler_params=granted(operands, outs, scratch, SMALL_MIB),
        name="sum_kernel",
    )(place, *operands)


def turned_dot(left, right):
    return lax.dot_general(
        left, right, (((0,), (0,)), ((), ())), preferred_element_type=jnp.float32
    )


def pack_kernel(place_ref, *refs, count, blocks, rows, across):
    first_ref, terms = refs[0], refs[1:count]
    (
        bottom_grad_ref, stacked_ref, stacked_grad_ref, pre_ref, bottom_ref,
        columns_ref, joined_ref, logit_grad_ref, down_hbm,
    ) = refs[count : count + 9]
    targets = refs[count + 9 : -4]
    pack_ref, grid_ref, down_ref, sems = refs[-4:]
    down_copy = fetch(down_hbm, down_ref, sems.at[0])
    lanes = pack_ref.shape[1]
    total = bottom_grad_ref[...].astype(jnp.float32) + add_all(
        first_ref[...], [term[...] for term in terms]
    )
    coarse_grad = total.astype(jnp.bfloat16)
    down_copy.wait()
    hidden_sum = transposed_dot(coarse_grad, down_ref[...]) + stacked_grad_ref[...].astype(
        jnp.float32
    )
    hidden_grad = (hidden_sum * silu_slope(pre_ref[...])).astype(jnp.bfloat16).astype(jnp.float32)
    positions, channels = grid_ref.shape
    half = across // 2
    for i in range(positions // (2 * across)):
        for a in range(2):
            for b in range(2):
                lane = (2 * a + b) * channels
                grid_ref[pl.ds((2 * i + a) * across + b, half, stride=2), :] = hidden_grad[
                    i * half : (i + 1) * half, lane : lane + channels
                ]
    grid = grid_ref[...].astype(jnp.bfloat16)

    def store(value, base):
        rounded = value.astype(jnp.bfloat16)
        times = lanes // value.shape[1]
        part = value.shape[0] // times
        for index in range(times):
            pack_ref[base : base + part, index * value.shape[1] : (index + 1) * value.shape[1]] = (
                rounded[index * part : (index + 1) * part, :]
            )
        return base + part

    base = store(turned_dot(stacked_ref[...], coarse_grad), 0)
    base = store(turned_dot(bottom_ref[...], stacked_grad_ref[...]), base)
    conv_grad = jnp.concatenate(
        [
            turned_dot(columns_ref[p * across : p * across + positions, :], grid)
            for p in range(3)
        ],
        axis=0,
    )
    base = store(conv_grad, base)
    class_grad = None
    class_lanes = logit_grad_ref.shape[1] // (joined_ref.shape[1] // channels)
    for block in range(joined_ref.shape[1] // channels):
        term = turned_dot(
            logit_grad_ref[:, block * class_lanes : (block + 1) * class_lanes],
            joined_ref[:, block * channels : (block + 1) * channels],
        )
        class_grad = term if class_grad is None else class_grad + term
    base = store(class_grad, base)
    if base < pack_ref.shape[0]:
        pack_ref[base:, :] = jnp.zeros((pack_ref.shape[0] - base, lanes), pack_ref.dtype)
    for index, target in enumerate(targets):
        start = block_start(place_ref, index % blocks, index // blocks, rows)
        target[...] = pack_ref[pl.ds(start, rows), :]


def pack_call(place, first, terms, operands, filled, blocks, across):
    lanes = first.shape[1]
    channels = operands[5].shape[1] // 3
    positions = 4 * first.shape[0]
    unit = 32 * blocks
    padded = -(-filled // unit) * unit
    block = jax.ShapeDtypeStruct((padded // (2 * blocks), lanes), jnp.bfloat16)
    return pl.pallas_call(
        functools.partial(
            pack_kernel, count=1 + len(terms), blocks=blocks, rows=padded // (2 * blocks),
            across=across,
        ),
        out_shape=(block,) * (2 * blocks),
        in_specs=[SMEM_SPEC] + [VMEM_SPEC] * (len(terms) + len(operands)) + [HBM_SPEC],
        out_specs=(VMEM_SPEC,) * (2 * blocks),
        scratch_shapes=[
            pltpu.VMEM((padded, lanes), jnp.bfloat16),
            pltpu.VMEM((positions, channels), jnp.float32),
            pltpu.VMEM(operands[-1].shape, jnp.bfloat16),
            pltpu.SemaphoreType.DMA((1,)),
        ],
        compiler_params=granted(
            (first, *terms, *operands), (block,) * (2 * blocks),
            (((padded, lanes), jnp.bfloat16), ((positions, channels), jnp.float32)),
            CORRELATE_MIB,
        ),
        name="pack_kernel",
    )(place, first, *terms, *operands)


def unpack_kernel(place_ref, *refs, blocks, count, shapes):
    pieces = refs[: 2 * blocks]
    outs = len(shapes)
    out_hbms = refs[2 * blocks : 2 * blocks + outs]
    out_refs = refs[2 * blocks + outs : 2 * blocks + 2 * outs]
    pack_ref, sems = refs[2 * blocks + 2 * outs :]
    lanes = pack_ref.shape[1]
    rows = pieces[0].shape[0]
    narrow = lanes // count
    for index, piece in enumerate(pieces):
        start = block_start(place_ref, index % blocks, index // blocks, rows)
        for mask in range(count):
            lane = pl.multiple_of((place_ref[2] ^ mask) * narrow, 128)
            pack_ref[pl.ds(start, rows), pl.ds(lane, narrow)] = piece[
                :, mask * narrow : (mask + 1) * narrow
            ]
    base = 0
    copies = []
    for place, (height, width) in enumerate(shapes):
        out_ref = out_refs[place]
        times = lanes // width
        part = height // times
        for index in range(times):
            value = pack_ref[base : base + part, index * width : (index + 1) * width]
            kept = min(part, out_ref.shape[0] - index * part)
            if kept > 0:
                out_ref[index * part : index * part + kept, :] = value.astype(jnp.float32)[:kept, :]
        base += part
        copies.append(fetch(out_ref, out_hbms[place], sems.at[place]))
    wait_all(copies)


def unpack_call(place, pieces, count, out_shapes, shapes):
    rows, lanes = pieces[0].shape
    outs = tuple(jax.ShapeDtypeStruct(shape, jnp.float32) for shape in out_shapes)
    scratch = ((rows * len(pieces), lanes), jnp.bfloat16)
    return pl.pallas_call(
        functools.partial(
            unpack_kernel, blocks=len(pieces) // 2, count=count, shapes=shapes
        ),
        out_shape=outs,
        in_specs=[SMEM_SPEC] + [VMEM_SPEC] * len(pieces),
        out_specs=(HBM_SPEC,) * len(out_shapes),
        scratch_shapes=[pltpu.VMEM(shape, jnp.float32) for shape in out_shapes]
        + [pltpu.VMEM(*scratch), pltpu.SemaphoreType.DMA((len(out_shapes),))],
        compiler_params=granted(pieces, outs, (scratch,), SMALL_MIB),
        name="unpack_kernel",
    )(place, *pieces)


def shift_columns(grid, offset):
    across = grid.shape[-2]
    pads = [(0, 0)] * grid.ndim
    if offset > 0:
        pads[-2] = (0, offset)
        return jnp.pad(lax.slice_in_dim(grid, offset, across, axis=-2 % grid.ndim), pads)
    if offset < 0:
        pads[-2] = (-offset, 0)
        return jnp.pad(lax.slice_in_dim(grid, 0, across + offset, axis=-2 % grid.ndim), pads)
    return grid


def shift_rows(grid, offset):
    height = grid.shape[-3]
    pads = [(0, 0)] * grid.ndim
    if offset > 0:
        pads[-3] = (0, offset)
        return jnp.pad(lax.slice_in_dim(grid, offset, height, axis=-3 % grid.ndim), pads)
    if offset < 0:
        pads[-3] = (-offset, 0)
        return jnp.pad(lax.slice_in_dim(grid, 0, height + offset, axis=-3 % grid.ndim), pads)
    return grid


def taps(grid, sign):
    columns = [shift_columns(grid, sign * (q - 1)) for q in range(3)]
    return [shift_rows(columns[q], sign * (p - 1)) for p in range(3) for q in range(3)]


def conv_in(grid, weight, sign, transposed):
    height, across, channels = grid.shape
    window = jnp.concatenate(taps(grid, sign), axis=-1).reshape(height * across, 9 * channels)
    if transposed:
        flat = jnp.transpose(weight, (0, 1, 3, 2)).reshape(9 * channels, weight.shape[2])
    else:
        flat = weight.reshape(9 * channels, weight.shape[3])
    result = jnp.dot(window, flat, preferred_element_type=jnp.float32)
    return result.reshape(height, across, -1)


def correlate_samples(left, right):
    samples, height, across, inward = left.shape
    outward = right.shape[-1]
    flat = left.reshape(samples * height * across, inward)
    shifted = jnp.concatenate(taps(right, -1), axis=-1).reshape(-1, 9 * outward)
    result = lax.dot_general(
        flat, shifted, (((0,), (0,)), ((), ())), preferred_element_type=jnp.float32
    )
    return jnp.transpose(result.reshape(inward, 3, 3, outward), (1, 2, 0, 3))


def join_blocks(mine, other):
    wide = lax.axis_size("wide")
    own = lax.axis_index("wide")
    stacked = jnp.stack([mine, other], axis=1).reshape((wide,) + mine.shape[1:])
    return stacked[jnp.arange(wide) ^ own].reshape(-1, mine.shape[-1])


def part_blocks(whole):
    wide = lax.axis_size("wide")
    own = lax.axis_index("wide")
    blocks = whole.reshape(wide, -1, whole.shape[-1])[jnp.arange(wide) ^ own]
    halves = blocks.reshape(wide // 2, 2, -1, whole.shape[-1])
    return [halves[r, half] for half in range(2) for r in range(wide // 2)]


def step(
    features,
    labels,
    conv_weight,
    down_weight,
    expand_weight,
    reduce_weight,
    up_weight,
    class_weight,
):
    crop_rows = features[0]
    height, across, channels = crop_rows.shape
    wide = lax.axis_size("wide")
    samples = lax.axis_size("samp")
    chips = chip_count()
    pixel_count = wide * samples * height * across
    loss_scale = 8.0 / math.sqrt(pixel_count)
    own = lax.axis_index("wide")
    place = jnp.stack([own % 2, own // 2, lax.axis_index("samp")]).astype(jnp.int32)
    base = down_weight.shape[1]
    inner = expand_weight.shape[-1]
    narrow = base // samples
    low_rows, low_across = height // 2, across // 2
    block_rows = low_rows * low_across
    grid = (wide * low_rows, low_across)
    class_count = class_weight.shape[1]
    class_lanes = 128
    own_kernels = inner % 128 == 0 and narrow % 128 == 0

    forward = [(i, i + 1) for i in range(wide - 1)]
    backward = [(target, source) for source, target in forward]
    above = lax.ppermute(crop_rows[height - 1], "wide", forward)
    below = lax.ppermute(crop_rows[0], "wide", backward)
    columns, hidden_pre, stacked, coarse, *coarse_sends = front_call(
        place, crop_rows.reshape(height * across, channels), above, below,
        in_hbm(conv_weight.reshape(9 * channels, -1)), in_hbm(down_weight), across, samples,
    )
    stacked_mine = gather_chips(stacked)
    stacked_other = swap_cores(stacked_mine)
    if own_kernels:
        coarse_part, expand_pre, expanded, *partial = bottleneck_call(
            forward_kernel, place, stacked_mine + stacked_other, down_weight,
            in_hbm(expand_weight), in_hbm(reduce_weight), None, low_across, samples,
        )
    else:
        stacked_all = join_blocks(jnp.stack(stacked_mine), jnp.stack(stacked_other))
        coarse_all = jnp.dot(stacked_all, down_weight, preferred_element_type=jnp.float32).astype(
            jnp.bfloat16
        )
        coarse_part = lane_block(coarse_all, lax.axis_index("samp"), samples)
        expand_grid = conv_in(coarse_all.reshape(*grid, base), expand_weight, 1, False)
        expanded_grid = jax.nn.silu(expand_grid).astype(jnp.bfloat16)
        partial = conv_in(expanded_grid, reduce_weight, 1, False).astype(jnp.bfloat16)
        partial = part_blocks(partial.reshape(-1, base))
        expanded = expanded_grid.reshape(-1, inner)
    coarse_slices = send_samples(coarse_sends)
    expanded_samples = [expanded] + send_samples([expanded] * (samples - 1))
    first, *terms = scatter_chips(partial[:chips], partial[chips:])
    bottom, joined, logit_grad, stacked_grad, bottom_grad, *bottom_sends = middle_call(
        place, first, terms, coarse, stacked, labels, class_weight.T, up_weight, loss_scale,
        class_lanes, samples,
    )
    grad_mine = gather_chips(stacked_grad)
    grad_other = swap_cores(grad_mine)
    if own_kernels:
        bottom_part, expanded_grad, *back = bottleneck_call(
            backward_kernel, place, grad_mine + grad_other, up_weight, expand_weight,
            reduce_weight, expand_pre, low_across, samples,
        )
    else:
        grad_all = join_blocks(jnp.stack(grad_mine), jnp.stack(grad_other))
        bottom_all = transposed_dot(grad_all, up_weight).astype(jnp.bfloat16)
        bottom_part = lane_block(bottom_all, lax.axis_index("samp"), samples)
        expanded_back = conv_in(bottom_all.reshape(*grid, base), reduce_weight, -1, True)
        grad_grid = (expanded_back * silu_slope(expand_grid)).astype(jnp.bfloat16)
        back = conv_in(grad_grid, expand_weight, -1, True).astype(jnp.bfloat16)
        back = part_blocks(back.reshape(-1, base))
        expanded_grad = grad_grid.reshape(-1, inner)
    bottom_slices = send_samples(bottom_sends)
    grad_samples = [expanded_grad] + send_samples([expanded_grad] * (samples - 1))
    first, *terms = scatter_chips(back[:chips], back[chips:])

    conv_out = conv_weight.shape[-1]
    shapes = (
        (down_weight.shape[0], base),
        (base, up_weight.shape[1]),
        (9 * channels, conv_out),
        (class_lanes, conv_out),
    )
    filled = sum(rows * lanes for rows, lanes in shapes) // base
    packed = pack_call(
        place, first, terms,
        (
            bottom_grad, stacked, stacked_grad, hidden_pre, bottom,
            columns, joined, logit_grad, down_weight,
        ),
        filled, chips, across,
    )
    first, *terms = scatter_chips(packed[:chips], packed[chips:])
    own_part, *part_sends, slices = sum_call(
        place, first, terms, coarse_slices + bottom_slices, samples
    )
    parts = send_samples(part_sends)
    slices_mine = gather_chips(slices)
    slices_other = swap_cores(slices_mine)
    total = add_all(own_part, parts).astype(jnp.bfloat16)
    own_total = jnp.concatenate(
        [total] + send_samples([total] * (samples - 1)), axis=1
    )
    total_mine = gather_chips(own_total)
    total_other = swap_cores(total_mine)
    out_shapes = shapes[:3] + ((class_count, conv_out),)
    down_total, up_total, conv_total, class_total = unpack_call(
        place, total_mine + total_other, samples, out_shapes, shapes,
    )

    if own_kernels:
        reduce_grad = correlate_call(
            place, expanded_samples, bottom_part, slices_mine + slices_other,
            samples - 1, False, low_across,
        )
        expand_grad = correlate_call(
            place, grad_samples, coarse_part, slices_mine + slices_other,
            0, True, low_across,
        )
    else:

        def join_samples(own_part, first_slice):
            joined_ = [own_part]
            for i in range(samples - 1):
                span = slice((first_slice + i) * block_rows, (first_slice + i + 1) * block_rows)
                joined_.append(
                    join_blocks(
                        jnp.stack([item[span] for item in slices_mine]),
                        jnp.stack([item[span] for item in slices_other]),
                    )
                )
            return jnp.stack(joined_).reshape(samples, *grid, narrow)

        reduce_grad = correlate_samples(
            jnp.stack(expanded_samples).reshape(samples, *grid, inner),
            join_samples(bottom_part, samples - 1),
        )
        expand_grad = correlate_samples(
            join_samples(coarse_part, 0),
            jnp.stack(grad_samples).reshape(samples, *grid, inner),
        )
    return (
        conv_total.reshape(conv_weight.shape),
        down_total,
        expand_grad,
        reduce_grad,
        up_total,
        class_total.T,
    )


def solution(mesh):
    return jax.shard_map(
        step,
        mesh=mesh,
        in_specs=(
            P("samp", "wide", None, None),
            P("samp", "wide", None),
            P(),
            P(),
            P(None, None, None, "wide"),
            P(None, None, "wide", None),
            P(),
            P(),
        ),
        out_specs=(
            P(),
            P(),
            P(None, None, "samp", "wide"),
            P(None, None, "wide", "samp"),
            P(),
            P(),
        ),
        check_vma=False,
    )
```

```python
import functools
import math

import jax
import jax.numpy as jnp
from jax import lax
from jax.experimental import pallas as pl
from jax.experimental.pallas import tpu as pltpu
from jax.sharding import PartitionSpec as P


def swap(values, axis, mask):
    count = lax.axis_size(axis)
    return lax.ppermute(values, axis, [(i, i ^ mask) for i in range(count)])


def chip_count():
    return lax.axis_size("wide") // 2


def gather_chips(piece):
    return [piece] + [swap(piece, "wide", 2 * r) for r in range(1, chip_count())]


def swap_cores(pieces):
    return [swap(piece, "wide", 1) for piece in pieces]


def scatter_chips(own, sent):
    chips = len(own)
    order = list(range(1, chips)) + [0]
    partner = {r: swap(sent[r], "wide", 1) for r in order}
    sends = [add_all(own[r], [partner[r]]).astype(jnp.bfloat16) for r in range(1, chips)]
    return [own[0], partner[0]] + send_chips(sends)


def send_chips(sends):
    return [swap(piece, "wide", 2 * (r + 1)) for r, piece in enumerate(sends)]


def send_samples(sends):
    return [swap(piece, "samp", mask + 1) for mask, piece in enumerate(sends)]


def lane_block(values, target, count):
    narrow = values.shape[-1] // count
    return lax.dynamic_slice_in_dim(values, target * narrow, narrow, axis=values.ndim - 1)


def in_hbm(values):
    return pltpu.with_memory_space_constraint(values, pltpu.HBM)


def add_all(first, rest):
    total = first.astype(jnp.float32)
    for item in rest:
        total = total + item.astype(jnp.float32)
    return total


def silu_slope(value):
    logistic = jax.nn.sigmoid(value)
    return logistic * (1.0 + value * (1.0 - logistic))


def column_mask(shape, column):
    return lax.broadcasted_iota(jnp.int32, shape, 1) == column


def from_left(values, across):
    view = values.reshape(-1, across, values.shape[-1])
    moved = pltpu.roll(view, 1, 1)
    return jnp.where(column_mask(view.shape, 0), 0.0, moved).reshape(values.shape)


def from_right(values, across):
    view = values.reshape(-1, across, values.shape[-1])
    moved = pltpu.roll(view, across - 1, 1)
    return jnp.where(column_mask(view.shape, across - 1), 0.0, moved).reshape(values.shape)


def block_start(place_ref, relative, half, rows, offset=0):
    chip = place_ref[1] ^ relative
    core = place_ref[0] ^ half
    return pl.multiple_of(offset + (2 * chip + core) * rows, 16)


def clear_edges(padded, across):
    total = padded.shape[0]
    blank = jnp.zeros((across, padded.shape[1]), padded.dtype)
    padded[0:across, :] = blank
    padded[total - across : total, :] = blank


def expand_copies_of(expand_hbm, expand_buf, sems):
    inner = expand_hbm.shape[-1]
    base = expand_hbm.shape[-2]
    return [
        pltpu.make_async_copy(
            expand_hbm.at[p, q],
            expand_buf.at[pl.ds(p * base, base), pl.ds(q * inner, inner)],
            sems.at[3 * p + q],
        )
        for p in range(3)
        for q in range(3)
    ]


def reduce_copies_of(reduce_hbm, reduce_buf, sems):
    inner = reduce_hbm.shape[-2]
    return [
        pltpu.make_async_copy(
            reduce_hbm.at[p, q],
            reduce_buf.at[pl.ds((3 * p + q) * inner, inner), :],
            sems.at[3 * p + q],
        )
        for p in range(3)
        for q in range(3)
    ]


def wait_all(copies):
    for copy in copies:
        copy.wait()


def plain_dot(left, right):
    return jnp.dot(left, right, preferred_element_type=jnp.float32)


def transposed_dot(left, right):
    return lax.dot_general(
        left, right, (((1,), (1,)), ((), ())), preferred_element_type=jnp.float32
    )


def gather_blocks(shifted, place_ref, half, offset, rows, blocks):
    return jnp.concatenate(
        [
            shifted[pl.ds(block_start(place_ref, block, half, rows, offset), rows), :]
            for block in range(blocks)
        ],
        axis=0,
    )


def fetch(source, target, sem):
    copy = pltpu.make_async_copy(source, target, sem)
    copy.start()
    return copy


def place_pieces(place_ref, pieces, target, blocks):
    rows = pieces[0].shape[0]
    for index, piece in enumerate(pieces):
        start = block_start(place_ref, index % blocks, index // blocks, rows)
        target[pl.ds(start, rows), :] = piece[...]


def store_own_lanes(place_ref, source, rows, target):
    narrow = target.shape[1]
    target[...] = source[rows, pl.ds(pl.multiple_of(place_ref[2] * narrow, 128), narrow)]


def store_rows(value, targets):
    rows = targets[0].shape[0]
    for index, target in enumerate(targets):
        target[...] = value[index * rows : (index + 1) * rows, :]


def forward_kernel(place_ref, *refs, blocks, rows, across):
    pieces = refs[: 2 * blocks]
    outer_ref, expand_buf, reduce_hbm, slice_ref, pre_ref, exp_ref, reduce_buf = refs[
        2 * blocks : 2 * blocks + 7
    ]
    own_refs = refs[2 * blocks + 7 : 3 * blocks + 7]
    sent_refs = refs[3 * blocks + 7 : 4 * blocks + 7]
    gathered, padded, shifted, sems = refs[4 * blocks + 7 :]
    reduce_copies = reduce_copies_of(reduce_hbm, reduce_buf, sems)
    for copy in reduce_copies:
        copy.start()
    clear_edges(padded, across)
    clear_edges(shifted, across)
    inner = pre_ref.shape[1]
    base = padded.shape[1]
    positions = pre_ref.shape[0]
    inside = pl.ds(across, positions)
    place_pieces(place_ref, pieces, gathered, blocks)
    padded[inside, :] = plain_dot(gathered[...], outer_ref[...]).astype(jnp.bfloat16)
    store_own_lanes(place_ref, padded, inside, slice_ref)
    total = None
    for p in range(3):
        term = plain_dot(
            padded[p * across : p * across + positions, :],
            expand_buf[p * base : (p + 1) * base, :],
        )
        total = term if total is None else total + term
    pre = (
        total[:, inner : 2 * inner]
        + from_left(total[:, 0:inner], across)
        + from_right(total[:, 2 * inner : 3 * inner], across)
    )
    pre_ref[...] = pre
    expanded = (pre * jax.nn.sigmoid(pre)).astype(jnp.bfloat16)
    exp_ref[...] = expanded
    wide = expanded.astype(jnp.float32)
    shifted[inside, 0:inner] = from_left(wide, across).astype(jnp.bfloat16)
    shifted[inside, inner : 2 * inner] = expanded
    shifted[inside, 2 * inner : 3 * inner] = from_right(wide, across).astype(jnp.bfloat16)
    wait_all(reduce_copies)
    for half, targets in ((1, sent_refs), (0, own_refs)):
        out = None
        for p in range(3):
            left = gather_blocks(shifted, place_ref, half, p * across, rows, blocks)
            term = plain_dot(left, reduce_buf[3 * p * inner : 3 * (p + 1) * inner, :])
            out = term if out is None else out + term
        store_rows(out.astype(jnp.bfloat16), targets)


def backward_kernel(place_ref, *refs, blocks, rows, across):
    pieces = refs[: 2 * blocks]
    outer_ref, expand_buf, reduce_buf, pre_ref, slice_ref, grad_ref = refs[
        2 * blocks : 2 * blocks + 6
    ]
    own_refs = refs[2 * blocks + 6 : 3 * blocks + 6]
    sent_refs = refs[3 * blocks + 6 : 4 * blocks + 6]
    gathered, padded, shifted = refs[4 * blocks + 6 :]
    clear_edges(padded, across)
    clear_edges(shifted, across)
    inner = pre_ref.shape[1]
    base = padded.shape[1]
    positions = pre_ref.shape[0]
    inside = pl.ds(across, positions)
    place_pieces(place_ref, pieces, gathered, blocks)
    padded[inside, :] = transposed_dot(gathered[...], outer_ref[...]).astype(jnp.bfloat16)
    store_own_lanes(place_ref, padded, inside, slice_ref)
    total = None
    for p in range(3):
        start = (2 - p) * across
        term = transposed_dot(
            padded[start : start + positions, :],
            reduce_buf[3 * p * inner : 3 * (p + 1) * inner, :],
        )
        total = term if total is None else total + term
    back = (
        total[:, inner : 2 * inner]
        + from_right(total[:, 0:inner], across)
        + from_left(total[:, 2 * inner : 3 * inner], across)
    )
    pre = pre_ref[...]
    grad = (back * silu_slope(pre)).astype(jnp.bfloat16)
    grad_ref[...] = grad
    wide = grad.astype(jnp.float32)
    shifted[inside, 0:inner] = from_right(wide, across).astype(jnp.bfloat16)
    shifted[inside, inner : 2 * inner] = grad
    shifted[inside, 2 * inner : 3 * inner] = from_left(wide, across).astype(jnp.bfloat16)
    for half, targets in ((1, sent_refs), (0, own_refs)):
        out = None
        for p in range(3):
            left = gather_blocks(shifted, place_ref, half, (2 - p) * across, rows, blocks)
            term = transposed_dot(left, expand_buf[p * base : (p + 1) * base, :])
            out = term if out is None else out + term
        store_rows(out.astype(jnp.bfloat16), targets)


BOTTLENECK_MIB = 12
CORRELATE_MIB = 8
SMALL_MIB = 6

VMEM_SPEC = pl.BlockSpec(memory_space=pltpu.VMEM)
SMEM_SPEC = pl.BlockSpec(memory_space=pltpu.SMEM)
HBM_SPEC = pl.BlockSpec(memory_space=pltpu.HBM)


def granted(operands, outs, scratch, temporaries):
    total = sum(math.prod(item.shape) * item.dtype.itemsize for item in (*operands, *outs))
    total += sum(math.prod(shape) * jnp.dtype(dtype).itemsize for shape, dtype in scratch)
    limit = min(int(total * 1.1) + (temporaries << 20), 60 << 20)
    return pltpu.CompilerParams(vmem_limit_bytes=limit)


def bottleneck_call(
    kernel, place, pieces, outer_weight, expand_held, reduce_held, pre, across, samples
):
    rows, outer = pieces[0].shape
    base = expand_held.shape[0] // 3
    inner = expand_held.shape[1] // 3
    positions = len(pieces) * rows
    inner_bf16 = jax.ShapeDtypeStruct((positions, inner), jnp.bfloat16)
    inner_f32 = jax.ShapeDtypeStruct((positions, inner), jnp.float32)
    held = jax.ShapeDtypeStruct((9 * inner, base), jnp.bfloat16)
    parts = (jax.ShapeDtypeStruct((rows, base), jnp.bfloat16),) * len(pieces)
    part = jax.ShapeDtypeStruct((positions, base // samples), jnp.bfloat16)
    operands = [*pieces, outer_weight, expand_held, reduce_held]
    specs = [SMEM_SPEC] + [VMEM_SPEC] * (len(pieces) + 2)
    scratch = (
        ((positions, outer), jnp.bfloat16),
        ((positions + 2 * across, base), jnp.bfloat16),
        ((positions + 2 * across, 3 * inner), jnp.bfloat16),
    )
    if pre is None:
        outs = (part, inner_f32, inner_bf16, held) + parts
        specs += [HBM_SPEC]
        sems = [pltpu.SemaphoreType.DMA((9,))]
    else:
        outs = (part, inner_bf16) + parts
        operands.append(pre)
        specs += [VMEM_SPEC] * 2
        sems = []
    return pl.pallas_call(
        functools.partial(kernel, blocks=len(pieces) // 2, rows=rows, across=across),
        out_shape=outs,
        in_specs=specs,
        out_specs=tuple(VMEM_SPEC for _ in outs),
        scratch_shapes=[pltpu.VMEM(*item) for item in scratch] + sems,
        compiler_params=granted(operands, outs, scratch, BOTTLENECK_MIB),
    )(place, *operands)


def correlate_kernel(place_ref, *refs, count, blocks, across, first_slice, split_left):
    whole = refs[:count]
    own = refs[count]
    others = refs[count + 1 : count + 1 + 2 * blocks]
    out_hbm, out_ref, joined, shifted, sems = refs[count + 1 + 2 * blocks :]
    copies = []
    rows = joined.shape[0] // (2 * blocks)
    outward = shifted.shape[-1] // 3
    positions = joined.shape[0]
    clear_edges(shifted, across)
    inside = pl.ds(across, positions)
    for sample in range(count):
        if sample == 0:
            part = own[...]
        else:
            first = (first_slice + sample - 1) * rows
            for index in range(2 * blocks):
                start = block_start(place_ref, index % blocks, index // blocks, rows)
                joined[pl.ds(start, rows), :] = others[index][first : first + rows, :]
            part = joined[...]
        if split_left:
            left, right = part, whole[sample][...]
        else:
            left, right = whole[sample][...], part
        turned = jnp.transpose(left, (1, 0))
        wide = right.astype(jnp.float32)
        shifted[inside, 0:outward] = from_right(wide, across).astype(jnp.bfloat16)
        shifted[inside, outward : 2 * outward] = right
        shifted[inside, 2 * outward : 3 * outward] = from_left(wide, across).astype(jnp.bfloat16)
        for p in range(3):
            start = (2 - p) * across
            term = plain_dot(turned, shifted[start : start + positions, :])
            for q in range(3):
                piece = term[:, q * outward : (q + 1) * outward]
                if sample == 0:
                    out_ref[p, q] = piece
                else:
                    out_ref[p, q] += piece
            if sample == count - 1:
                copies.append(fetch(out_ref.at[p], out_hbm.at[p], sems.at[p]))
    wait_all(copies)


def correlate_call(place, whole, own, others, first_slice, split_left, across):
    count = len(whole)
    positions, full_lanes = whole[0].shape
    part_lanes = own.shape[1]
    inward, outward = (part_lanes, full_lanes) if split_left else (full_lanes, part_lanes)
    out = jax.ShapeDtypeStruct((3, 3, inward, outward), jnp.float32)
    scratch = (
        ((positions, part_lanes), jnp.bfloat16),
        ((positions + 2 * across, 3 * outward), jnp.bfloat16),
    )
    operands = (*whole, own, *others)
    return pl.pallas_call(
        functools.partial(
            correlate_kernel, count=count, blocks=len(others) // 2, across=across,
            first_slice=first_slice, split_left=split_left,
        ),
        out_shape=out,
        in_specs=[SMEM_SPEC] + [VMEM_SPEC] * len(operands),
        out_specs=HBM_SPEC,
        scratch_shapes=[pltpu.VMEM(out.shape, out.dtype)]
        + [pltpu.VMEM(*item) for item in scratch]
        + [pltpu.SemaphoreType.DMA((3,))],
        compiler_params=granted(operands, (out,), scratch, CORRELATE_MIB),
        name="correlate_kernel",
    )(place, *operands)


def store_lane_blocks(place_ref, source, targets):
    narrow = targets[0].shape[1]
    for index, target in enumerate(targets):
        lane = pl.multiple_of((place_ref[2] ^ (index + 1)) * narrow, 128)
        target[...] = source[:, pl.ds(lane, narrow)]


def front_kernel(
    place_ref, cross_ref, core_row_ref, crop_hbm, conv_hbm, down_hbm, *refs, across, hold
):
    held, refs = (refs[:1], refs[1:]) if hold else ((), refs)
    columns_ref, pre_ref, stacked_ref, coarse_ref, down_buf = refs[:5]
    slice_refs = refs[5 + hold : -4]
    near_ref, grid_ref, conv_buf, sems = refs[-4:]
    positions, channels = crop_hbm.shape
    crop_copy = fetch(crop_hbm, near_ref.at[pl.ds(across, positions), :], sems.at[11])
    conv_copy = fetch(conv_hbm, conv_buf, sems.at[9])
    down_copy = fetch(down_hbm, down_buf, sems.at[10])
    expand_copies = expand_copies_of(held[0], refs[5], sems) if hold else []
    for copy in expand_copies:
        copy.start()
    core = place_ref[0]
    far = across + positions
    near_ref[pl.ds(pl.multiple_of(core * far, 16), across), :] = cross_ref[...]
    near_ref[pl.ds(pl.multiple_of((1 - core) * far, 16), across), :] = core_row_ref[...]
    crop_copy.wait()
    wide = near_ref[...].astype(jnp.float32)
    columns_ref[:, 0:channels] = from_left(wide, across).astype(jnp.bfloat16)
    columns_ref[:, channels : 2 * channels] = near_ref[...]
    columns_ref[:, 2 * channels :] = from_right(wide, across).astype(jnp.bfloat16)
    left = jnp.concatenate(
        [columns_ref[p * across : p * across + positions, :] for p in range(3)], axis=1
    )
    conv_copy.wait()
    grid_ref[...] = plain_dot(left, conv_buf[...])
    out = grid_ref.shape[1]
    half = across // 2
    for i in range(positions // (2 * across)):
        for a in range(2):
            for b in range(2):
                lane = (2 * a + b) * out
                pre_ref[i * half : (i + 1) * half, lane : lane + out] = grid_ref[
                    pl.ds((2 * i + a) * across + b, half, stride=2), :
                ]
    pre = pre_ref[...]
    stacked = (pre * jax.nn.sigmoid(pre)).astype(jnp.bfloat16)
    stacked_ref[...] = stacked
    down_copy.wait()
    coarse_ref[...] = plain_dot(stacked, down_buf[...]).astype(jnp.bfloat16)
    store_lane_blocks(place_ref, coarse_ref, slice_refs)
    wait_all(expand_copies)


def front_call(
    place, crop, cross, core_row, conv_flat, down_weight, expand_weight, across, samples
):
    hold = expand_weight is not None
    positions, channels = crop.shape
    out = conv_flat.shape[1]
    low = positions // 4
    base = down_weight.shape[1]
    outs = (
        jax.ShapeDtypeStruct((positions + 2 * across, 3 * channels), jnp.bfloat16),
        jax.ShapeDtypeStruct((low, 4 * out), jnp.float32),
        jax.ShapeDtypeStruct((low, 4 * out), jnp.bfloat16),
        jax.ShapeDtypeStruct((low, base), jnp.bfloat16),
        jax.ShapeDtypeStruct(down_weight.shape, jnp.bfloat16),
    )
    weights = (conv_flat, down_weight)
    if hold:
        weights += (expand_weight,)
        outs += (jax.ShapeDtypeStruct((3 * base, 3 * expand_weight.shape[-1]), jnp.bfloat16),)
    outs += (jax.ShapeDtypeStruct((low, base // samples), jnp.bfloat16),) * (samples - 1)
    scratch = (
        ((positions + 2 * across, channels), jnp.bfloat16),
        ((positions, out), jnp.float32),
        (conv_flat.shape, jnp.bfloat16),
    )
    return pl.pallas_call(
        functools.partial(front_kernel, across=across, hold=int(hold)),
        out_shape=outs,
        in_specs=[SMEM_SPEC] + [VMEM_SPEC] * 2 + [HBM_SPEC] * (1 + len(weights)),
        out_specs=(VMEM_SPEC,) * len(outs),
        scratch_shapes=[pltpu.VMEM(*item) for item in scratch] + [pltpu.SemaphoreType.DMA((12,))],
        compiler_params=granted((crop, cross, core_row), outs, scratch, SMALL_MIB),
        name="front_kernel",
    )(place, cross, core_row, crop, *weights)


def middle_kernel(place_ref, *refs, count, loss_scale, class_count):
    first_ref, terms = refs[0], refs[1:count]
    coarse_ref, stacked_ref, label_ref, class_turned_ref, up_hbm = refs[count : count + 5]
    bottom_ref, joined_ref, logit_grad_ref, stacked_grad_ref, bottom_grad_ref = refs[
        count + 5 : count + 10
    ]
    slice_refs = refs[count + 10 : -3]
    class_ref, up_ref, sems = refs[-3:]
    up_copy = fetch(up_hbm, up_ref, sems.at[0])
    lanes, channels = class_ref.shape
    class_ref[...] = jnp.zeros(class_ref.shape, class_ref.dtype)
    class_ref[0:class_count, :] = class_turned_ref[...]
    height, across = label_ref.shape[1:]
    half = across // 2
    label_rows = label_ref[0].astype(jnp.float32).astype(jnp.bfloat16)
    row = lax.broadcasted_iota(jnp.int32, (half, across), 0)
    pixel = lax.broadcasted_iota(jnp.int32, (half, across), 1)
    label_columns = [
        transposed_dot((pixel == 2 * row + b).astype(jnp.float32).astype(jnp.bfloat16), label_rows)
        for b in range(2)
    ]
    total = coarse_ref[...].astype(jnp.float32) + add_all(
        first_ref[...], [term[...] for term in terms]
    )
    bottom = total.astype(jnp.bfloat16)
    bottom_ref[...] = bottom
    up_copy.wait()
    joined_pre = plain_dot(bottom, up_ref[...]) + stacked_ref[...].astype(jnp.float32)
    joined_ref[...] = (joined_pre * jax.nn.sigmoid(joined_pre)).astype(jnp.bfloat16)
    slope = silu_slope(joined_pre)
    column = lax.broadcasted_iota(jnp.int32, (joined_pre.shape[0], lanes), 1)
    column_value = column.astype(jnp.float32)
    for a in range(2):
        for b in range(2):
            block = 2 * a + b
            span = slice(block * channels, (block + 1) * channels)
            label = jnp.concatenate(
                [label_columns[b][:, 2 * i + a : 2 * i + a + 1] for i in range(height // 2)],
                axis=0,
            )
            logits = transposed_dot(joined_ref[:, span], class_ref[...])
            powers = jnp.where(column < class_count, jnp.exp(logits), 0.0)
            probability = powers / jnp.sum(powers, axis=-1, keepdims=True)
            onehot = (column_value == label).astype(jnp.float32)
            logit_grad = ((probability - onehot) * loss_scale).astype(jnp.bfloat16)
            logit_grad_ref[:, block * lanes : (block + 1) * lanes] = logit_grad
            joined_grad = plain_dot(logit_grad, class_ref[...])
            stacked_grad_ref[:, span] = (joined_grad * slope[:, span]).astype(jnp.bfloat16)
    bottom_grad_ref[...] = transposed_dot(stacked_grad_ref[...], up_ref[...]).astype(jnp.bfloat16)
    store_lane_blocks(place_ref, bottom_grad_ref, slice_refs)


def middle_call(
    place, first, terms, coarse, stacked, labels, class_turned, up_weight, loss_scale, class_lanes,
    samples,
):
    rows, base = coarse.shape
    wide = stacked.shape[1]
    channels = class_turned.shape[1]
    shapes = (base, wide, wide // channels * class_lanes, wide, base)
    shapes += (base // samples,) * (samples - 1)
    outs = tuple(jax.ShapeDtypeStruct((rows, lanes), jnp.bfloat16) for lanes in shapes)
    operands = (first, *terms, coarse, stacked, labels, class_turned)
    scratch = (((class_lanes, channels), jnp.bfloat16), (up_weight.shape, jnp.bfloat16))
    return pl.pallas_call(
        functools.partial(
            middle_kernel, count=1 + len(terms), loss_scale=loss_scale,
            class_count=class_turned.shape[0],
        ),
        out_shape=outs,
        in_specs=[SMEM_SPEC] + [VMEM_SPEC] * len(operands) + [HBM_SPEC],
        out_specs=(VMEM_SPEC,) * len(outs),
        scratch_shapes=[pltpu.VMEM(*item) for item in scratch] + [pltpu.SemaphoreType.DMA((1,))],
        compiler_params=granted(operands, outs, scratch, SMALL_MIB),
        name="middle_kernel",
    )(place, *operands, up_weight)


def sum_kernel(place_ref, *refs, count, slices):
    first_ref, terms = refs[0], refs[1:count]
    slice_refs = refs[count : count + slices]
    own_ref = refs[count + slices]
    send_refs = refs[count + slices + 1 : -2]
    stack_ref, total_ref = refs[-2:]
    total_ref[...] = add_all(first_ref[...], [term[...] for term in terms]).astype(jnp.bfloat16)
    narrow = own_ref.shape[1]
    own_ref[...] = total_ref[:, pl.ds(pl.multiple_of(place_ref[2] * narrow, 128), narrow)]
    store_lane_blocks(place_ref, total_ref, send_refs)
    for index, source in enumerate(slice_refs):
        rows = source.shape[0]
        stack_ref[index * rows : (index + 1) * rows, :] = source[...]


def sum_call(place, first, terms, slices, samples):
    rows, lanes = first.shape
    block = jax.ShapeDtypeStruct((rows, lanes // samples), jnp.bfloat16)
    stack = jax.ShapeDtypeStruct((len(slices) * slices[0].shape[0], slices[0].shape[1]), jnp.bfloat16)
    outs = (block,) * samples + (stack,)
    operands = (first, *terms, *slices)
    scratch = ((first.shape, jnp.bfloat16),)
    return pl.pallas_call(
        functools.partial(sum_kernel, count=1 + len(terms), slices=len(slices)),
        out_shape=outs,
        in_specs=[SMEM_SPEC] + [VMEM_SPEC] * len(operands),
        out_specs=(VMEM_SPEC,) * len(outs),
        scratch_shapes=[pltpu.VMEM(*item) for item in scratch],
        compiler_params=granted(operands, outs, scratch, SMALL_MIB),
        name="sum_kernel",
    )(place, *operands)


def turned_dot(left, right):
    return lax.dot_general(
        left, right, (((0,), (0,)), ((), ())), preferred_element_type=jnp.float32
    )


def pack_kernel(place_ref, *refs, count, blocks, rows, across):
    first_ref, terms = refs[0], refs[1:count]
    (
        bottom_grad_ref, stacked_ref, stacked_grad_ref, pre_ref, bottom_ref,
        columns_ref, joined_ref, logit_grad_ref, down_hbm,
    ) = refs[count : count + 9]
    targets = refs[count + 9 : -4]
    pack_ref, grid_ref, down_ref, sems = refs[-4:]
    down_copy = fetch(down_hbm, down_ref, sems.at[0])
    lanes = pack_ref.shape[1]
    total = bottom_grad_ref[...].astype(jnp.float32) + add_all(
        first_ref[...], [term[...] for term in terms]
    )
    coarse_grad = total.astype(jnp.bfloat16)
    down_copy.wait()
    hidden_sum = transposed_dot(coarse_grad, down_ref[...]) + stacked_grad_ref[...].astype(
        jnp.float32
    )
    hidden_grad = (hidden_sum * silu_slope(pre_ref[...])).astype(jnp.bfloat16).astype(jnp.float32)
    positions, channels = grid_ref.shape
    half = across // 2
    for i in range(positions // (2 * across)):
        for a in range(2):
            for b in range(2):
                lane = (2 * a + b) * channels
                grid_ref[pl.ds((2 * i + a) * across + b, half, stride=2), :] = hidden_grad[
                    i * half : (i + 1) * half, lane : lane + channels
                ]
    grid = grid_ref[...].astype(jnp.bfloat16)

    def store(value, base):
        rounded = value.astype(jnp.bfloat16)
        times = lanes // value.shape[1]
        part = value.shape[0] // times
        for index in range(times):
            pack_ref[base : base + part, index * value.shape[1] : (index + 1) * value.shape[1]] = (
                rounded[index * part : (index + 1) * part, :]
            )
        return base + part

    base = store(turned_dot(stacked_ref[...], coarse_grad), 0)
    base = store(turned_dot(bottom_ref[...], stacked_grad_ref[...]), base)
    conv_grad = jnp.concatenate(
        [
            turned_dot(columns_ref[p * across : p * across + positions, :], grid)
            for p in range(3)
        ],
        axis=0,
    )
    base = store(conv_grad, base)
    class_grad = None
    class_lanes = logit_grad_ref.shape[1] // (joined_ref.shape[1] // channels)
    for block in range(joined_ref.shape[1] // channels):
        term = turned_dot(
            logit_grad_ref[:, block * class_lanes : (block + 1) * class_lanes],
            joined_ref[:, block * channels : (block + 1) * channels],
        )
        class_grad = term if class_grad is None else class_grad + term
    base = store(class_grad, base)
    if base < pack_ref.shape[0]:
        pack_ref[base:, :] = jnp.zeros((pack_ref.shape[0] - base, lanes), pack_ref.dtype)
    for index, target in enumerate(targets):
        start = block_start(place_ref, index % blocks, index // blocks, rows)
        target[...] = pack_ref[pl.ds(start, rows), :]


def pack_call(place, first, terms, operands, filled, blocks, across):
    lanes = first.shape[1]
    channels = operands[5].shape[1] // 3
    positions = 4 * first.shape[0]
    unit = 32 * blocks
    padded = -(-filled // unit) * unit
    block = jax.ShapeDtypeStruct((padded // (2 * blocks), lanes), jnp.bfloat16)
    return pl.pallas_call(
        functools.partial(
            pack_kernel, count=1 + len(terms), blocks=blocks, rows=padded // (2 * blocks),
            across=across,
        ),
        out_shape=(block,) * (2 * blocks),
        in_specs=[SMEM_SPEC] + [VMEM_SPEC] * (len(terms) + len(operands)) + [HBM_SPEC],
        out_specs=(VMEM_SPEC,) * (2 * blocks),
        scratch_shapes=[
            pltpu.VMEM((padded, lanes), jnp.bfloat16),
            pltpu.VMEM((positions, channels), jnp.float32),
            pltpu.VMEM(operands[-1].shape, jnp.bfloat16),
            pltpu.SemaphoreType.DMA((1,)),
        ],
        compiler_params=granted(
            (first, *terms, *operands), (block,) * (2 * blocks),
            (((padded, lanes), jnp.bfloat16), ((positions, channels), jnp.float32)),
            CORRELATE_MIB,
        ),
        name="pack_kernel",
    )(place, first, *terms, *operands)


def unpack_kernel(place_ref, *refs, blocks, count, shapes):
    pieces = refs[: 2 * blocks]
    outs = len(shapes)
    out_hbms = refs[2 * blocks : 2 * blocks + outs]
    out_refs = refs[2 * blocks + outs : 2 * blocks + 2 * outs]
    pack_ref, sems = refs[2 * blocks + 2 * outs :]
    lanes = pack_ref.shape[1]
    rows = pieces[0].shape[0]
    narrow = lanes // count
    for index, piece in enumerate(pieces):
        start = block_start(place_ref, index % blocks, index // blocks, rows)
        for mask in range(count):
            lane = pl.multiple_of((place_ref[2] ^ mask) * narrow, 128)
            pack_ref[pl.ds(start, rows), pl.ds(lane, narrow)] = piece[
                :, mask * narrow : (mask + 1) * narrow
            ]
    base = 0
    copies = []
    for place, (height, width) in enumerate(shapes):
        out_ref = out_refs[place]
        times = lanes // width
        part = height // times
        for index in range(times):
            value = pack_ref[base : base + part, index * width : (index + 1) * width]
            kept = min(part, out_ref.shape[0] - index * part)
            if kept > 0:
                out_ref[index * part : index * part + kept, :] = value.astype(jnp.float32)[:kept, :]
        base += part
        copies.append(fetch(out_ref, out_hbms[place], sems.at[place]))
    wait_all(copies)


def unpack_call(place, pieces, count, out_shapes, shapes):
    rows, lanes = pieces[0].shape
    outs = tuple(jax.ShapeDtypeStruct(shape, jnp.float32) for shape in out_shapes)
    scratch = ((rows * len(pieces), lanes), jnp.bfloat16)
    return pl.pallas_call(
        functools.partial(
            unpack_kernel, blocks=len(pieces) // 2, count=count, shapes=shapes
        ),
        out_shape=outs,
        in_specs=[SMEM_SPEC] + [VMEM_SPEC] * len(pieces),
        out_specs=(HBM_SPEC,) * len(out_shapes),
        scratch_shapes=[pltpu.VMEM(shape, jnp.float32) for shape in out_shapes]
        + [pltpu.VMEM(*scratch), pltpu.SemaphoreType.DMA((len(out_shapes),))],
        compiler_params=granted(pieces, outs, (scratch,), SMALL_MIB),
        name="unpack_kernel",
    )(place, *pieces)


def shift_columns(grid, offset):
    across = grid.shape[-2]
    pads = [(0, 0)] * grid.ndim
    if offset > 0:
        pads[-2] = (0, offset)
        return jnp.pad(lax.slice_in_dim(grid, offset, across, axis=-2 % grid.ndim), pads)
    if offset < 0:
        pads[-2] = (-offset, 0)
        return jnp.pad(lax.slice_in_dim(grid, 0, across + offset, axis=-2 % grid.ndim), pads)
    return grid


def shift_rows(grid, offset):
    height = grid.shape[-3]
    pads = [(0, 0)] * grid.ndim
    if offset > 0:
        pads[-3] = (0, offset)
        return jnp.pad(lax.slice_in_dim(grid, offset, height, axis=-3 % grid.ndim), pads)
    if offset < 0:
        pads[-3] = (-offset, 0)
        return jnp.pad(lax.slice_in_dim(grid, 0, height + offset, axis=-3 % grid.ndim), pads)
    return grid


def taps(grid, sign):
    columns = [shift_columns(grid, sign * (q - 1)) for q in range(3)]
    return [shift_rows(columns[q], sign * (p - 1)) for p in range(3) for q in range(3)]


def conv_in(grid, weight, sign, transposed):
    height, across, channels = grid.shape
    window = jnp.concatenate(taps(grid, sign), axis=-1).reshape(height * across, 9 * channels)
    if transposed:
        flat = jnp.transpose(weight, (0, 1, 3, 2)).reshape(9 * channels, weight.shape[2])
    else:
        flat = weight.reshape(9 * channels, weight.shape[3])
    result = jnp.dot(window, flat, preferred_element_type=jnp.float32)
    return result.reshape(height, across, -1)


def correlate_samples(left, right):
    samples, height, across, inward = left.shape
    outward = right.shape[-1]
    flat = left.reshape(samples * height * across, inward)
    shifted = jnp.concatenate(taps(right, -1), axis=-1).reshape(-1, 9 * outward)
    result = lax.dot_general(
        flat, shifted, (((0,), (0,)), ((), ())), preferred_element_type=jnp.float32
    )
    return jnp.transpose(result.reshape(inward, 3, 3, outward), (1, 2, 0, 3))


def join_blocks(mine, other):
    wide = lax.axis_size("wide")
    own = lax.axis_index("wide")
    stacked = jnp.stack([mine, other], axis=1).reshape((wide,) + mine.shape[1:])
    return stacked[jnp.arange(wide) ^ own].reshape(-1, mine.shape[-1])


def part_blocks(whole):
    wide = lax.axis_size("wide")
    own = lax.axis_index("wide")
    blocks = whole.reshape(wide, -1, whole.shape[-1])[jnp.arange(wide) ^ own]
    halves = blocks.reshape(wide // 2, 2, -1, whole.shape[-1])
    return [halves[r, half] for half in range(2) for r in range(wide // 2)]


def step(
    features,
    labels,
    conv_weight,
    down_weight,
    expand_weight,
    reduce_weight,
    up_weight,
    class_weight,
):
    crop_rows = features[0]
    height, across, channels = crop_rows.shape
    wide = lax.axis_size("wide")
    samples = lax.axis_size("samp")
    chips = chip_count()
    pixel_count = wide * samples * height * across
    loss_scale = 8.0 / math.sqrt(pixel_count)
    own = lax.axis_index("wide")
    place = jnp.stack([own % 2, own // 2, lax.axis_index("samp")]).astype(jnp.int32)
    base = down_weight.shape[1]
    inner = expand_weight.shape[-1]
    narrow = base // samples
    low_rows, low_across = height // 2, across // 2
    block_rows = low_rows * low_across
    grid = (wide * low_rows, low_across)
    class_count = class_weight.shape[1]
    class_lanes = 128
    own_kernels = inner % 128 == 0 and narrow % 128 == 0

    first_row, last_row = crop_rows[0], crop_rows[height - 1]
    even = own % 2 == 0
    pairs = [(i, i + 1) for i in range(1, wide - 1, 2)]
    pairs += [(target, source) for source, target in pairs]
    cross = lax.ppermute(jnp.where(even, first_row, last_row), "wide", pairs)
    core_row = swap(jnp.where(even, last_row, first_row), "wide", 1)
    columns, hidden_pre, stacked, coarse, down_held, *rest = front_call(
        place, in_hbm(crop_rows.reshape(height * across, channels)), cross, core_row,
        in_hbm(conv_weight.reshape(9 * channels, -1)), in_hbm(down_weight),
        in_hbm(expand_weight) if own_kernels else None, across, samples,
    )
    expand_held, coarse_sends = (rest[0], rest[1:]) if own_kernels else (None, rest)
    stacked_mine = gather_chips(stacked)
    stacked_other = swap_cores(stacked_mine)
    if own_kernels:
        coarse_part, expand_pre, expanded, reduce_held, *partial = bottleneck_call(
            forward_kernel, place, stacked_mine + stacked_other, down_held, expand_held,
            in_hbm(reduce_weight), None, low_across, samples,
        )
    else:
        stacked_all = join_blocks(jnp.stack(stacked_mine), jnp.stack(stacked_other))
        coarse_all = jnp.dot(stacked_all, down_weight, preferred_element_type=jnp.float32).astype(
            jnp.bfloat16
        )
        coarse_part = lane_block(coarse_all, lax.axis_index("samp"), samples)
        expand_grid = conv_in(coarse_all.reshape(*grid, base), expand_weight, 1, False)
        expanded_grid = jax.nn.silu(expand_grid).astype(jnp.bfloat16)
        partial = conv_in(expanded_grid, reduce_weight, 1, False).astype(jnp.bfloat16)
        partial = part_blocks(partial.reshape(-1, base))
        expanded = expanded_grid.reshape(-1, inner)
    coarse_slices = send_samples(coarse_sends)
    expanded_samples = [expanded] + send_samples([expanded] * (samples - 1))
    first, *terms = scatter_chips(partial[:chips], partial[chips:])
    bottom, joined, logit_grad, stacked_grad, bottom_grad, *bottom_sends = middle_call(
        place, first, terms, coarse, stacked, labels, class_weight.T, up_weight, loss_scale,
        class_lanes, samples,
    )
    grad_mine = gather_chips(stacked_grad)
    grad_other = swap_cores(grad_mine)
    if own_kernels:
        bottom_part, expanded_grad, *back = bottleneck_call(
            backward_kernel, place, grad_mine + grad_other, up_weight, expand_held,
            reduce_held, expand_pre, low_across, samples,
        )
    else:
        grad_all = join_blocks(jnp.stack(grad_mine), jnp.stack(grad_other))
        bottom_all = transposed_dot(grad_all, up_weight).astype(jnp.bfloat16)
        bottom_part = lane_block(bottom_all, lax.axis_index("samp"), samples)
        expanded_back = conv_in(bottom_all.reshape(*grid, base), reduce_weight, -1, True)
        grad_grid = (expanded_back * silu_slope(expand_grid)).astype(jnp.bfloat16)
        back = conv_in(grad_grid, expand_weight, -1, True).astype(jnp.bfloat16)
        back = part_blocks(back.reshape(-1, base))
        expanded_grad = grad_grid.reshape(-1, inner)
    bottom_slices = send_samples(bottom_sends)
    grad_samples = [expanded_grad] + send_samples([expanded_grad] * (samples - 1))
    first, *terms = scatter_chips(back[:chips], back[chips:])

    conv_out = conv_weight.shape[-1]
    shapes = (
        (down_weight.shape[0], base),
        (base, up_weight.shape[1]),
        (9 * channels, conv_out),
        (class_lanes, conv_out),
    )
    filled = sum(rows * lanes for rows, lanes in shapes) // base
    packed = pack_call(
        place, first, terms,
        (
            bottom_grad, stacked, stacked_grad, hidden_pre, bottom,
            columns, joined, logit_grad, down_weight,
        ),
        filled, chips, across,
    )
    first, *terms = scatter_chips(packed[:chips], packed[chips:])
    own_part, *part_sends, slices = sum_call(
        place, first, terms, coarse_slices + bottom_slices, samples
    )
    parts = send_samples(part_sends)
    slices_mine = gather_chips(slices)
    slices_other = swap_cores(slices_mine)
    total = add_all(own_part, parts).astype(jnp.bfloat16)
    own_total = jnp.concatenate(
        [total] + send_samples([total] * (samples - 1)), axis=1
    )
    total_mine = gather_chips(own_total)
    total_other = swap_cores(total_mine)
    out_shapes = shapes[:3] + ((class_count, conv_out),)
    down_total, up_total, conv_total, class_total = unpack_call(
        place, total_mine + total_other, samples, out_shapes, shapes,
    )

    if own_kernels:
        reduce_grad = correlate_call(
            place, expanded_samples, bottom_part, slices_mine + slices_other,
            samples - 1, False, low_across,
        )
        expand_grad = correlate_call(
            place, grad_samples, coarse_part, slices_mine + slices_other,
            0, True, low_across,
        )
    else:

        def join_samples(own_part, first_slice):
            joined_ = [own_part]
            for i in range(samples - 1):
                span = slice((first_slice + i) * block_rows, (first_slice + i + 1) * block_rows)
                joined_.append(
                    join_blocks(
                        jnp.stack([item[span] for item in slices_mine]),
                        jnp.stack([item[span] for item in slices_other]),
                    )
                )
            return jnp.stack(joined_).reshape(samples, *grid, narrow)

        reduce_grad = correlate_samples(
            jnp.stack(expanded_samples).reshape(samples, *grid, inner),
            join_samples(bottom_part, samples - 1),
        )
        expand_grad = correlate_samples(
            join_samples(coarse_part, 0),
            jnp.stack(grad_samples).reshape(samples, *grid, inner),
        )
    return (
        conv_total.reshape(conv_weight.shape),
        down_total,
        expand_grad,
        reduce_grad,
        up_total,
        class_total.T,
    )


def solution(mesh):
    return jax.shard_map(
        step,
        mesh=mesh,
        in_specs=(
            P("samp", "wide", None, None),
            P("samp", "wide", None),
            P(),
            P(),
            P(None, None, None, "wide"),
            P(None, None, "wide", None),
            P(),
            P(),
        ),
        out_specs=(
            P(),
            P(),
            P(None, None, "samp", "wide"),
            P(None, None, "wide", "samp"),
            P(),
            P(),
        ),
        check_vma=False,
    )
```

```python
import functools
import math

import jax
import jax.numpy as jnp
from jax import lax
from jax.experimental import pallas as pl
from jax.experimental.pallas import tpu as pltpu
from jax.sharding import PartitionSpec as P


def swap(values, axis, mask):
    count = lax.axis_size(axis)
    return lax.ppermute(values, axis, [(i, i ^ mask) for i in range(count)])


def chip_count():
    return lax.axis_size("wide") // 2


def gather_chips(piece):
    return [piece] + [swap(piece, "wide", 2 * r) for r in range(1, chip_count())]


def swap_cores(pieces):
    return [swap(piece, "wide", 1) for piece in pieces]


def scatter_chips(own, sent):
    chips = len(own)
    order = list(range(1, chips)) + [0]
    partner = {r: swap(sent[r], "wide", 1) for r in order}
    sends = [add_all(own[r], [partner[r]]).astype(jnp.bfloat16) for r in range(1, chips)]
    return [own[0], partner[0]] + send_chips(sends)


def send_chips(sends):
    return [swap(piece, "wide", 2 * (r + 1)) for r, piece in enumerate(sends)]


def send_samples(sends):
    return [swap(piece, "samp", mask + 1) for mask, piece in enumerate(sends)]


def lane_block(values, target, count):
    narrow = values.shape[-1] // count
    return lax.dynamic_slice_in_dim(values, target * narrow, narrow, axis=values.ndim - 1)


def in_hbm(values):
    return pltpu.with_memory_space_constraint(values, pltpu.HBM)


def add_all(first, rest):
    total = first.astype(jnp.float32)
    for item in rest:
        total = total + item.astype(jnp.float32)
    return total


def silu_slope(value):
    logistic = jax.nn.sigmoid(value)
    return logistic * (1.0 + value * (1.0 - logistic))


def column_mask(shape, column):
    return lax.broadcasted_iota(jnp.int32, shape, 1) == column


def from_left(values, across):
    view = values.reshape(-1, across, values.shape[-1])
    moved = pltpu.roll(view, 1, 1)
    return jnp.where(column_mask(view.shape, 0), 0.0, moved).reshape(values.shape)


def from_right(values, across):
    view = values.reshape(-1, across, values.shape[-1])
    moved = pltpu.roll(view, across - 1, 1)
    return jnp.where(column_mask(view.shape, across - 1), 0.0, moved).reshape(values.shape)


def block_start(place_ref, relative, half, rows, offset=0):
    chip = place_ref[1] ^ relative
    core = place_ref[0] ^ half
    return pl.multiple_of(offset + (2 * chip + core) * rows, 16)


def clear_edges(padded, across):
    total = padded.shape[0]
    blank = jnp.zeros((across, padded.shape[1]), padded.dtype)
    padded[0:across, :] = blank
    padded[total - across : total, :] = blank


def expand_copies_of(expand_hbm, expand_buf, sems):
    inner = expand_hbm.shape[-1]
    base = expand_hbm.shape[-2]
    return [
        pltpu.make_async_copy(
            expand_hbm.at[p, q],
            expand_buf.at[pl.ds(p * base, base), pl.ds(q * inner, inner)],
            sems.at[3 * p + q],
        )
        for p in range(3)
        for q in range(3)
    ]


def reduce_copies_of(reduce_hbm, reduce_buf, sems):
    inner = reduce_hbm.shape[-2]
    return [
        pltpu.make_async_copy(
            reduce_hbm.at[p, q],
            reduce_buf.at[pl.ds((3 * p + q) * inner, inner), :],
            sems.at[3 * p + q],
        )
        for p in range(3)
        for q in range(3)
    ]


def wait_all(copies):
    for copy in copies:
        copy.wait()


def plain_dot(left, right):
    return jnp.dot(left, right, preferred_element_type=jnp.float32)


def transposed_dot(left, right):
    return lax.dot_general(
        left, right, (((1,), (1,)), ((), ())), preferred_element_type=jnp.float32
    )


def gather_blocks(shifted, place_ref, half, offset, rows, blocks):
    return jnp.concatenate(
        [
            shifted[pl.ds(block_start(place_ref, block, half, rows, offset), rows), :]
            for block in range(blocks)
        ],
        axis=0,
    )


def fetch(source, target, sem):
    copy = pltpu.make_async_copy(source, target, sem)
    copy.start()
    return copy


def place_pieces(place_ref, pieces, target, blocks):
    rows = pieces[0].shape[0]
    for index, piece in enumerate(pieces):
        start = block_start(place_ref, index % blocks, index // blocks, rows)
        target[pl.ds(start, rows), :] = piece[...]


def store_own_lanes(place_ref, source, rows, target):
    narrow = target.shape[1]
    target[...] = source[rows, pl.ds(pl.multiple_of(place_ref[2] * narrow, 128), narrow)]


def store_rows(value, targets):
    rows = targets[0].shape[0]
    for index, target in enumerate(targets):
        target[...] = value[index * rows : (index + 1) * rows, :]


def forward_kernel(place_ref, *refs, blocks, rows, across):
    pieces = refs[: 2 * blocks]
    outer_ref, expand_buf, reduce_hbm, slice_ref, pre_ref, exp_ref, reduce_buf = refs[
        2 * blocks : 2 * blocks + 7
    ]
    own_refs = refs[2 * blocks + 7 : 3 * blocks + 7]
    sent_refs = refs[3 * blocks + 7 : 4 * blocks + 7]
    gathered, padded, shifted, sems = refs[4 * blocks + 7 :]
    reduce_copies = reduce_copies_of(reduce_hbm, reduce_buf, sems)
    for copy in reduce_copies:
        copy.start()
    clear_edges(padded, across)
    clear_edges(shifted, across)
    inner = pre_ref.shape[1]
    base = padded.shape[1]
    positions = pre_ref.shape[0]
    inside = pl.ds(across, positions)
    place_pieces(place_ref, pieces, gathered, blocks)
    padded[inside, :] = plain_dot(gathered[...], outer_ref[...]).astype(jnp.bfloat16)
    store_own_lanes(place_ref, padded, inside, slice_ref)
    total = None
    for p in range(3):
        term = plain_dot(
            padded[p * across : p * across + positions, :],
            expand_buf[p * base : (p + 1) * base, :],
        )
        total = term if total is None else total + term
    pre = (
        total[:, inner : 2 * inner]
        + from_left(total[:, 0:inner], across)
        + from_right(total[:, 2 * inner : 3 * inner], across)
    )
    pre_ref[...] = pre
    expanded = (pre * jax.nn.sigmoid(pre)).astype(jnp.bfloat16)
    exp_ref[...] = expanded
    wide = expanded.astype(jnp.float32)
    shifted[inside, 0:inner] = from_left(wide, across).astype(jnp.bfloat16)
    shifted[inside, inner : 2 * inner] = expanded
    shifted[inside, 2 * inner : 3 * inner] = from_right(wide, across).astype(jnp.bfloat16)
    wait_all(reduce_copies)
    for half, targets in ((1, sent_refs), (0, own_refs)):
        out = None
        for p in range(3):
            left = gather_blocks(shifted, place_ref, half, p * across, rows, blocks)
            term = plain_dot(left, reduce_buf[3 * p * inner : 3 * (p + 1) * inner, :])
            out = term if out is None else out + term
        store_rows(out.astype(jnp.bfloat16), targets)


def backward_kernel(place_ref, *refs, blocks, rows, across):
    pieces = refs[: 2 * blocks]
    outer_ref, expand_buf, reduce_buf, pre_ref, slice_ref, grad_ref = refs[
        2 * blocks : 2 * blocks + 6
    ]
    own_refs = refs[2 * blocks + 6 : 3 * blocks + 6]
    sent_refs = refs[3 * blocks + 6 : 4 * blocks + 6]
    gathered, padded, shifted = refs[4 * blocks + 6 :]
    clear_edges(padded, across)
    clear_edges(shifted, across)
    inner = pre_ref.shape[1]
    base = padded.shape[1]
    positions = pre_ref.shape[0]
    inside = pl.ds(across, positions)
    place_pieces(place_ref, pieces, gathered, blocks)
    padded[inside, :] = transposed_dot(gathered[...], outer_ref[...]).astype(jnp.bfloat16)
    store_own_lanes(place_ref, padded, inside, slice_ref)
    total = None
    for p in range(3):
        start = (2 - p) * across
        term = transposed_dot(
            padded[start : start + positions, :],
            reduce_buf[3 * p * inner : 3 * (p + 1) * inner, :],
        )
        total = term if total is None else total + term
    back = (
        total[:, inner : 2 * inner]
        + from_right(total[:, 0:inner], across)
        + from_left(total[:, 2 * inner : 3 * inner], across)
    )
    pre = pre_ref[...]
    grad = (back * silu_slope(pre)).astype(jnp.bfloat16)
    grad_ref[...] = grad
    wide = grad.astype(jnp.float32)
    shifted[inside, 0:inner] = from_right(wide, across).astype(jnp.bfloat16)
    shifted[inside, inner : 2 * inner] = grad
    shifted[inside, 2 * inner : 3 * inner] = from_left(wide, across).astype(jnp.bfloat16)
    for half, targets in ((1, sent_refs), (0, own_refs)):
        out = None
        for p in range(3):
            left = gather_blocks(shifted, place_ref, half, (2 - p) * across, rows, blocks)
            term = transposed_dot(left, expand_buf[p * base : (p + 1) * base, :])
            out = term if out is None else out + term
        store_rows(out.astype(jnp.bfloat16), targets)


BOTTLENECK_MIB = 12
CORRELATE_MIB = 8
SMALL_MIB = 6

VMEM_SPEC = pl.BlockSpec(memory_space=pltpu.VMEM)
SMEM_SPEC = pl.BlockSpec(memory_space=pltpu.SMEM)
HBM_SPEC = pl.BlockSpec(memory_space=pltpu.HBM)


def granted(operands, outs, scratch, temporaries):
    total = sum(math.prod(item.shape) * item.dtype.itemsize for item in (*operands, *outs))
    total += sum(math.prod(shape) * jnp.dtype(dtype).itemsize for shape, dtype in scratch)
    limit = min(int(total * 1.1) + (temporaries << 20), 60 << 20)
    return pltpu.CompilerParams(vmem_limit_bytes=limit)


def bottleneck_call(
    kernel, place, pieces, outer_weight, expand_held, reduce_held, pre, across, samples
):
    rows, outer = pieces[0].shape
    base = expand_held.shape[0] // 3
    inner = expand_held.shape[1] // 3
    positions = len(pieces) * rows
    inner_bf16 = jax.ShapeDtypeStruct((positions, inner), jnp.bfloat16)
    inner_f32 = jax.ShapeDtypeStruct((positions, inner), jnp.float32)
    held = jax.ShapeDtypeStruct((9 * inner, base), jnp.bfloat16)
    parts = (jax.ShapeDtypeStruct((rows, base), jnp.bfloat16),) * len(pieces)
    part = jax.ShapeDtypeStruct((positions, base // samples), jnp.bfloat16)
    operands = [*pieces, outer_weight, expand_held, reduce_held]
    specs = [SMEM_SPEC] + [VMEM_SPEC] * (len(pieces) + 2)
    scratch = (
        ((positions, outer), jnp.bfloat16),
        ((positions + 2 * across, base), jnp.bfloat16),
        ((positions + 2 * across, 3 * inner), jnp.bfloat16),
    )
    if pre is None:
        outs = (part, inner_f32, inner_bf16, held) + parts
        specs += [HBM_SPEC]
        sems = [pltpu.SemaphoreType.DMA((9,))]
    else:
        outs = (part, inner_bf16) + parts
        operands.append(pre)
        specs += [VMEM_SPEC] * 2
        sems = []
    return pl.pallas_call(
        functools.partial(kernel, blocks=len(pieces) // 2, rows=rows, across=across),
        out_shape=outs,
        in_specs=specs,
        out_specs=tuple(VMEM_SPEC for _ in outs),
        scratch_shapes=[pltpu.VMEM(*item) for item in scratch] + sems,
        compiler_params=granted(operands, outs, scratch, BOTTLENECK_MIB),
    )(place, *operands)


def correlate_kernel(place_ref, *refs, count, blocks, across, first_slice, split_left):
    whole = refs[:count]
    own = refs[count]
    others = refs[count + 1 : count + 1 + 2 * blocks]
    out_hbm, out_ref, joined, shifted, sems = refs[count + 1 + 2 * blocks :]
    copies = []
    rows = joined.shape[0] // (2 * blocks)
    outward = shifted.shape[-1] // 3
    positions = joined.shape[0]
    clear_edges(shifted, across)
    inside = pl.ds(across, positions)
    for sample in range(count):
        if sample == 0:
            part = own[...]
        else:
            first = (first_slice + sample - 1) * rows
            for index in range(2 * blocks):
                start = block_start(place_ref, index % blocks, index // blocks, rows)
                joined[pl.ds(start, rows), :] = others[index][first : first + rows, :]
            part = joined[...]
        if split_left:
            left, right = part, whole[sample][...]
        else:
            left, right = whole[sample][...], part
        turned = jnp.transpose(left, (1, 0))
        wide = right.astype(jnp.float32)
        shifted[inside, 0:outward] = from_right(wide, across).astype(jnp.bfloat16)
        shifted[inside, outward : 2 * outward] = right
        shifted[inside, 2 * outward : 3 * outward] = from_left(wide, across).astype(jnp.bfloat16)
        for p in range(3):
            start = (2 - p) * across
            term = plain_dot(turned, shifted[start : start + positions, :])
            for q in range(3):
                piece = term[:, q * outward : (q + 1) * outward]
                if sample == 0:
                    out_ref[p, q] = piece
                else:
                    out_ref[p, q] += piece
            if sample == count - 1:
                copies.append(fetch(out_ref.at[p], out_hbm.at[p], sems.at[p]))
    wait_all(copies)


def correlate_call(place, whole, own, others, first_slice, split_left, across):
    count = len(whole)
    positions, full_lanes = whole[0].shape
    part_lanes = own.shape[1]
    inward, outward = (part_lanes, full_lanes) if split_left else (full_lanes, part_lanes)
    out = jax.ShapeDtypeStruct((3, 3, inward, outward), jnp.float32)
    scratch = (
        ((positions, part_lanes), jnp.bfloat16),
        ((positions + 2 * across, 3 * outward), jnp.bfloat16),
    )
    operands = (*whole, own, *others)
    return pl.pallas_call(
        functools.partial(
            correlate_kernel, count=count, blocks=len(others) // 2, across=across,
            first_slice=first_slice, split_left=split_left,
        ),
        out_shape=out,
        in_specs=[SMEM_SPEC] + [VMEM_SPEC] * len(operands),
        out_specs=HBM_SPEC,
        scratch_shapes=[pltpu.VMEM(out.shape, out.dtype)]
        + [pltpu.VMEM(*item) for item in scratch]
        + [pltpu.SemaphoreType.DMA((3,))],
        compiler_params=granted(operands, (out,), scratch, CORRELATE_MIB),
        name="correlate_kernel",
    )(place, *operands)


def store_lane_blocks(place_ref, source, targets):
    narrow = targets[0].shape[1]
    for index, target in enumerate(targets):
        lane = pl.multiple_of((place_ref[2] ^ (index + 1)) * narrow, 128)
        target[...] = source[:, pl.ds(lane, narrow)]


def front_kernel(
    place_ref, cross_ref, core_row_ref, crop_hbm, conv_hbm, down_hbm, *refs, across, hold
):
    held, refs = (refs[:1], refs[1:]) if hold else ((), refs)
    columns_ref, pre_ref, stacked_ref, coarse_ref, down_buf = refs[:5]
    slice_refs = refs[5 + hold : -4]
    near_ref, grid_ref, conv_buf, sems = refs[-4:]
    positions, channels = crop_hbm.shape
    crop_copy = fetch(crop_hbm, near_ref.at[pl.ds(across, positions), :], sems.at[11])
    conv_copy = fetch(conv_hbm, conv_buf, sems.at[9])
    down_copy = fetch(down_hbm, down_buf, sems.at[10])
    expand_copies = expand_copies_of(held[0], refs[5], sems) if hold else []
    for copy in expand_copies:
        copy.start()
    core = place_ref[0]
    far = across + positions
    near_ref[pl.ds(pl.multiple_of(core * far, 16), across), :] = cross_ref[...]
    near_ref[pl.ds(pl.multiple_of((1 - core) * far, 16), across), :] = core_row_ref[...]
    crop_copy.wait()
    wide = near_ref[...].astype(jnp.float32)
    columns_ref[:, 0:channels] = from_left(wide, across).astype(jnp.bfloat16)
    columns_ref[:, channels : 2 * channels] = near_ref[...]
    columns_ref[:, 2 * channels :] = from_right(wide, across).astype(jnp.bfloat16)
    left = jnp.concatenate(
        [columns_ref[p * across : p * across + positions, :] for p in range(3)], axis=1
    )
    conv_copy.wait()
    grid_ref[...] = plain_dot(left, conv_buf[...])
    out = grid_ref.shape[1]
    half = across // 2
    for i in range(positions // (2 * across)):
        for a in range(2):
            for b in range(2):
                lane = (2 * a + b) * out
                pre_ref[i * half : (i + 1) * half, lane : lane + out] = grid_ref[
                    pl.ds((2 * i + a) * across + b, half, stride=2), :
                ]
    pre = pre_ref[...]
    stacked = (pre * jax.nn.sigmoid(pre)).astype(jnp.bfloat16)
    stacked_ref[...] = stacked
    down_copy.wait()
    coarse_ref[...] = plain_dot(stacked, down_buf[...]).astype(jnp.bfloat16)
    store_lane_blocks(place_ref, coarse_ref, slice_refs)
    wait_all(expand_copies)


def front_call(
    place, crop, cross, core_row, conv_flat, down_weight, expand_weight, across, samples
):
    hold = expand_weight is not None
    positions, channels = crop.shape
    out = conv_flat.shape[1]
    low = positions // 4
    base = down_weight.shape[1]
    outs = (
        jax.ShapeDtypeStruct((positions + 2 * across, 3 * channels), jnp.bfloat16),
        jax.ShapeDtypeStruct((low, 4 * out), jnp.float32),
        jax.ShapeDtypeStruct((low, 4 * out), jnp.bfloat16),
        jax.ShapeDtypeStruct((low, base), jnp.bfloat16),
        jax.ShapeDtypeStruct(down_weight.shape, jnp.bfloat16),
    )
    weights = (conv_flat, down_weight)
    if hold:
        weights += (expand_weight,)
        outs += (jax.ShapeDtypeStruct((3 * base, 3 * expand_weight.shape[-1]), jnp.bfloat16),)
    outs += (jax.ShapeDtypeStruct((low, base // samples), jnp.bfloat16),) * (samples - 1)
    scratch = (
        ((positions + 2 * across, channels), jnp.bfloat16),
        ((positions, out), jnp.float32),
        (conv_flat.shape, jnp.bfloat16),
    )
    return pl.pallas_call(
        functools.partial(front_kernel, across=across, hold=int(hold)),
        out_shape=outs,
        in_specs=[SMEM_SPEC] + [VMEM_SPEC] * 2 + [HBM_SPEC] * (1 + len(weights)),
        out_specs=(VMEM_SPEC,) * len(outs),
        scratch_shapes=[pltpu.VMEM(*item) for item in scratch] + [pltpu.SemaphoreType.DMA((12,))],
        compiler_params=granted((crop, cross, core_row), outs, scratch, SMALL_MIB),
        name="front_kernel",
    )(place, cross, core_row, crop, *weights)


def middle_kernel(place_ref, *refs, count, loss_scale, class_count):
    first_ref, terms = refs[0], refs[1:count]
    coarse_ref, stacked_ref, label_ref, class_turned_ref, up_hbm = refs[count : count + 5]
    bottom_ref, joined_ref, logit_grad_ref, stacked_grad_ref, bottom_grad_ref = refs[
        count + 5 : count + 10
    ]
    slice_refs = refs[count + 10 : -3]
    class_ref, up_ref, sems = refs[-3:]
    up_copy = fetch(up_hbm, up_ref, sems.at[0])
    lanes, channels = class_ref.shape
    class_ref[...] = jnp.zeros(class_ref.shape, class_ref.dtype)
    class_ref[0:class_count, :] = class_turned_ref[...]
    height, across = label_ref.shape[1:]
    half = across // 2
    label_rows = label_ref[0].astype(jnp.float32).astype(jnp.bfloat16)
    row = lax.broadcasted_iota(jnp.int32, (half, across), 0)
    pixel = lax.broadcasted_iota(jnp.int32, (half, across), 1)
    label_columns = [
        transposed_dot((pixel == 2 * row + b).astype(jnp.float32).astype(jnp.bfloat16), label_rows)
        for b in range(2)
    ]
    total = coarse_ref[...].astype(jnp.float32) + add_all(
        first_ref[...], [term[...] for term in terms]
    )
    bottom = total.astype(jnp.bfloat16)
    bottom_ref[...] = bottom
    up_copy.wait()
    joined_pre = plain_dot(bottom, up_ref[...]) + stacked_ref[...].astype(jnp.float32)
    joined_ref[...] = (joined_pre * jax.nn.sigmoid(joined_pre)).astype(jnp.bfloat16)
    slope = silu_slope(joined_pre)
    column = lax.broadcasted_iota(jnp.int32, (joined_pre.shape[0], lanes), 1)
    column_value = column.astype(jnp.float32)
    for a in range(2):
        for b in range(2):
            block = 2 * a + b
            span = slice(block * channels, (block + 1) * channels)
            label = jnp.concatenate(
                [label_columns[b][:, 2 * i + a : 2 * i + a + 1] for i in range(height // 2)],
                axis=0,
            )
            logits = transposed_dot(joined_ref[:, span], class_ref[...])
            powers = jnp.where(column < class_count, jnp.exp(logits), 0.0)
            probability = powers / jnp.sum(powers, axis=-1, keepdims=True)
            onehot = (column_value == label).astype(jnp.float32)
            logit_grad = ((probability - onehot) * loss_scale).astype(jnp.bfloat16)
            logit_grad_ref[:, block * lanes : (block + 1) * lanes] = logit_grad
            joined_grad = plain_dot(logit_grad, class_ref[...])
            stacked_grad_ref[:, span] = (joined_grad * slope[:, span]).astype(jnp.bfloat16)
    bottom_grad_ref[...] = transposed_dot(stacked_grad_ref[...], up_ref[...]).astype(jnp.bfloat16)
    store_lane_blocks(place_ref, bottom_grad_ref, slice_refs)


def middle_call(
    place, first, terms, coarse, stacked, labels, class_turned, up_weight, loss_scale, class_lanes,
    samples,
):
    rows, base = coarse.shape
    wide = stacked.shape[1]
    channels = class_turned.shape[1]
    shapes = (base, wide, wide // channels * class_lanes, wide, base)
    shapes += (base // samples,) * (samples - 1)
    outs = tuple(jax.ShapeDtypeStruct((rows, lanes), jnp.bfloat16) for lanes in shapes)
    operands = (first, *terms, coarse, stacked, labels, class_turned)
    scratch = (((class_lanes, channels), jnp.bfloat16), (up_weight.shape, jnp.bfloat16))
    return pl.pallas_call(
        functools.partial(
            middle_kernel, count=1 + len(terms), loss_scale=loss_scale,
            class_count=class_turned.shape[0],
        ),
        out_shape=outs,
        in_specs=[SMEM_SPEC] + [VMEM_SPEC] * len(operands) + [HBM_SPEC],
        out_specs=(VMEM_SPEC,) * len(outs),
        scratch_shapes=[pltpu.VMEM(*item) for item in scratch] + [pltpu.SemaphoreType.DMA((1,))],
        compiler_params=granted(operands, outs, scratch, SMALL_MIB),
        name="middle_kernel",
    )(place, *operands, up_weight)


def sum_kernel(place_ref, *refs, count, slices):
    first_ref, terms = refs[0], refs[1:count]
    slice_refs = refs[count : count + slices]
    own_ref = refs[count + slices]
    send_refs = refs[count + slices + 1 : -2]
    stack_ref, total_ref = refs[-2:]
    total_ref[...] = add_all(first_ref[...], [term[...] for term in terms]).astype(jnp.bfloat16)
    narrow = own_ref.shape[1]
    own_ref[...] = total_ref[:, pl.ds(pl.multiple_of(place_ref[2] * narrow, 128), narrow)]
    store_lane_blocks(place_ref, total_ref, send_refs)
    for index, source in enumerate(slice_refs):
        rows = source.shape[0]
        stack_ref[index * rows : (index + 1) * rows, :] = source[...]


def sum_call(place, first, terms, slices, samples):
    rows, lanes = first.shape
    block = jax.ShapeDtypeStruct((rows, lanes // samples), jnp.bfloat16)
    stack = jax.ShapeDtypeStruct((len(slices) * slices[0].shape[0], slices[0].shape[1]), jnp.bfloat16)
    outs = (block,) * samples + (stack,)
    operands = (first, *terms, *slices)
    scratch = ((first.shape, jnp.bfloat16),)
    return pl.pallas_call(
        functools.partial(sum_kernel, count=1 + len(terms), slices=len(slices)),
        out_shape=outs,
        in_specs=[SMEM_SPEC] + [VMEM_SPEC] * len(operands),
        out_specs=(VMEM_SPEC,) * len(outs),
        scratch_shapes=[pltpu.VMEM(*item) for item in scratch],
        compiler_params=granted(operands, outs, scratch, SMALL_MIB),
        name="sum_kernel",
    )(place, *operands)


def turned_dot(left, right):
    return lax.dot_general(
        left, right, (((0,), (0,)), ((), ())), preferred_element_type=jnp.float32
    )


def pack_start(place_ref, relative, half, rows, lanes):
    start = pl.multiple_of((place_ref[1] ^ relative) * rows, 16)
    return start, pl.multiple_of((place_ref[0] ^ half) * lanes, 128)


def pack_kernel(place_ref, *refs, count, blocks, rows, across):
    first_ref, terms = refs[0], refs[1:count]
    (
        bottom_grad_ref, stacked_ref, stacked_grad_ref, pre_ref, bottom_ref,
        columns_ref, joined_ref, logit_grad_ref, down_hbm,
    ) = refs[count : count + 9]
    targets = refs[count + 9 : -4]
    pack_ref, grid_ref, down_ref, sems = refs[-4:]
    down_copy = fetch(down_hbm, down_ref, sems.at[0])
    lanes = pack_ref.shape[1]
    total = bottom_grad_ref[...].astype(jnp.float32) + add_all(
        first_ref[...], [term[...] for term in terms]
    )
    coarse_grad = total.astype(jnp.bfloat16)
    down_copy.wait()
    hidden_sum = transposed_dot(coarse_grad, down_ref[...]) + stacked_grad_ref[...].astype(
        jnp.float32
    )
    hidden_grad = (hidden_sum * silu_slope(pre_ref[...])).astype(jnp.bfloat16).astype(jnp.float32)
    positions, channels = grid_ref.shape
    half = across // 2
    for i in range(positions // (2 * across)):
        for a in range(2):
            for b in range(2):
                lane = (2 * a + b) * channels
                grid_ref[pl.ds((2 * i + a) * across + b, half, stride=2), :] = hidden_grad[
                    i * half : (i + 1) * half, lane : lane + channels
                ]
    grid = grid_ref[...].astype(jnp.bfloat16)

    def store(value, base):
        rounded = value.astype(jnp.bfloat16)
        times = lanes // value.shape[1]
        part = value.shape[0] // times
        for index in range(times):
            pack_ref[base : base + part, index * value.shape[1] : (index + 1) * value.shape[1]] = (
                rounded[index * part : (index + 1) * part, :]
            )
        return base + part

    base = store(turned_dot(stacked_ref[...], coarse_grad), 0)
    base = store(turned_dot(bottom_ref[...], stacked_grad_ref[...]), base)
    conv_grad = jnp.concatenate(
        [
            turned_dot(columns_ref[p * across : p * across + positions, :], grid)
            for p in range(3)
        ],
        axis=0,
    )
    base = store(conv_grad, base)
    class_grad = None
    class_lanes = logit_grad_ref.shape[1] // (joined_ref.shape[1] // channels)
    for block in range(joined_ref.shape[1] // channels):
        term = turned_dot(
            logit_grad_ref[:, block * class_lanes : (block + 1) * class_lanes],
            joined_ref[:, block * channels : (block + 1) * channels],
        )
        class_grad = term if class_grad is None else class_grad + term
    base = store(class_grad, base)
    if base < pack_ref.shape[0]:
        pack_ref[base:, :] = jnp.zeros((pack_ref.shape[0] - base, lanes), pack_ref.dtype)
    for index, target in enumerate(targets):
        start, lane = pack_start(place_ref, index % blocks, index // blocks, rows, lanes // 2)
        target[...] = pack_ref[pl.ds(start, rows), pl.ds(lane, lanes // 2)]


def pack_call(place, first, terms, operands, filled, blocks, across):
    lanes = first.shape[1]
    channels = operands[5].shape[1] // 3
    positions = 4 * first.shape[0]
    unit = 16 * blocks
    padded = -(-filled // unit) * unit
    block = jax.ShapeDtypeStruct((padded // blocks, lanes // 2), jnp.bfloat16)
    return pl.pallas_call(
        functools.partial(
            pack_kernel, count=1 + len(terms), blocks=blocks, rows=padded // blocks,
            across=across,
        ),
        out_shape=(block,) * (2 * blocks),
        in_specs=[SMEM_SPEC] + [VMEM_SPEC] * (len(terms) + len(operands)) + [HBM_SPEC],
        out_specs=(VMEM_SPEC,) * (2 * blocks),
        scratch_shapes=[
            pltpu.VMEM((padded, lanes), jnp.bfloat16),
            pltpu.VMEM((positions, channels), jnp.float32),
            pltpu.VMEM(operands[-1].shape, jnp.bfloat16),
            pltpu.SemaphoreType.DMA((1,)),
        ],
        compiler_params=granted(
            (first, *terms, *operands), (block,) * (2 * blocks),
            (((padded, lanes), jnp.bfloat16), ((positions, channels), jnp.float32)),
            CORRELATE_MIB,
        ),
        name="pack_kernel",
    )(place, first, *terms, *operands)


def unpack_kernel(place_ref, *refs, blocks, count, shapes):
    pieces = refs[: 2 * blocks]
    outs = len(shapes)
    out_hbms = refs[2 * blocks : 2 * blocks + outs]
    out_refs = refs[2 * blocks + outs : 2 * blocks + 2 * outs]
    pack_ref, sems = refs[2 * blocks + 2 * outs :]
    lanes = pack_ref.shape[1]
    rows = pieces[0].shape[0]
    narrow = lanes // (2 * count)
    for index, piece in enumerate(pieces):
        start, core_lane = pack_start(
            place_ref, index % blocks, index // blocks, rows, lanes // 2
        )
        for mask in range(count):
            lane = pl.multiple_of(core_lane + (place_ref[2] ^ mask) * narrow, 128)
            pack_ref[pl.ds(start, rows), pl.ds(lane, narrow)] = piece[
                :, mask * narrow : (mask + 1) * narrow
            ]
    base = 0
    copies = []
    for place, (height, width) in enumerate(shapes):
        out_ref = out_refs[place]
        times = lanes // width
        part = height // times
        for index in range(times):
            value = pack_ref[base : base + part, index * width : (index + 1) * width]
            kept = min(part, out_ref.shape[0] - index * part)
            if kept > 0:
                out_ref[index * part : index * part + kept, :] = value.astype(jnp.float32)[:kept, :]
        base += part
        copies.append(fetch(out_ref, out_hbms[place], sems.at[place]))
    wait_all(copies)


def unpack_call(place, pieces, count, out_shapes, shapes):
    rows, lanes = pieces[0].shape
    outs = tuple(jax.ShapeDtypeStruct(shape, jnp.float32) for shape in out_shapes)
    scratch = ((rows * len(pieces) // 2, 2 * lanes), jnp.bfloat16)
    return pl.pallas_call(
        functools.partial(
            unpack_kernel, blocks=len(pieces) // 2, count=count, shapes=shapes
        ),
        out_shape=outs,
        in_specs=[SMEM_SPEC] + [VMEM_SPEC] * len(pieces),
        out_specs=(HBM_SPEC,) * len(out_shapes),
        scratch_shapes=[pltpu.VMEM(shape, jnp.float32) for shape in out_shapes]
        + [pltpu.VMEM(*scratch), pltpu.SemaphoreType.DMA((len(out_shapes),))],
        compiler_params=granted(pieces, outs, (scratch,), SMALL_MIB),
        name="unpack_kernel",
    )(place, *pieces)


def shift_columns(grid, offset):
    across = grid.shape[-2]
    pads = [(0, 0)] * grid.ndim
    if offset > 0:
        pads[-2] = (0, offset)
        return jnp.pad(lax.slice_in_dim(grid, offset, across, axis=-2 % grid.ndim), pads)
    if offset < 0:
        pads[-2] = (-offset, 0)
        return jnp.pad(lax.slice_in_dim(grid, 0, across + offset, axis=-2 % grid.ndim), pads)
    return grid


def shift_rows(grid, offset):
    height = grid.shape[-3]
    pads = [(0, 0)] * grid.ndim
    if offset > 0:
        pads[-3] = (0, offset)
        return jnp.pad(lax.slice_in_dim(grid, offset, height, axis=-3 % grid.ndim), pads)
    if offset < 0:
        pads[-3] = (-offset, 0)
        return jnp.pad(lax.slice_in_dim(grid, 0, height + offset, axis=-3 % grid.ndim), pads)
    return grid


def taps(grid, sign):
    columns = [shift_columns(grid, sign * (q - 1)) for q in range(3)]
    return [shift_rows(columns[q], sign * (p - 1)) for p in range(3) for q in range(3)]


def conv_in(grid, weight, sign, transposed):
    height, across, channels = grid.shape
    window = jnp.concatenate(taps(grid, sign), axis=-1).reshape(height * across, 9 * channels)
    if transposed:
        flat = jnp.transpose(weight, (0, 1, 3, 2)).reshape(9 * channels, weight.shape[2])
    else:
        flat = weight.reshape(9 * channels, weight.shape[3])
    result = jnp.dot(window, flat, preferred_element_type=jnp.float32)
    return result.reshape(height, across, -1)


def correlate_samples(left, right):
    samples, height, across, inward = left.shape
    outward = right.shape[-1]
    flat = left.reshape(samples * height * across, inward)
    shifted = jnp.concatenate(taps(right, -1), axis=-1).reshape(-1, 9 * outward)
    result = lax.dot_general(
        flat, shifted, (((0,), (0,)), ((), ())), preferred_element_type=jnp.float32
    )
    return jnp.transpose(result.reshape(inward, 3, 3, outward), (1, 2, 0, 3))


def join_blocks(mine, other):
    wide = lax.axis_size("wide")
    own = lax.axis_index("wide")
    stacked = jnp.stack([mine, other], axis=1).reshape((wide,) + mine.shape[1:])
    return stacked[jnp.arange(wide) ^ own].reshape(-1, mine.shape[-1])


def part_blocks(whole):
    wide = lax.axis_size("wide")
    own = lax.axis_index("wide")
    blocks = whole.reshape(wide, -1, whole.shape[-1])[jnp.arange(wide) ^ own]
    halves = blocks.reshape(wide // 2, 2, -1, whole.shape[-1])
    return [halves[r, half] for half in range(2) for r in range(wide // 2)]


def step(
    features,
    labels,
    conv_weight,
    down_weight,
    expand_weight,
    reduce_weight,
    up_weight,
    class_weight,
):
    crop_rows = features[0]
    height, across, channels = crop_rows.shape
    wide = lax.axis_size("wide")
    samples = lax.axis_size("samp")
    chips = chip_count()
    pixel_count = wide * samples * height * across
    loss_scale = 8.0 / math.sqrt(pixel_count)
    own = lax.axis_index("wide")
    place = jnp.stack([own % 2, own // 2, lax.axis_index("samp")]).astype(jnp.int32)
    base = down_weight.shape[1]
    inner = expand_weight.shape[-1]
    narrow = base // samples
    low_rows, low_across = height // 2, across // 2
    block_rows = low_rows * low_across
    grid = (wide * low_rows, low_across)
    class_count = class_weight.shape[1]
    class_lanes = 128
    own_kernels = inner % 128 == 0 and narrow % 128 == 0

    first_row, last_row = crop_rows[0], crop_rows[height - 1]
    even = own % 2 == 0
    pairs = [(i, i + 1) for i in range(1, wide - 1, 2)]
    pairs += [(target, source) for source, target in pairs]
    cross = lax.ppermute(jnp.where(even, first_row, last_row), "wide", pairs)
    core_row = swap(jnp.where(even, last_row, first_row), "wide", 1)
    columns, hidden_pre, stacked, coarse, down_held, *rest = front_call(
        place, in_hbm(crop_rows.reshape(height * across, channels)), cross, core_row,
        in_hbm(conv_weight.reshape(9 * channels, -1)), in_hbm(down_weight),
        in_hbm(expand_weight) if own_kernels else None, across, samples,
    )
    expand_held, coarse_sends = (rest[0], rest[1:]) if own_kernels else (None, rest)
    stacked_mine = gather_chips(stacked)
    stacked_other = swap_cores(stacked_mine)
    if own_kernels:
        coarse_part, expand_pre, expanded, reduce_held, *partial = bottleneck_call(
            forward_kernel, place, stacked_mine + stacked_other, down_held, expand_held,
            in_hbm(reduce_weight), None, low_across, samples,
        )
    else:
        stacked_all = join_blocks(jnp.stack(stacked_mine), jnp.stack(stacked_other))
        coarse_all = jnp.dot(stacked_all, down_weight, preferred_element_type=jnp.float32).astype(
            jnp.bfloat16
        )
        coarse_part = lane_block(coarse_all, lax.axis_index("samp"), samples)
        expand_grid = conv_in(coarse_all.reshape(*grid, base), expand_weight, 1, False)
        expanded_grid = jax.nn.silu(expand_grid).astype(jnp.bfloat16)
        partial = conv_in(expanded_grid, reduce_weight, 1, False).astype(jnp.bfloat16)
        partial = part_blocks(partial.reshape(-1, base))
        expanded = expanded_grid.reshape(-1, inner)
    coarse_slices = send_samples(coarse_sends)
    expanded_samples = [expanded] + send_samples([expanded] * (samples - 1))
    first, *terms = scatter_chips(partial[:chips], partial[chips:])
    bottom, joined, logit_grad, stacked_grad, bottom_grad, *bottom_sends = middle_call(
        place, first, terms, coarse, stacked, labels, class_weight.T, up_weight, loss_scale,
        class_lanes, samples,
    )
    grad_mine = gather_chips(stacked_grad)
    grad_other = swap_cores(grad_mine)
    if own_kernels:
        bottom_part, expanded_grad, *back = bottleneck_call(
            backward_kernel, place, grad_mine + grad_other, up_weight, expand_held,
            reduce_held, expand_pre, low_across, samples,
        )
    else:
        grad_all = join_blocks(jnp.stack(grad_mine), jnp.stack(grad_other))
        bottom_all = transposed_dot(grad_all, up_weight).astype(jnp.bfloat16)
        bottom_part = lane_block(bottom_all, lax.axis_index("samp"), samples)
        expanded_back = conv_in(bottom_all.reshape(*grid, base), reduce_weight, -1, True)
        grad_grid = (expanded_back * silu_slope(expand_grid)).astype(jnp.bfloat16)
        back = conv_in(grad_grid, expand_weight, -1, True).astype(jnp.bfloat16)
        back = part_blocks(back.reshape(-1, base))
        expanded_grad = grad_grid.reshape(-1, inner)
    bottom_slices = send_samples(bottom_sends)
    grad_samples = [expanded_grad] + send_samples([expanded_grad] * (samples - 1))
    first, *terms = scatter_chips(back[:chips], back[chips:])

    conv_out = conv_weight.shape[-1]
    shapes = (
        (down_weight.shape[0], base),
        (base, up_weight.shape[1]),
        (9 * channels, conv_out),
        (class_lanes, conv_out),
    )
    filled = sum(rows * lanes for rows, lanes in shapes) // base
    packed = pack_call(
        place, first, terms,
        (
            bottom_grad, stacked, stacked_grad, hidden_pre, bottom,
            columns, joined, logit_grad, down_weight,
        ),
        filled, chips, across,
    )
    first, *terms = scatter_chips(packed[:chips], packed[chips:])
    own_part, *part_sends, slices = sum_call(
        place, first, terms, coarse_slices + bottom_slices, samples
    )
    parts = send_samples(part_sends)
    slices_mine = gather_chips(slices)
    slices_other = swap_cores(slices_mine)
    total = add_all(own_part, parts).astype(jnp.bfloat16)
    own_total = jnp.concatenate(
        [total] + send_samples([total] * (samples - 1)), axis=1
    )
    total_mine = gather_chips(own_total)
    total_other = swap_cores(total_mine)
    out_shapes = shapes[:3] + ((class_count, conv_out),)
    down_total, up_total, conv_total, class_total = unpack_call(
        place, total_mine + total_other, samples, out_shapes, shapes,
    )

    if own_kernels:
        reduce_grad = correlate_call(
            place, expanded_samples, bottom_part, slices_mine + slices_other,
            samples - 1, False, low_across,
        )
        expand_grad = correlate_call(
            place, grad_samples, coarse_part, slices_mine + slices_other,
            0, True, low_across,
        )
    else:

        def join_samples(own_part, first_slice):
            joined_ = [own_part]
            for i in range(samples - 1):
                span = slice((first_slice + i) * block_rows, (first_slice + i + 1) * block_rows)
                joined_.append(
                    join_blocks(
                        jnp.stack([item[span] for item in slices_mine]),
                        jnp.stack([item[span] for item in slices_other]),
                    )
                )
            return jnp.stack(joined_).reshape(samples, *grid, narrow)

        reduce_grad = correlate_samples(
            jnp.stack(expanded_samples).reshape(samples, *grid, inner),
            join_samples(bottom_part, samples - 1),
        )
        expand_grad = correlate_samples(
            join_samples(coarse_part, 0),
            jnp.stack(grad_samples).reshape(samples, *grid, inner),
        )
    return (
        conv_total.reshape(conv_weight.shape),
        down_total,
        expand_grad,
        reduce_grad,
        up_total,
        class_total.T,
    )


def solution(mesh):
    return jax.shard_map(
        step,
        mesh=mesh,
        in_specs=(
            P("samp", "wide", None, None),
            P("samp", "wide", None),
            P(),
            P(),
            P(None, None, None, "wide"),
            P(None, None, "wide", None),
            P(),
            P(),
        ),
        out_specs=(
            P(),
            P(),
            P(None, None, "samp", "wide"),
            P(None, None, "wide", "samp"),
            P(),
            P(),
        ),
        check_vma=False,
    )
```
